512 devices in a mesh: shot: 16 (over x, y), tx: 4 (over z_hi, core), ty: 8 (over z_lo).
Axes of the slice: x: 4, y: 4, z: 16 (z_hi: 2, z_lo: 8; z = z_hi * 8 + z_lo), core: 2. Of those that a mesh axis runs over, the one named last changes fastest.
Arguments:
- forward_prev: float32 [16, 128, 64, 256], P('shot', 'tx', 'ty'), may hold values from -6 to 6
- forward_now: float32 [16, 128, 64, 256], P('shot', 'tx', 'ty'), may hold values from -6 to 6
- adjoint_prev: float32 [16, 128, 64, 256], P('shot', 'tx', 'ty'), may hold values from -6 to 6
- adjoint_now: float32 [16, 128, 64, 256], P('shot', 'tx', 'ty'), may hold values from -6 to 6
- velocity_model: bfloat16 [32, 512, 8, 256], P(('tx', 'ty'), 'shot'), may hold values from 1.5 to 4.5
- aperture: int32 [16, 32, 32], P('shot', ('tx', 'ty')), may hold values from 0 to 511, as said below
- source_cell: int32 [16, 2], P('shot'), may hold values from 0 to 127, as said below
- source_strength: float32 [16], P('shot'), may hold values from -60 to 60
- receiver_cell: int32 [16, 128, 2], P('shot'), may hold values from 0 to 127, as said below
- receiver_trace: float32 [16, 128], P('shot'), may hold values from -60 to 60
Outputs:
- forward_next: float32 [16, 128, 64, 256], P('shot', 'tx', 'ty')
- adjoint_next: float32 [16, 128, 64, 256], P('shot', 'tx', 'ty')
- image_slab: float32 [32, 512, 8, 256], P(('tx', 'ty'), 'shot')
The draws below stay inside these ranges and needn't reach their ends.
Inputs may be any that keep to these rules, and one draw needn't show every extreme that they name: `aperture`: each list of 32 block ids (one shot, one tile position) names every owner, id // 32, at most 2 times, and some owner exactly 2 times. `source_cell`: first entry below 128, second below 64. `receiver_cell`: first entry below 128, second below 64; receivers may share a cell.
All inputs are finite; a program needn't handle non-finite values.
Results may differ from the reference program's by a relative error of at most 0.0004.
Values may be sent and summed in bfloat16 or wider, within the bound.
A program may use at most 64 MiB of HBM per device.

```python
import jax
import jax.numpy as jnp
from jax import lax

CX = 32
CY = 8
CZ = 256
SLAB = 32
NREC = 128
SURFACE_DEPTH = 8
CAP = 2
NTILE = 32
NBLK = 512
NX = 128
NY = 64
N_SHOT = 16
N_TX = 4
N_TY = 8


def draw_aperture(key, part):
    list_total = N_SHOT * NTILE
    row_keys = jax.random.split(key, list_total)
    marked_list = jax.random.randint(jax.random.fold_in(key, 11), (), 0, list_total)
    last_owner = N_SHOT - 1

    def one_list(row_key, list_number):
        key_owner, key_order, key_local = jax.random.split(row_key, 3)
        shuffled = jax.random.permutation(key_owner, N_SHOT).astype(jnp.int32)
        forced = list_number == marked_list
        spot = jnp.sum(jnp.where(shuffled == last_owner, jnp.arange(N_SHOT), 0))
        first_value = shuffled[0]
        swapped = jnp.where(jnp.arange(N_SHOT) == spot, first_value, shuffled)
        swapped = jnp.where(jnp.arange(N_SHOT) == 0, last_owner, swapped)
        shuffled = jnp.where(forced, swapped, shuffled)
        places = jnp.arange(CX)
        owner_slot = jnp.where(places < CAP, 0, 1 + (places - CAP) % max(N_SHOT - 1, 1))
        owners = shuffled[owner_slot]
        owners = owners[jax.random.permutation(key_order, CX)]
        local_ids = jax.random.randint(key_local, (CX,), 0, SLAB)
        local_ids = jnp.where(forced & (owners == last_owner), SLAB - 1, local_ids)
        return (owners * SLAB + local_ids).astype(jnp.int32)
    lists = jax.vmap(one_list)(row_keys, jnp.arange(list_total))
    return lists.reshape(N_SHOT, NTILE, CX)


def draw_source_cell(key, part):
    key_first, key_second, key_pick = jax.random.split(key, 3)
    along_x = jax.random.randint(key_first, (N_SHOT,), 0, NX)
    along_y = jax.random.randint(key_second, (N_SHOT,), 0, NY)
    picks = jax.random.randint(key_pick, (2,), 0, N_SHOT)
    shots = jnp.arange(N_SHOT)
    along_x = jnp.where(shots == picks[0], NX - 1, along_x)
    along_y = jnp.where(shots == picks[1], NY - 1, along_y)
    return jnp.stack([along_x, along_y], axis=1).astype(jnp.int32)


def draw_receiver_cell(key, part):
    key_first, key_second, key_pick = jax.random.split(jax.random.fold_in(key, 7), 3)
    along_x = jax.random.randint(key_first, (N_SHOT, NREC), 0, NX)
    along_y = jax.random.randint(key_second, (N_SHOT, NREC), 0, NY)
    picks = jax.random.randint(key_pick, (2,), 0, N_SHOT * NREC)
    flat = jnp.arange(N_SHOT * NREC).reshape(N_SHOT, NREC)
    along_x = jnp.where(flat == picks[0], NX - 1, along_x)
    along_y = jnp.where(flat == picks[1], NY - 1, along_y)
    return jnp.stack([along_x, along_y], axis=2).astype(jnp.int32)


def levels(rng, shape, cuts, low, largest):
    level, own = 1.0, jax.random.fold_in(rng, 6)
    for dim, parts in cuts:
        heights = jnp.exp(jax.random.uniform(jax.random.fold_in(own, dim), (parts,), jnp.float32, low / len(cuts), largest / len(cuts)))
        level = level * jnp.repeat(heights, shape[dim] // parts).reshape([-1 if axis == dim else 1 for axis in range(len(shape))])
    return level


def noise(stream_key, dims, spread, most, shards=(), kind=jnp.bfloat16):
    gain = levels(stream_key, dims, shards, -0.22, 0.18) if shards else 1.0
    result = jax.random.normal(stream_key, dims, jnp.float32) * spread * gain
    return jnp.minimum(jnp.maximum(result, -most), most).astype(kind)


def setup_inputs(seed: int = 0) -> dict:
    keys = jax.random.split(jax.random.key(seed), 11)
    return {
        "forward_prev": noise(keys[0], (N_SHOT, NX, NY, CZ), 1.0, 6.0, ((0, 16), (1, 4), (2, 8)), jnp.float32),
        "forward_now": noise(keys[1], (N_SHOT, NX, NY, CZ), 1.0, 6.0, ((0, 16), (1, 4), (2, 8)), jnp.float32),
        "adjoint_prev": noise(keys[2], (N_SHOT, NX, NY, CZ), 1.0, 6.0, ((0, 16), (1, 4), (2, 8)), jnp.float32),
        "adjoint_now": noise(keys[3], (N_SHOT, NX, NY, CZ), 1.0, 6.0, ((0, 16), (1, 4), (2, 8)), jnp.float32),
        "velocity_model": jnp.clip(1.5 + 3.0 * jax.random.uniform(keys[4], (NTILE, NBLK, CY, CZ), jnp.float32) ** levels(keys[4], (NTILE, NBLK, CY, CZ), ((0, 32), (1, 16)), -0.2, 0.2), 1.5, 4.5).astype(jnp.bfloat16),
        "aperture": draw_aperture(jax.random.fold_in(keys[10], 71), 0),
        "source_cell": draw_source_cell(jax.random.fold_in(keys[10], 71), 0),
        "source_strength": noise(keys[7], (N_SHOT,), 10.0, 60.0, ((0, 16),), jnp.float32),
        "receiver_cell": draw_receiver_cell(jax.random.fold_in(keys[10], 71), 0),
        "receiver_trace": noise(keys[9], (N_SHOT, NREC), 10.0, 60.0, ((0, 16),), jnp.float32),
    }


STENCIL_WEIGHTS = (-205.0 / 72.0, 8.0 / 5.0, -1.0 / 5.0, 8.0 / 315.0, -1.0 / 560.0)
STEP_RATIO = 0.1


def laplacian(padded):
    extent_x = padded.shape[-3] - 8
    extent_y = padded.shape[-2] - 8
    extent_z = padded.shape[-1] - 8
    centre = padded[..., 4:4 + extent_x, 4:4 + extent_y, 4:4 + extent_z]
    summed = (3.0 * STENCIL_WEIGHTS[0]) * centre
    for offset in range(1, 5):
        neighbours = (padded[..., 4 + offset:4 + offset + extent_x, 4:4 + extent_y, 4:4 + extent_z]
                      + padded[..., 4 - offset:4 - offset + extent_x, 4:4 + extent_y, 4:4 + extent_z]
                      + padded[..., 4:4 + extent_x, 4 + offset:4 + offset + extent_y, 4:4 + extent_z]
                      + padded[..., 4:4 + extent_x, 4 - offset:4 - offset + extent_y, 4:4 + extent_z]
                      + padded[..., 4:4 + extent_x, 4:4 + extent_y, 4 + offset:4 + offset + extent_z]
                      + padded[..., 4:4 + extent_x, 4:4 + extent_y, 4 - offset:4 - offset + extent_z])
        summed = summed + STENCIL_WEIGHTS[offset] * neighbours
    return summed


def injections(anchor_x, anchor_y, cells_x, cells_y, cells_z, source_xy, strength, receiver_xy, traces):
    grid_x = lax.iota(jnp.int32, cells_x) + anchor_x
    grid_y = lax.iota(jnp.int32, cells_y) + anchor_y
    depth_mark = (lax.iota(jnp.int32, cells_z) == SURFACE_DEPTH).astype(jnp.float32)
    mark_x = (grid_x == source_xy[0]).astype(jnp.float32)
    mark_y = (grid_y == source_xy[1]).astype(jnp.float32)
    injected = strength * mark_x[:, None, None] * mark_y[None, :, None] * depth_mark[None, None, :]
    receiver_x = (receiver_xy[:, 0][:, None] == grid_x[None, :]).astype(jnp.float32) * traces[:, None]
    receiver_y = (receiver_xy[:, 1][:, None] == grid_y[None, :]).astype(jnp.float32)
    surface = jnp.dot(receiver_x.T, receiver_y, precision=lax.Precision.HIGHEST)
    recorded = surface[:, :, None] * depth_mark[None, None, :]
    return injected, recorded


def reference(forward_prev, forward_now, adjoint_prev, adjoint_now, velocity_model, aperture,
              source_cell, source_strength, receiver_cell, receiver_trace):
    tile_index = jnp.arange(NTILE, dtype=jnp.int32)[:, None]

    def one_shot(image_sum, inputs):
        f_prev, f_now, a_prev, a_now, block_ids, source_xy, strength, receiver_xy, traces = inputs
        tiles = velocity_model[tile_index, block_ids].astype(jnp.float32)
        tiles = tiles.reshape(N_TX, N_TY, CX, CY, CZ).transpose(0, 2, 1, 3, 4).reshape(NX, NY, CZ)
        scaled = tiles * STEP_RATIO
        courant = scaled * scaled
        injected, recorded = injections(0, 0, NX, NY, CZ, source_xy, strength, receiver_xy, traces)
        pads = ((4, 4), (4, 4), (4, 4))
        f_next = 2.0 * f_now - f_prev + courant * (laplacian(jnp.pad(f_now, pads)) + injected)
        a_next = 2.0 * a_now - a_prev + courant * (laplacian(jnp.pad(a_now, pads)) + recorded)
        correlation = (f_next * a_next).reshape(N_TX, CX, N_TY, CY, CZ).transpose(0, 2, 1, 3, 4)
        correlation = correlation.reshape(NTILE, CX, CY, CZ)
        image_sum = image_sum.at[tile_index, block_ids].add(correlation)
        return image_sum, (f_next, a_next)

    start_image = jnp.zeros((NTILE, NBLK, CY, CZ), jnp.float32)
    image_slab, outputs = lax.scan(one_shot, start_image,
                                   (forward_prev, forward_now, adjoint_prev, adjoint_now, aperture,
                                    source_cell, source_strength, receiver_cell, receiver_trace))
    return outputs[0], outputs[1], image_slab
```

```python
import functools

import jax
import jax.numpy as jnp
import ml_dtypes
import numpy as np
from jax import lax
from jax.experimental import pallas as pl
from jax.experimental.pallas import tpu as pltpu
from jax.sharding import PartitionSpec as P

SURFACE_DEPTH = 8
STENCIL_WEIGHTS = (-205.0 / 72.0, 8.0 / 5.0, -1.0 / 5.0, 8.0 / 315.0, -1.0 / 560.0)
STEP_RATIO = 0.1
MESH = pl.DeviceIdType.MESH
NS, NTX, NTY = 16, 4, 8
CX, CY, CZ = 32, 8, 256
ROWS = CX * CY
SLAB = 32
NREC = 128
YH = CX * 4
XH = 4 * CY
HALO = 2 * YH + 2 * XH


def stencil_constants():
    w = np.array(STENCIL_WEIGHTS)
    band = np.zeros(600)
    band[1:5] = w[1:]
    row = np.arange(ROWS)
    x, y = row // CY, row % CY
    dx, dy = np.abs(x[:, None] - x[None, :]), np.abs(y[:, None] - y[None, :])
    inner = band[dx] * (dy == 0) + band[dy] * (dx == 0) + 3.0 * w[0] * ((dx == 0) & (dy == 0))
    z = np.arange(CZ)
    depth = band[np.abs(z[:, None] - z[None, :])]
    pick = np.zeros((ROWS, ROWS))
    halo = np.zeros((ROWS, 384))
    for cx in range(CX):
        for q in range(4):
            pick[cx * 4 + q, cx * CY + CY - 4 + q] = 1.0
            pick[YH + cx * 4 + q, cx * CY + q] = 1.0
            for cy in range(CY):
                halo[cx * CY + cy, cx * 4 + q] = band[cy + 4 - q]
                halo[cx * CY + cy, YH + cx * 4 + q] = band[CY + q - cy]
    for q in range(4):
        for cx in range(CX):
            for cy in range(CY):
                halo[cx * CY + cy, 2 * YH + q * CY + cy] = band[cx + 4 - q]
                halo[cx * CY + cy, 2 * YH + XH + q * CY + cy] = band[CX + q - cx]

    def parts(matrix):
        high = matrix.astype(np.float32).astype(ml_dtypes.bfloat16)
        low = (matrix - high.astype(np.float64)).astype(np.float32).astype(ml_dtypes.bfloat16)
        return [high, low]

    square = np.concatenate(parts(inner) + parts(depth) + parts(pick)[:1], axis=0)
    return square, np.concatenate(parts(halo), axis=0)


def mm(a, b):
    return jnp.dot(a, b, preferred_element_type=jnp.float32)


def kernel(
    f_prev, f_now, a_prev, a_now, velocity, aperture, source_cell, strength, receivers, traces,
    square_hbm, halo_hbm,
    f_out, a_out, image_out,
    now, prev, lap, high, low, slab_b, slab, ids, cell_v, trace_v, square, halo_w,
    pick_send, halo, tables, wanted, wanted_v, wanted_by, blocks, arrived, speed, corr_send, corr_in,
    hit, image,
    smem_tables, source_s, strength_s,
    load_sem, table_sem, id_send, id_recv, halo_send, halo_recv, v_send, v_recv, c_send, c_recv,
    out_sem,
):
    me = lax.axis_index("shot")
    tx = lax.axis_index("tx")
    ty = lax.axis_index("ty")

    loads = [
        pltpu.make_async_copy(aperture.at[0], ids, load_sem.at[0]),
        pltpu.make_async_copy(f_now.at[0], now.at[0], load_sem.at[1]),
        pltpu.make_async_copy(a_now.at[0], now.at[1], load_sem.at[2]),
        pltpu.make_async_copy(square_hbm, square, load_sem.at[3]),
        pltpu.make_async_copy(velocity.at[0], slab_b, load_sem.at[4]),
        pltpu.make_async_copy(halo_hbm, halo_w, load_sem.at[5]),
        pltpu.make_async_copy(f_prev.at[0], prev.at[0], load_sem.at[6]),
        pltpu.make_async_copy(a_prev.at[0], prev.at[1], load_sem.at[7]),
        pltpu.make_async_copy(receivers.at[0], cell_v, load_sem.at[8]),
        pltpu.make_async_copy(traces, trace_v, load_sem.at[9]),
        pltpu.make_async_copy(source_cell, source_s, load_sem.at[10]),
        pltpu.make_async_copy(strength, strength_s, load_sem.at[11]),
    ]
    for load in loads:
        load.start()

    barrier = pltpu.get_barrier_semaphore()

    @pl.loop(1, NS)
    def _(d):
        pl.semaphore_signal(
            barrier, inc=1, device_id={"shot": lax.rem(me + d, NS)}, device_id_type=MESH
        )

    sides = [
        (ty < NTY - 1, "ty", ty + 1),
        (ty > 0, "ty", ty - 1),
        (tx < NTX - 1, "tx", tx + 1),
        (tx > 0, "tx", tx - 1),
    ]
    for present, axis, other in sides:

        @pl.when(present)
        def _():
            pl.semaphore_signal(barrier, inc=1, device_id={axis: other}, device_id_type=MESH)

    for present, start, size in (
        (ty > 0, 0, YH),
        (ty < NTY - 1, YH, YH),
        (tx > 0, 2 * YH, XH),
        (tx < NTX - 1, 2 * YH + XH, XH),
    ):

        @pl.when(jnp.logical_not(present))
        def _():
            halo[:, start : start + size, :] = jnp.zeros((2, size, CZ), jnp.bfloat16)

    loads[0].wait()
    row_l = lax.broadcasted_iota(jnp.int32, (CX, CX), 1)
    row_s = lax.broadcasted_iota(jnp.int32, (CX, CX), 0)
    ids_l = jnp.broadcast_to(ids[...], (CX, CX))
    ids_s = ids_l.T
    earlier = ((ids_s >> 5) == (ids_l >> 5)) & (row_s < row_l)
    rank = jnp.sum(earlier.astype(jnp.int32), axis=0, keepdims=True)
    slot = 2 * (ids[...] >> 5) + rank
    placed = jnp.broadcast_to(slot, (CX, CX)).T == row_l
    tables[0, :, 0:CX] = slot
    tables[1, :, 0:CX] = jnp.sum(jnp.where(placed, row_s, 0), axis=0, keepdims=True)
    wanted[:, 0:CX] = jnp.sum(jnp.where(placed, ids_s & (SLAB - 1), 0), axis=0, keepdims=True)
    table_copy = pltpu.make_async_copy(tables, smem_tables, table_sem.at[0])
    table_copy.start()
    own_copy = pltpu.make_async_copy(wanted, wanted_by.at[me], table_sem.at[1])
    own_copy.start()

    for field in range(2):
        loads[1 + field].wait()
        u = now[field].reshape(ROWS, CZ)
        top = u.astype(jnp.bfloat16)
        high[field] = top
        low[field] = (u - top.astype(jnp.float32)).astype(jnp.bfloat16)
    loads[3].wait()
    for field in range(2):
        picked = mm(square[4 * ROWS : 5 * ROWS, :], high[field]).astype(jnp.bfloat16)
        pick_send[0, field] = picked[0:YH]
        pick_send[1, field] = picked[YH:]

    partners = (
        NS - 1
        + (ty > 0).astype(jnp.int32)
        + (ty < NTY - 1).astype(jnp.int32)
        + (tx > 0).astype(jnp.int32)
        + (tx < NTX - 1).astype(jnp.int32)
    )
    pl.semaphore_wait(barrier, partners)

    def id_copy(d):
        return pltpu.make_async_remote_copy(
            src_ref=wanted,
            dst_ref=wanted_v.at[me],
            send_sem=id_send.at[d],
            recv_sem=id_recv.at[d],
            device_id={"shot": lax.rem(me + d, NS)},
            device_id_type=MESH,
        )

    @pl.loop(1, NS)
    def _(d):
        id_copy(d).start()

    def halo_copy(n):
        axis, other = sides[n][1], sides[n][2]
        start = (0, YH, 2 * YH, 2 * YH + XH)[n]
        if n < 2:
            source, size = pick_send.at[n], YH
        else:
            source, size = high.at[:, pl.ds((CX - 4) * CY if n == 2 else 0, XH)], XH
        return pltpu.make_async_remote_copy(
            src_ref=source,
            dst_ref=halo.at[:, pl.ds(start, size)],
            send_sem=halo_send.at[n],
            recv_sem=halo_recv.at[n],
            device_id={axis: other},
            device_id_type=MESH,
        )

    for n in (2, 3, 0, 1):

        @pl.when(sides[n][0])
        def _():
            halo_copy(n).start()

    loads[4].wait()
    slab[...] = slab_b[...].astype(jnp.float32)

    own_copy.wait()
    depth_l = lax.broadcasted_iota(jnp.int32, (CY, ROWS), 1)
    same_y = (depth_l & (CY - 1)) == lax.broadcasted_iota(jnp.int32, (CY, ROWS), 0)
    block_l = jnp.where(same_y, depth_l >> 3, -1)

    def serve(shot):
        first = wanted_by[shot, 0, 2 * me]
        second = wanted_by[shot, 0, 2 * me + 1]
        pair = jnp.concatenate([slab[first], slab[second]], axis=0).astype(jnp.bfloat16)
        hits = jnp.concatenate([block_l == first, block_l == second], axis=0)
        hit[pl.ds(pl.multiple_of(shot * 16, 16), 16), :] = jnp.where(hits, 1.0, 0.0)
        return pair

    arrived[me] = serve(me)

    def block_copy(d):
        shot = lax.rem(me - d + NS, NS)
        return pltpu.make_async_remote_copy(
            src_ref=blocks.at[shot],
            dst_ref=arrived.at[me],
            send_sem=v_send.at[d],
            recv_sem=v_recv.at[d],
            device_id={"shot": shot},
            device_id_type=MESH,
        )

    @pl.loop(1, NS)
    def _(d):
        id_copy(d).wait_recv()
        shot = lax.rem(me - d + NS, NS)
        local = pltpu.make_async_copy(wanted_v.at[shot], wanted_by.at[shot], table_sem.at[1])
        local.start()
        local.wait()
        blocks[shot] = serve(shot)
        block_copy(d).start()

    for field in range(2):
        top, rest = high[field], low[field]
        lap[field] = (
            mm(square[0:ROWS, :], top)
            + mm(square[0:ROWS, :], rest)
            + mm(square[ROWS : 2 * ROWS, :], top)
            + mm(top, square[2 * ROWS : 3 * ROWS, :])
            + mm(rest, square[2 * ROWS : 3 * ROWS, :])
            + mm(top, square[3 * ROWS : 4 * ROWS, :])
        ).reshape(CX, CY, CZ)

    for load in loads[8:]:
        load.wait()
    row = lax.broadcasted_iota(jnp.int32, (ROWS, 1), 0)

    def local_row(along_x, along_y):
        inside = (along_x >= tx * CX) & (along_x < tx * CX + CX)
        inside = inside & (along_y >= ty * CY) & (along_y < ty * CY + CY)
        return jnp.where(inside, (along_x - tx * CX) * CY + along_y - ty * CY, -1)

    source_row = local_row(source_s[0, 0], source_s[0, 1])
    cell_row = local_row(cell_v[0:1, :], cell_v[1:2, :])
    injected = jnp.where(row == source_row, strength_s[0], 0.0)
    recorded = jnp.sum(
        jnp.where(jnp.broadcast_to(row, (ROWS, NREC)) == cell_row, trace_v[...], 0.0),
        axis=1,
        keepdims=True,
    )
    surface = lax.broadcasted_iota(jnp.int32, (ROWS, CZ), 1) == SURFACE_DEPTH

    loads[5].wait()
    loads[6].wait()
    loads[7].wait()
    for n in (2, 3, 0, 1):
        came_from = sides[(1, 0, 3, 2)[n]][0]

        @pl.when(came_from)
        def _():
            halo_copy(n).wait_recv()

    for field, extra in ((0, injected), (1, recorded)):
        layers = halo[field]
        beyond = mm(halo_w[0:ROWS, 0:HALO], layers) + mm(halo_w[ROWS:, 0:HALO], layers)
        beyond = beyond + jnp.where(surface, jnp.broadcast_to(extra, (ROWS, CZ)), 0.0)
        lap[field] = lap[field] + beyond.reshape(CX, CY, CZ)
        prev[field] = 2.0 * now[field] - prev[field]

    table_copy.wait()

    def corr_copy(d):
        owner = lax.rem(me + d, NS)
        return pltpu.make_async_remote_copy(
            src_ref=corr_send.at[owner],
            dst_ref=corr_in.at[me],
            send_sem=c_send.at[d],
            recv_sem=c_recv.at[d],
            device_id={"shot": owner},
            device_id_type=MESH,
        )

    def contribute(owner):
        pair = arrived[owner].astype(jnp.float32)
        products = []
        for k in range(2):
            scaled = pair[k * CY : (k + 1) * CY] * STEP_RATIO
            courant = scaled * scaled
            speed[2 * owner + k] = courant
            r = smem_tables[1, 0, 2 * owner + k]
            products.append(
                (prev[0, r] + courant * lap[0, r]) * (prev[1, r] + courant * lap[1, r])
            )
        both = jnp.concatenate(products, axis=0)
        top = both.astype(jnp.bfloat16)
        return top, (both - top.astype(jnp.float32)).astype(jnp.bfloat16)

    corr_in[me, 0], corr_in[me, 1] = contribute(me)

    @pl.loop(1, NS)
    def _(d):
        block_copy(d).wait_recv()
        owner = lax.rem(me + d, NS)
        corr_send[owner, 0], corr_send[owner, 1] = contribute(owner)
        corr_copy(d).start()

    @pl.loop(0, CX)
    def _(r):
        courant = speed[smem_tables[0, 0, r]]
        for field in range(2):
            prev[field, r] = prev[field, r] + courant * lap[field, r]

    outs = [
        pltpu.make_async_copy(prev.at[0], f_out.at[0], out_sem.at[0]),
        pltpu.make_async_copy(prev.at[1], a_out.at[0], out_sem.at[1]),
        pltpu.make_async_copy(image, image_out.at[0], out_sem.at[2]),
    ]
    outs[0].start()
    outs[1].start()
    chosen = hit[...].T.astype(jnp.bfloat16)

    @pl.loop(1, NS)
    def _(d):
        corr_copy(d).wait_recv()

    tops = corr_in[:, 0].reshape(ROWS, CZ)
    rests = corr_in[:, 1].reshape(ROWS, CZ)
    image[...] = (mm(chosen, tops) + mm(chosen, rests)).reshape(SLAB, CY, CZ)
    outs[2].start()

    @pl.loop(1, NS)
    def _(d):
        id_copy(d).wait_send()
        block_copy(d).wait_send()
        corr_copy(d).wait_send()

    for n in range(4):

        @pl.when(sides[n][0])
        def _():
            halo_copy(n).wait_send()

    for out in outs:
        out.wait()


def on_device(*arrays):
    arrays = arrays[:8] + (jnp.swapaxes(arrays[8], 1, 2),) + arrays[9:]
    square, halo_w = stencil_constants()
    field = jax.ShapeDtypeStruct((1, CX, CY, CZ), jnp.float32)
    dma = pltpu.SemaphoreType.DMA
    bf, f32, i32 = jnp.bfloat16, jnp.float32, jnp.int32
    scratch = [
        pltpu.VMEM((2, CX, CY, CZ), f32),
        pltpu.VMEM((2, CX, CY, CZ), f32),
        pltpu.VMEM((2, CX, CY, CZ), f32),
        pltpu.VMEM((2, ROWS, CZ), bf),
        pltpu.VMEM((2, ROWS, CZ), bf),
        pltpu.VMEM((SLAB, CY, CZ), bf),
        pltpu.VMEM((SLAB, CY, CZ), f32),
        pltpu.VMEM((1, CX), i32),
        pltpu.VMEM((2, NREC), i32),
        pltpu.VMEM((1, NREC), f32),
        pltpu.VMEM(square.shape, bf),
        pltpu.VMEM(halo_w.shape, bf),
        pltpu.VMEM((2, 2, YH, CZ), bf),
        pltpu.VMEM((2, HALO, CZ), bf),
        pltpu.VMEM((2, 1, 128), i32),
        pltpu.VMEM((1, 128), i32),
        pltpu.VMEM((NS, 1, 128), i32),
        pltpu.SMEM((NS, 1, 128), i32),
        pltpu.VMEM((NS, 2 * CY, CZ), bf),
        pltpu.VMEM((NS, 2 * CY, CZ), bf),
        pltpu.VMEM((2 * NS, CY, CZ), f32),
        pltpu.VMEM((NS, 2, 2 * CY, CZ), bf),
        pltpu.VMEM((NS, 2, 2 * CY, CZ), bf),
        pltpu.VMEM((ROWS, ROWS), f32),
        pltpu.VMEM((SLAB, CY, CZ), f32),
        pltpu.SMEM((2, 1, 128), i32),
        pltpu.SMEM((1, 2), i32),
        pltpu.SMEM((1,), f32),
        dma((12,)),
        dma((2,)),
        dma((NS,)),
        dma((NS,)),
        dma((4,)),
        dma((4,)),
        dma((NS,)),
        dma((NS,)),
        dma((NS,)),
        dma((NS,)),
        dma((3,)),
    ]
    anywhere = pl.BlockSpec(memory_space=pl.ANY)
    hbm = pl.BlockSpec(memory_space=pltpu.HBM)
    return pl.pallas_call(
        kernel,
        out_shape=(field, field, field),
        in_specs=[hbm] * 12,
        out_specs=(anywhere,) * 3,
        scratch_shapes=scratch,
        compiler_params=pltpu.CompilerParams(
            collective_id=0, has_side_effects=True, vmem_limit_bytes=64 * 1024 * 1024
        ),
    )(*arrays, jnp.asarray(square), jnp.asarray(halo_w))


def solution(mesh):
    in_specs = (
        P("shot", "tx", "ty", None),
        P("shot", "tx", "ty", None),
        P("shot", "tx", "ty", None),
        P("shot", "tx", "ty", None),
        P(("tx", "ty"), "shot", None, None),
        P("shot", ("tx", "ty"), None),
        P("shot", None),
        P("shot"),
        P("shot", None, None),
        P("shot", None),
    )
    out_specs = (
        P("shot", "tx", "ty", None),
        P("shot", "tx", "ty", None),
        P(("tx", "ty"), "shot", None, None),
    )
    return jax.shard_map(
        on_device, mesh=mesh, in_specs=in_specs, out_specs=out_specs, check_vma=False
    )
```

```python
import functools

import jax
import jax.numpy as jnp
import ml_dtypes
import numpy as np
from jax import lax
from jax.experimental import pallas as pl
from jax.experimental.pallas import tpu as pltpu
from jax.sharding import PartitionSpec as P

SURFACE_DEPTH = 8
STENCIL_WEIGHTS = (-205.0 / 72.0, 8.0 / 5.0, -1.0 / 5.0, 8.0 / 315.0, -1.0 / 560.0)
STEP_RATIO = 0.1
MESH = pl.DeviceIdType.MESH
NS, NTX, NTY = 16, 4, 8
CX, CY, CZ = 32, 8, 256
ROWS = CX * CY
SLAB = 32
NREC = 128
YH = CX * 4
XH = 4 * CY
HALO = 2 * YH + 2 * XH
AHEAD = 4
LIMIT = 62 * 1024 * 1024


def stencil_constants():
    w = np.array(STENCIL_WEIGHTS)
    band = np.zeros(600)
    band[1:5] = w[1:]
    row = np.arange(ROWS)
    x, y = row // CY, row % CY
    dx, dy = np.abs(x[:, None] - x[None, :]), np.abs(y[:, None] - y[None, :])
    inner = band[dx] * (dy == 0) + band[dy] * (dx == 0) + 3.0 * w[0] * ((dx == 0) & (dy == 0))
    z = np.arange(CZ)
    depth = band[np.abs(z[:, None] - z[None, :])]
    pick = np.zeros((ROWS, ROWS))
    halo = np.zeros((ROWS, 384))
    for cx in range(CX):
        for q in range(4):
            pick[cx * 4 + q, cx * CY + CY - 4 + q] = 1.0
            pick[YH + cx * 4 + q, cx * CY + q] = 1.0
            for cy in range(CY):
                halo[cx * CY + cy, cx * 4 + q] = band[cy + 4 - q]
                halo[cx * CY + cy, YH + cx * 4 + q] = band[CY + q - cy]
    for q in range(4):
        for cx in range(CX):
            for cy in range(CY):
                halo[cx * CY + cy, 2 * YH + q * CY + cy] = band[cx + 4 - q]
                halo[cx * CY + cy, 2 * YH + XH + q * CY + cy] = band[CX + q - cx]

    def parts(matrix):
        high = matrix.astype(np.float32).astype(ml_dtypes.bfloat16)
        low = (matrix - high.astype(np.float64)).astype(np.float32).astype(ml_dtypes.bfloat16)
        return [high, low]

    square = np.concatenate(parts(inner) + parts(depth) + parts(pick)[:1], axis=0)
    return square, np.concatenate(parts(halo), axis=0)


def mm(a, b):
    return jnp.dot(a, b, preferred_element_type=jnp.float32)


def kernel(
    f_prev, f_now, a_prev, a_now, velocity, aperture, source_cell, strength, receivers, traces,
    square_hbm, halo_hbm,
    prev, corr_in, hit_out,
    now, lap, high, low, slab_b, slab, ids, cell_v, trace_v, square, halo_w,
    pick_send, halo, tables, wanted, wanted_v, wanted_by, blocks, arrived, speed, corr_send,
    hit,
    smem_tables, source_s, strength_s,
    load_sem, table_sem, id_sem, id_send, id_recv, halo_send, halo_recv, v_send, v_recv,
    c_send, c_recv, ready,
):
    me = lax.axis_index("shot")
    tx = lax.axis_index("tx")
    ty = lax.axis_index("ty")

    loads = [
        pltpu.make_async_copy(aperture.at[0], ids, load_sem.at[0]),
        pltpu.make_async_copy(f_now.at[0], now.at[0], load_sem.at[1]),
        pltpu.make_async_copy(a_now.at[0], now.at[1], load_sem.at[2]),
        pltpu.make_async_copy(square_hbm, square, load_sem.at[3]),
        pltpu.make_async_copy(velocity.at[0], slab_b, load_sem.at[4]),
        pltpu.make_async_copy(halo_hbm, halo_w, load_sem.at[5]),
        pltpu.make_async_copy(f_prev.at[0], prev.at[0], load_sem.at[6]),
        pltpu.make_async_copy(a_prev.at[0], prev.at[1], load_sem.at[7]),
        pltpu.make_async_copy(receivers.at[0], cell_v, load_sem.at[8]),
        pltpu.make_async_copy(traces, trace_v, load_sem.at[9]),
        pltpu.make_async_copy(source_cell, source_s, load_sem.at[10]),
        pltpu.make_async_copy(strength, strength_s, load_sem.at[11]),
    ]
    for load in loads:
        load.start()

    barrier = pltpu.get_barrier_semaphore()

    @pl.loop(1, NS)
    def _(d):
        pl.semaphore_signal(
            barrier, inc=1, device_id={"shot": lax.rem(me + d, NS)}, device_id_type=MESH
        )

    odd = lax.rem(tx, 2) == 1
    sides = [
        (ty < NTY - 1, "ty", ty + 1),
        (ty > 0, "ty", ty - 1),
        (tx < NTX - 1, "tx", tx + 1),
        (tx > 0, "tx", tx - 1),
    ]
    first = [ty < NTY - 1, None, odd & (tx < NTX - 1), odd & (tx > 0)]
    second = [None, ty > 0, jnp.logical_not(odd) & (tx < NTX - 1), jnp.logical_not(odd) & (tx > 0)]
    for n in (0, 2, 3):

        @pl.when(first[n])
        def _():
            axis, other = sides[n][1:]
            pl.semaphore_signal(barrier, inc=1, device_id={axis: other}, device_id_type=MESH)

    for present, start, size in (
        (ty > 0, 0, YH),
        (ty < NTY - 1, YH, YH),
        (tx > 0, 2 * YH, XH),
        (tx < NTX - 1, 2 * YH + XH, XH),
    ):

        @pl.when(jnp.logical_not(present))
        def _():
            halo[:, start : start + size, :] = jnp.zeros((2, size, CZ), jnp.bfloat16)

    loads[0].wait()
    row_l = lax.broadcasted_iota(jnp.int32, (CX, CX), 1)
    row_s = lax.broadcasted_iota(jnp.int32, (CX, CX), 0)
    ids_l = jnp.broadcast_to(ids[...], (CX, CX))
    ids_s = ids_l.T
    earlier = ((ids_s >> 5) == (ids_l >> 5)) & (row_s < row_l)
    rank = jnp.sum(earlier.astype(jnp.int32), axis=0, keepdims=True)
    slot = 2 * (ids[...] >> 5) + rank
    placed = jnp.broadcast_to(slot, (CX, CX)).T == row_l
    tables[0, :, 0:CX] = slot
    tables[1, :, 0:CX] = jnp.sum(jnp.where(placed, row_s, 0), axis=0, keepdims=True)
    wanted[:, 0:CX] = jnp.sum(jnp.where(placed, ids_s & (SLAB - 1), 0), axis=0, keepdims=True)
    table_copy = pltpu.make_async_copy(tables, smem_tables, table_sem.at[0])
    table_copy.start()
    own_copy = pltpu.make_async_copy(wanted, wanted_by.at[me], table_sem.at[1])
    own_copy.start()

    for field in range(2):
        loads[1 + field].wait()
        u = now[field].reshape(ROWS, CZ)
        top = u.astype(jnp.bfloat16)
        high[field] = top
        low[field] = (u - top.astype(jnp.float32)).astype(jnp.bfloat16)
    loads[3].wait()
    for field in range(2):
        picked = mm(square[4 * ROWS : 5 * ROWS, :], high[field]).astype(jnp.bfloat16)
        pick_send[0, field] = picked[0:YH]
        pick_send[1, field] = picked[YH:]

    partners = NS - 1
    for n in (1, 2, 3):
        partners = partners + second[n].astype(jnp.int32)
    pl.semaphore_wait(barrier, partners)

    for n in (1, 2, 3):

        @pl.when(second[n])
        def _():
            axis, other = sides[n][1:]
            pl.semaphore_signal(
                ready.at[(1, 0, 3, 2)[n]], inc=1, device_id={axis: other}, device_id_type=MESH
            )

    def id_copy(d):
        return pltpu.make_async_remote_copy(
            src_ref=wanted,
            dst_ref=wanted_v.at[me],
            send_sem=id_send.at[d],
            recv_sem=id_recv.at[d],
            device_id={"shot": lax.rem(me + d, NS)},
            device_id_type=MESH,
        )

    @pl.loop(1, NS)
    def _(d):
        id_copy(d).start()

    def halo_copy(n):
        axis, other = sides[n][1], sides[n][2]
        start = (0, YH, 2 * YH, 2 * YH + XH)[n]
        if n < 2:
            source, size = pick_send.at[n], YH
        else:
            source, size = high.at[:, pl.ds((CX - 4) * CY if n == 2 else 0, XH)], XH
        return pltpu.make_async_remote_copy(
            src_ref=source,
            dst_ref=halo.at[:, pl.ds(start, size)],
            send_sem=halo_send.at[n],
            recv_sem=halo_recv.at[n],
            device_id={axis: other},
            device_id_type=MESH,
        )

    for n in (2, 3, 1):

        @pl.when(second[n])
        def _():
            halo_copy(n).start()

    def answer(n):
        @pl.when(first[n])
        def _():
            pl.semaphore_wait(ready.at[n], 1)
            halo_copy(n).start()

    loads[4].wait()
    slab[...] = slab_b[...].astype(jnp.float32)

    own_copy.wait()
    depth_l = lax.broadcasted_iota(jnp.int32, (CY, ROWS), 1)
    same_y = (depth_l & (CY - 1)) == lax.broadcasted_iota(jnp.int32, (CY, ROWS), 0)
    block_l = jnp.where(same_y, depth_l >> 3, -1)

    def serve(shot):
        first = wanted_by[shot, 0, 2 * me]
        second = wanted_by[shot, 0, 2 * me + 1]
        pair = jnp.concatenate([slab[first], slab[second]], axis=0).astype(jnp.bfloat16)
        hits = jnp.concatenate([block_l == first, block_l == second], axis=0)
        hit[pl.ds(pl.multiple_of(shot * 16, 16), 16), :] = jnp.where(hits, 1.0, 0.0)
        return pair

    arrived[me] = serve(me)

    def block_copy(d):
        shot = lax.rem(me - d + NS, NS)
        return pltpu.make_async_remote_copy(
            src_ref=blocks.at[shot],
            dst_ref=arrived.at[me],
            send_sem=v_send.at[d],
            recv_sem=v_recv.at[d],
            device_id={"shot": shot},
            device_id_type=MESH,
        )

    def id_local(d):
        shot = lax.rem(me - d + NS, NS)
        return pltpu.make_async_copy(wanted_v.at[shot], wanted_by.at[shot], id_sem.at[d])

    @pl.loop(1, NS + AHEAD)
    def _(step):
        @pl.when(step < NS)
        def _():
            id_copy(step).wait_recv()
            id_local(step).start()

        @pl.when(step > AHEAD)
        def _():
            d = step - AHEAD
            id_local(d).wait()
            shot = lax.rem(me - d + NS, NS)
            blocks[shot] = serve(shot)
            block_copy(d).start()

    answer(0)

    for field in range(2):
        top, rest = high[field], low[field]
        lap[field] = (
            mm(square[0:ROWS, :], top)
            + mm(square[0:ROWS, :], rest)
            + mm(square[ROWS : 2 * ROWS, :], top)
            + mm(top, square[2 * ROWS : 3 * ROWS, :])
            + mm(rest, square[2 * ROWS : 3 * ROWS, :])
            + mm(top, square[3 * ROWS : 4 * ROWS, :])
        ).reshape(CX, CY, CZ)

    for load in loads[8:]:
        load.wait()
    row = lax.broadcasted_iota(jnp.int32, (ROWS, 1), 0)

    def local_row(along_x, along_y):
        inside = (along_x >= tx * CX) & (along_x < tx * CX + CX)
        inside = inside & (along_y >= ty * CY) & (along_y < ty * CY + CY)
        return jnp.where(inside, (along_x - tx * CX) * CY + along_y - ty * CY, -1)

    source_row = local_row(source_s[0, 0], source_s[0, 1])
    cell_row = local_row(cell_v[0:1, :], cell_v[1:2, :])
    injected = jnp.where(row == source_row, strength_s[0], 0.0)
    recorded = jnp.sum(
        jnp.where(jnp.broadcast_to(row, (ROWS, NREC)) == cell_row, trace_v[...], 0.0),
        axis=1,
        keepdims=True,
    )
    surface = lax.broadcasted_iota(jnp.int32, (ROWS, CZ), 1) == SURFACE_DEPTH

    loads[5].wait()
    loads[6].wait()
    loads[7].wait()
    answer(3)
    answer(2)
    for n in (2, 3, 0, 1):
        came_from = sides[(1, 0, 3, 2)[n]][0]

        @pl.when(came_from)
        def _():
            halo_copy(n).wait_recv()

    for field, extra in ((0, injected), (1, recorded)):
        layers = halo[field]
        beyond = mm(halo_w[0:ROWS, 0:HALO], layers) + mm(halo_w[ROWS:, 0:HALO], layers)
        beyond = beyond + jnp.where(surface, jnp.broadcast_to(extra, (ROWS, CZ)), 0.0)
        lap[field] = lap[field] + beyond.reshape(CX, CY, CZ)
        prev[field] = 2.0 * now[field] - prev[field]

    table_copy.wait()

    def corr_copy(d):
        owner = lax.rem(me + d, NS)
        return pltpu.make_async_remote_copy(
            src_ref=corr_send.at[owner],
            dst_ref=corr_in.at[me],
            send_sem=c_send.at[d],
            recv_sem=c_recv.at[d],
            device_id={"shot": owner},
            device_id_type=MESH,
        )

    def contribute(owner):
        pair = arrived[owner].astype(jnp.float32)
        products = []
        for k in range(2):
            scaled = pair[k * CY : (k + 1) * CY] * STEP_RATIO
            courant = scaled * scaled
            speed[2 * owner + k] = courant
            r = smem_tables[1, 0, 2 * owner + k]
            products.append(
                (prev[0, r] + courant * lap[0, r]) * (prev[1, r] + courant * lap[1, r])
            )
        both = jnp.concatenate(products, axis=0)
        top = both.astype(jnp.bfloat16)
        return top, (both - top.astype(jnp.float32)).astype(jnp.bfloat16)

    corr_in[me, 0], corr_in[me, 1] = contribute(me)

    @pl.loop(1, NS)
    def _(d):
        block_copy(d).wait_recv()
        owner = lax.rem(me + d, NS)
        corr_send[owner, 0], corr_send[owner, 1] = contribute(owner)
        corr_copy(d).start()

    @pl.loop(0, CX)
    def _(r):
        courant = speed[smem_tables[0, 0, r]]
        for field in range(2):
            prev[field, r] = prev[field, r] + courant * lap[field, r]

    hit_out[...] = hit[...].T.astype(jnp.bfloat16)

    @pl.loop(1, NS)
    def _(d):
        corr_copy(d).wait_recv()

    @pl.loop(1, NS)
    def _(d):
        id_copy(d).wait_send()
        block_copy(d).wait_send()
        corr_copy(d).wait_send()

    for n in range(4):

        @pl.when(sides[n][0])
        def _():
            halo_copy(n).wait_send()


def finish(values, corr_in, hit, f_out, a_out, image_out, image, out_sem):
    outs = [
        pltpu.make_async_copy(values.at[0], f_out.at[0], out_sem.at[0]),
        pltpu.make_async_copy(values.at[1], a_out.at[0], out_sem.at[1]),
        pltpu.make_async_copy(image, image_out.at[0], out_sem.at[2]),
    ]
    outs[0].start()
    outs[1].start()
    tops = corr_in[:, 0].reshape(ROWS, CZ)
    rests = corr_in[:, 1].reshape(ROWS, CZ)
    image[...] = (mm(hit[...], tops) + mm(hit[...], rests)).reshape(SLAB, CY, CZ)
    outs[2].start()
    for out in outs:
        out.wait()


def on_device(*arrays):
    arrays = arrays[:8] + (jnp.swapaxes(arrays[8], 1, 2),) + arrays[9:]
    square, halo_w = stencil_constants()
    field = jax.ShapeDtypeStruct((1, CX, CY, CZ), jnp.float32)
    dma = pltpu.SemaphoreType.DMA
    bf, f32, i32 = jnp.bfloat16, jnp.float32, jnp.int32
    scratch = [
        pltpu.VMEM((2, CX, CY, CZ), f32),
        pltpu.VMEM((2, CX, CY, CZ), f32),
        pltpu.VMEM((2, ROWS, CZ), bf),
        pltpu.VMEM((2, ROWS, CZ), bf),
        pltpu.VMEM((SLAB, CY, CZ), bf),
        pltpu.VMEM((SLAB, CY, CZ), f32),
        pltpu.VMEM((1, CX), i32),
        pltpu.VMEM((2, NREC), i32),
        pltpu.VMEM((1, NREC), f32),
        pltpu.VMEM(square.shape, bf),
        pltpu.VMEM(halo_w.shape, bf),
        pltpu.VMEM((2, 2, YH, CZ), bf),
        pltpu.VMEM((2, HALO, CZ), bf),
        pltpu.VMEM((2, 1, 128), i32),
        pltpu.VMEM((1, 128), i32),
        pltpu.VMEM((NS, 1, 128), i32),
        pltpu.SMEM((NS, 1, 128), i32),
        pltpu.VMEM((NS, 2 * CY, CZ), bf),
        pltpu.VMEM((NS, 2 * CY, CZ), bf),
        pltpu.VMEM((2 * NS, CY, CZ), f32),
        pltpu.VMEM((NS, 2, 2 * CY, CZ), bf),
        pltpu.VMEM((ROWS, ROWS), f32),
        pltpu.SMEM((2, 1, 128), i32),
        pltpu.SMEM((1, 2), i32),
        pltpu.SMEM((1,), f32),
        dma((12,)),
        dma((2,)),
        dma((NS,)),
        dma((NS,)),
        dma((NS,)),
        dma((4,)),
        dma((4,)),
        dma((NS,)),
        dma((NS,)),
        dma((NS,)),
        dma((NS,)),
        pltpu.SemaphoreType.REGULAR((4,)),
    ]
    anywhere = pl.BlockSpec(memory_space=pl.ANY)
    vmem = pl.BlockSpec(memory_space=pltpu.VMEM)
    values, corr_in, hit = pl.pallas_call(
        kernel,
        out_shape=(
            jax.ShapeDtypeStruct((2, CX, CY, CZ), f32),
            jax.ShapeDtypeStruct((NS, 2, 2 * CY, CZ), bf),
            jax.ShapeDtypeStruct((ROWS, ROWS), bf),
        ),
        in_specs=[anywhere] * 12,
        out_specs=(vmem,) * 3,
        scratch_shapes=scratch,
        compiler_params=pltpu.CompilerParams(
            collective_id=0, has_side_effects=True, vmem_limit_bytes=LIMIT
        ),
    )(*arrays, jnp.asarray(square), jnp.asarray(halo_w))
    return pl.pallas_call(
        finish,
        out_shape=(field, field, field),
        in_specs=[vmem] * 3,
        out_specs=(anywhere,) * 3,
        scratch_shapes=[pltpu.VMEM((SLAB, CY, CZ), f32), dma((3,))],
        compiler_params=pltpu.CompilerParams(vmem_limit_bytes=LIMIT),
    )(values, corr_in, hit)


def solution(mesh):
    in_specs = (
        P("shot", "tx", "ty", None),
        P("shot", "tx", "ty", None),
        P("shot", "tx", "ty", None),
        P("shot", "tx", "ty", None),
        P(("tx", "ty"), "shot", None, None),
        P("shot", ("tx", "ty"), None),
        P("shot", None),
        P("shot"),
        P("shot", None, None),
        P("shot", None),
    )
    out_specs = (
        P("shot", "tx", "ty", None),
        P("shot", "tx", "ty", None),
        P(("tx", "ty"), "shot", None, None),
    )
    return jax.shard_map(
        on_device, mesh=mesh, in_specs=in_specs, out_specs=out_specs, check_vma=False
    )
```

```python
import functools

import jax
import jax.numpy as jnp
import ml_dtypes
import numpy as np
from jax import lax
from jax.experimental import pallas as pl
from jax.experimental.pallas import tpu as pltpu
from jax.sharding import PartitionSpec as P

SURFACE_DEPTH = 8
STENCIL_WEIGHTS = (-205.0 / 72.0, 8.0 / 5.0, -1.0 / 5.0, 8.0 / 315.0, -1.0 / 560.0)
STEP_RATIO = 0.1
MESH = pl.DeviceIdType.MESH
NS, NTX, NTY = 16, 4, 8
CX, CY, CZ = 32, 8, 256
ROWS = CX * CY
SLAB = 32
NREC = 128
YH = CX * 4
XH = 4 * CY
HALO = 2 * YH + 2 * XH
LIMIT = 40 * 1024 * 1024


def stencil_constants():
    w = np.array(STENCIL_WEIGHTS)
    band = np.zeros(600)
    band[1:5] = w[1:]
    row = np.arange(ROWS)
    x, y = row // CY, row % CY
    dx, dy = np.abs(x[:, None] - x[None, :]), np.abs(y[:, None] - y[None, :])
    inner = band[dx] * (dy == 0) + band[dy] * (dx == 0) + 3.0 * w[0] * ((dx == 0) & (dy == 0))
    z = np.arange(CZ)
    depth = band[np.abs(z[:, None] - z[None, :])]
    pick = np.zeros((ROWS, ROWS))
    halo = np.zeros((ROWS, 384))
    for cx in range(CX):
        for q in range(4):
            pick[cx * 4 + q, cx * CY + CY - 4 + q] = 1.0
            pick[YH + cx * 4 + q, cx * CY + q] = 1.0
            for cy in range(CY):
                halo[cx * CY + cy, cx * 4 + q] = band[cy + 4 - q]
                halo[cx * CY + cy, YH + cx * 4 + q] = band[CY + q - cy]
    for q in range(4):
        for cx in range(CX):
            for cy in range(CY):
                halo[cx * CY + cy, 2 * YH + q * CY + cy] = band[cx + 4 - q]
                halo[cx * CY + cy, 2 * YH + XH + q * CY + cy] = band[CX + q - cx]

    def parts(matrix):
        high = matrix.astype(np.float32).astype(ml_dtypes.bfloat16)
        low = (matrix - high.astype(np.float64)).astype(np.float32).astype(ml_dtypes.bfloat16)
        return [high, low]

    square = np.concatenate(parts(inner) + parts(depth) + parts(pick)[:1], axis=0)
    return square, np.concatenate(parts(halo), axis=0)


def mm(a, b):
    return jnp.dot(a, b, preferred_element_type=jnp.float32)


def kernel(
    f_prev, f_now, a_prev, a_now, velocity, aperture, source_cell, strength, receivers, traces,
    square_hbm, halo_hbm,
    prev, corr_in, hit_out,
    now, lap, high, low, slab_b, slab, ids, cell_v, trace_v, square, halo_w,
    pick_send, halo, tables, wanted, wanted_v, wanted_by, blocks, arrived, speed, corr_send,
    hit,
    smem_tables, source_s, strength_s,
    load_sem, table_sem, id_sem, id_send, id_recv, halo_send, halo_recv, v_send, v_recv,
    c_send, c_recv, ready, go,
):
    me = lax.axis_index("shot")
    tx = lax.axis_index("tx")
    ty = lax.axis_index("ty")

    loads = [
        pltpu.make_async_copy(aperture.at[0], ids, load_sem.at[0]),
        pltpu.make_async_copy(f_now.at[0], now.at[0], load_sem.at[1]),
        pltpu.make_async_copy(a_now.at[0], now.at[1], load_sem.at[2]),
        pltpu.make_async_copy(square_hbm, square, load_sem.at[3]),
        pltpu.make_async_copy(velocity.at[0], slab_b, load_sem.at[4]),
        pltpu.make_async_copy(halo_hbm, halo_w, load_sem.at[5]),
        pltpu.make_async_copy(f_prev.at[0], prev.at[0], load_sem.at[6]),
        pltpu.make_async_copy(a_prev.at[0], prev.at[1], load_sem.at[7]),
        pltpu.make_async_copy(receivers.at[0], cell_v, load_sem.at[8]),
        pltpu.make_async_copy(traces, trace_v, load_sem.at[9]),
        pltpu.make_async_copy(source_cell, source_s, load_sem.at[10]),
        pltpu.make_async_copy(strength, strength_s, load_sem.at[11]),
    ]
    for load in loads:
        load.start()

    relayed = tx == 2
    home = tx + relayed.astype(jnp.int32)
    odd = lax.rem(tx, 2) == 1
    sides = [
        (ty < NTY - 1, "ty", ty + 1),
        (ty > 0, "ty", ty - 1),
        (tx < NTX - 1, "tx", tx + 1),
        (tx > 0, "tx", tx - 1),
    ]
    first = [ty < NTY - 1, None, tx == 1, tx == 1]

    barrier = pltpu.get_barrier_semaphore()

    @pl.loop(1 - relayed.astype(jnp.int32), NS)
    def _(d):
        pl.semaphore_signal(
            barrier,
            inc=1,
            device_id={"shot": lax.rem(me + d, NS), "tx": home},
            device_id_type=MESH,
        )

    @pl.when(first[0])
    def _():
        pl.semaphore_signal(
            barrier, inc=1, device_id={"tx": home, "ty": ty + 1}, device_id_type=MESH
        )

    for n in (2, 3):

        @pl.when(first[n])
        def _():
            pl.semaphore_signal(
                barrier, inc=1, device_id={"tx": sides[n][2]}, device_id_type=MESH
            )

    for present, start, size in (
        (ty > 0, 0, YH),
        (ty < NTY - 1, YH, YH),
        (tx > 0, 2 * YH, XH),
        (tx < NTX - 1, 2 * YH + XH, XH),
    ):

        @pl.when(jnp.logical_not(present))
        def _():
            halo[:, start : start + size, :] = jnp.zeros((2, size, CZ), jnp.bfloat16)

    for field in range(2):
        loads[1 + field].wait()
        u = now[field].reshape(ROWS, CZ)
        top = u.astype(jnp.bfloat16)
        high[field] = top
        low[field] = (u - top.astype(jnp.float32)).astype(jnp.bfloat16)

    def halo_copy(n):
        axis, other = sides[n][1], sides[n][2]
        start = (0, YH, 2 * YH, 2 * YH + XH)[n]
        if n < 2:
            source, size = pick_send.at[n], YH
        else:
            source, size = high.at[:, pl.ds((CX - 4) * CY if n == 2 else 0, XH)], XH
        return pltpu.make_async_remote_copy(
            src_ref=source,
            dst_ref=halo.at[:, pl.ds(start, size)],
            send_sem=halo_send.at[n],
            recv_sem=halo_recv.at[n],
            device_id={axis: other},
            device_id_type=MESH,
        )

    def answer_first(n):
        axis, other = sides[n][1:]
        pl.semaphore_signal(
            ready.at[(1, 0, 3, 2)[n]], inc=1, device_id={axis: other}, device_id_type=MESH
        )

    @pl.when(relayed)
    def _():
        pl.semaphore_wait(barrier, 1)
        answer_first(3)
        halo_copy(3).start()

    loads[0].wait()
    row_l = lax.broadcasted_iota(jnp.int32, (CX, CX), 1)
    row_s = lax.broadcasted_iota(jnp.int32, (CX, CX), 0)
    ids_l = jnp.broadcast_to(ids[...], (CX, CX))
    ids_s = ids_l.T
    earlier = ((ids_s >> 5) == (ids_l >> 5)) & (row_s < row_l)
    rank = jnp.sum(earlier.astype(jnp.int32), axis=0, keepdims=True)
    slot = 2 * (ids[...] >> 5) + rank
    placed = jnp.broadcast_to(slot, (CX, CX)).T == row_l
    tables[0, :, 0:CX] = slot
    tables[1, :, 0:CX] = jnp.sum(jnp.where(placed, row_s, 0), axis=0, keepdims=True)
    wanted[:, 0:CX] = jnp.sum(jnp.where(placed, ids_s & (SLAB - 1), 0), axis=0, keepdims=True)
    table_copy = pltpu.make_async_copy(tables, smem_tables, table_sem.at[0])
    table_copy.start()
    own_copy = pltpu.make_async_copy(wanted, wanted_by.at[me], table_sem.at[1])
    own_copy.start()

    loads[3].wait()
    for field in range(2):
        picked = mm(square[4 * ROWS : 5 * ROWS, :], high[field]).astype(jnp.bfloat16)
        pick_send[0, field] = picked[0:YH]
        pick_send[1, field] = picked[YH:]

    partners = NS - 1 + (ty > 0).astype(jnp.int32) + (tx == 0).astype(jnp.int32)
    partners = partners + jnp.where(tx == 3, NS + (ty > 0).astype(jnp.int32), 0)

    @pl.when(jnp.logical_not(relayed))
    def _():
        pl.semaphore_wait(barrier, partners)

    @pl.when(tx == 3)
    def _():
        pl.semaphore_signal(go, inc=1, device_id={"tx": 2}, device_id_type=MESH)

    @pl.when(relayed)
    def _():
        pl.semaphore_wait(go, 1)

    def id_copy(d):
        return pltpu.make_async_remote_copy(
            src_ref=wanted,
            dst_ref=wanted_v.at[me],
            send_sem=id_send.at[d],
            recv_sem=id_recv.at[d],
            device_id={"shot": lax.rem(me + d, NS)},
            device_id_type=MESH,
        )

    @pl.loop(1, NS)
    def _(d):
        id_copy(d).start()

    @pl.when(ty > 0)
    def _():
        answer_first(1)

    @pl.when(tx == 0)
    def _():
        answer_first(2)

    @pl.when(jnp.logical_not(odd))
    def _():
        halo_copy(2).start()

    @pl.when(tx == 3)
    def _():
        halo_copy(3).start()

    @pl.when(ty > 0)
    def _():
        halo_copy(1).start()

    def answer(n):
        @pl.when(first[n])
        def _():
            pl.semaphore_wait(ready.at[n], 1)
            halo_copy(n).start()

    loads[4].wait()
    slab[...] = slab_b[...].astype(jnp.float32)

    own_copy.wait()
    depth_l = lax.broadcasted_iota(jnp.int32, (CY, ROWS), 1)
    same_y = (depth_l & (CY - 1)) == lax.broadcasted_iota(jnp.int32, (CY, ROWS), 0)
    block_l = jnp.where(same_y, depth_l >> 3, -1)

    def serve(shot):
        first = wanted_by[shot, 0, 2 * me]
        second = wanted_by[shot, 0, 2 * me + 1]
        pair = jnp.concatenate([slab[first], slab[second]], axis=0).astype(jnp.bfloat16)
        hits = jnp.concatenate([block_l == first, block_l == second], axis=0)
        hit[pl.ds(pl.multiple_of(shot * 16, 16), 16), :] = jnp.where(hits, 1.0, 0.0)
        return pair

    arrived[me] = serve(me)

    def block_copy(d):
        shot = lax.rem(me - d + NS, NS)
        return pltpu.make_async_remote_copy(
            src_ref=blocks.at[shot],
            dst_ref=arrived.at[me],
            send_sem=v_send.at[d],
            recv_sem=v_recv.at[d],
            device_id={"shot": shot},
            device_id_type=MESH,
        )

    def id_local(d):
        shot = lax.rem(me - d + NS, NS)
        return pltpu.make_async_copy(wanted_v.at[shot], wanted_by.at[shot], id_sem.at[d])

    @pl.loop(1, NS)
    def _(d):
        id_copy(d).wait_recv()
        id_local(d).start()

    @pl.loop(1, NS)
    def _(d):
        id_local(d).wait()
        shot = lax.rem(me - d + NS, NS)
        blocks[shot] = serve(shot)
        block_copy(d).start()

    answer(0)

    for field in range(2):
        top, rest = high[field], low[field]
        lap[field] = (
            mm(square[0:ROWS, :], top)
            + mm(square[0:ROWS, :], rest)
            + mm(square[ROWS : 2 * ROWS, :], top)
            + mm(top, square[2 * ROWS : 3 * ROWS, :])
            + mm(rest, square[2 * ROWS : 3 * ROWS, :])
            + mm(top, square[3 * ROWS : 4 * ROWS, :])
        ).reshape(CX, CY, CZ)

    for load in loads[8:]:
        load.wait()
    row = lax.broadcasted_iota(jnp.int32, (ROWS, 1), 0)

    def local_row(along_x, along_y):
        inside = (along_x >= tx * CX) & (along_x < tx * CX + CX)
        inside = inside & (along_y >= ty * CY) & (along_y < ty * CY + CY)
        return jnp.where(inside, (along_x - tx * CX) * CY + along_y - ty * CY, -1)

    source_row = local_row(source_s[0, 0], source_s[0, 1])
    cell_row = local_row(cell_v[0:1, :], cell_v[1:2, :])
    injected = jnp.where(row == source_row, strength_s[0, 0], 0.0)
    recorded = jnp.sum(
        jnp.where(jnp.broadcast_to(row, (ROWS, NREC)) == cell_row, trace_v[...], 0.0),
        axis=1,
        keepdims=True,
    )
    surface = lax.broadcasted_iota(jnp.int32, (ROWS, CZ), 1) == SURFACE_DEPTH

    loads[5].wait()
    loads[6].wait()
    loads[7].wait()
    answer(3)
    answer(2)
    for n in (2, 3, 0, 1):
        came_from = sides[(1, 0, 3, 2)[n]][0]

        @pl.when(came_from)
        def _():
            halo_copy(n).wait_recv()

    for field, extra in ((0, injected), (1, recorded)):
        layers = halo[field]
        beyond = mm(halo_w[0:ROWS, 0:HALO], layers) + mm(halo_w[ROWS:, 0:HALO], layers)
        beyond = beyond + jnp.where(surface, jnp.broadcast_to(extra, (ROWS, CZ)), 0.0)
        lap[field] = lap[field] + beyond.reshape(CX, CY, CZ)
        prev[field] = 2.0 * now[field] - prev[field]

    table_copy.wait()

    def corr_copy(d):
        owner = lax.rem(me + d, NS)
        return pltpu.make_async_remote_copy(
            src_ref=corr_send.at[owner],
            dst_ref=corr_in.at[me],
            send_sem=c_send.at[d],
            recv_sem=c_recv.at[d],
            device_id={"shot": owner},
            device_id_type=MESH,
        )

    def contribute(owner):
        pair = arrived[owner].astype(jnp.float32)
        products = []
        for k in range(2):
            scaled = pair[k * CY : (k + 1) * CY] * STEP_RATIO
            courant = scaled * scaled
            speed[2 * owner + k] = courant
            r = smem_tables[1, 0, 2 * owner + k]
            products.append(
                (prev[0, r] + courant * lap[0, r]) * (prev[1, r] + courant * lap[1, r])
            )
        both = jnp.concatenate(products, axis=0)
        top = both.astype(jnp.bfloat16)
        return top, (both - top.astype(jnp.float32)).astype(jnp.bfloat16)

    corr_in[me, 0], corr_in[me, 1] = contribute(me)

    @pl.loop(1, NS)
    def _(d):
        block_copy(d).wait_recv()
        owner = lax.rem(me + d, NS)
        corr_send[owner, 0], corr_send[owner, 1] = contribute(owner)
        corr_copy(d).start()

    @pl.loop(0, CX)
    def _(r):
        courant = speed[smem_tables[0, 0, r]]
        for field in range(2):
            prev[field, r] = prev[field, r] + courant * lap[field, r]

    hit_out[...] = hit[...].T.astype(jnp.bfloat16)

    @pl.loop(1, NS)
    def _(d):
        corr_copy(d).wait_recv()

    @pl.loop(1, NS)
    def _(d):
        id_copy(d).wait_send()
        block_copy(d).wait_send()
        corr_copy(d).wait_send()

    for n in range(4):

        @pl.when(sides[n][0])
        def _():
            halo_copy(n).wait_send()


def finish(values, corr_in, hit, f_out, a_out, image_out, image, out_sem):
    outs = [
        pltpu.make_async_copy(values.at[0], f_out.at[0], out_sem.at[0]),
        pltpu.make_async_copy(values.at[1], a_out.at[0], out_sem.at[1]),
        pltpu.make_async_copy(image, image_out.at[0], out_sem.at[2]),
    ]
    outs[0].start()
    outs[1].start()
    tops = corr_in[:, 0].reshape(ROWS, CZ)
    rests = corr_in[:, 1].reshape(ROWS, CZ)
    image[...] = (mm(hit[...], tops) + mm(hit[...], rests)).reshape(SLAB, CY, CZ)
    outs[2].start()
    for out in outs:
        out.wait()


def on_device(*arrays):
    square, halo_w = stencil_constants()
    arrays = (
        *arrays[:7],
        arrays[7].reshape(1, 1),
        jnp.swapaxes(arrays[8], 1, 2),
        arrays[9],
        jnp.asarray(square),
        jnp.asarray(halo_w),
    )
    field = jax.ShapeDtypeStruct((1, CX, CY, CZ), jnp.float32)
    dma = pltpu.SemaphoreType.DMA
    bf, f32, i32 = jnp.bfloat16, jnp.float32, jnp.int32
    scratch = [
        pltpu.VMEM((2, CX, CY, CZ), f32),
        pltpu.VMEM((2, CX, CY, CZ), f32),
        pltpu.VMEM((2, ROWS, CZ), bf),
        pltpu.VMEM((2, ROWS, CZ), bf),
        pltpu.VMEM((SLAB, CY, CZ), bf),
        pltpu.VMEM((SLAB, CY, CZ), f32),
        pltpu.VMEM((1, CX), i32),
        pltpu.VMEM((2, NREC), i32),
        pltpu.VMEM((1, NREC), f32),
        pltpu.VMEM(square.shape, bf),
        pltpu.VMEM(halo_w.shape, bf),
        pltpu.VMEM((2, 2, YH, CZ), bf),
        pltpu.VMEM((2, HALO, CZ), bf),
        pltpu.VMEM((2, 1, 128), i32),
        pltpu.VMEM((1, 128), i32),
        pltpu.VMEM((NS, 1, 128), i32),
        pltpu.SMEM((NS, 1, 128), i32),
        pltpu.VMEM((NS, 2 * CY, CZ), bf),
        pltpu.VMEM((NS, 2 * CY, CZ), bf),
        pltpu.VMEM((2 * NS, CY, CZ), f32),
        pltpu.VMEM((NS, 2, 2 * CY, CZ), bf),
        pltpu.VMEM((ROWS, ROWS), f32),
        pltpu.SMEM((2, 1, 128), i32),
        pltpu.SMEM((1, 2), i32),
        pltpu.SMEM((1, 1), f32),
        dma((12,)),
        dma((2,)),
        dma((NS,)),
        dma((NS,)),
        dma((NS,)),
        dma((4,)),
        dma((4,)),
        dma((NS,)),
        dma((NS,)),
        dma((NS,)),
        dma((NS,)),
        pltpu.SemaphoreType.REGULAR((4,)),
        pltpu.SemaphoreType.REGULAR,
    ]
    anywhere = pl.BlockSpec(memory_space=pl.ANY)
    vmem = pl.BlockSpec(memory_space=pltpu.VMEM)
    values, corr_in, hit = pl.pallas_call(
        kernel,
        out_shape=(
            jax.ShapeDtypeStruct((2, CX, CY, CZ), f32),
            jax.ShapeDtypeStruct((NS, 2, 2 * CY, CZ), bf),
            jax.ShapeDtypeStruct((ROWS, ROWS), bf),
        ),
        in_specs=[anywhere] * 12,
        out_specs=(vmem,) * 3,
        scratch_shapes=scratch,
        compiler_params=pltpu.CompilerParams(
            collective_id=0, has_side_effects=True, vmem_limit_bytes=LIMIT
        ),
    )(*[a if a.size == 1 else pltpu.with_memory_space_constraint(a, pltpu.HBM) for a in arrays])
    return pl.pallas_call(
        finish,
        out_shape=(field, field, field),
        in_specs=[vmem] * 3,
        out_specs=(anywhere,) * 3,
        scratch_shapes=[pltpu.VMEM((SLAB, CY, CZ), f32), dma((3,))],
        compiler_params=pltpu.CompilerParams(vmem_limit_bytes=LIMIT),
    )(values, corr_in, hit)


def solution(mesh):
    in_specs = (
        P("shot", "tx", "ty", None),
        P("shot", "tx", "ty", None),
        P("shot", "tx", "ty", None),
        P("shot", "tx", "ty", None),
        P(("tx", "ty"), "shot", None, None),
        P("shot", ("tx", "ty"), None),
        P("shot", None),
        P("shot"),
        P("shot", None, None),
        P("shot", None),
    )
    out_specs = (
        P("shot", "tx", "ty", None),
        P("shot", "tx", "ty", None),
        P(("tx", "ty"), "shot", None, None),
    )
    return jax.shard_map(
        on_device, mesh=mesh, in_specs=in_specs, out_specs=out_specs, check_vma=False
    )
```

```python
import functools

import jax
import jax.numpy as jnp
import ml_dtypes
import numpy as np
from jax import lax
from jax.experimental import pallas as pl
from jax.experimental.pallas import tpu as pltpu
from jax.sharding import PartitionSpec as P

SURFACE_DEPTH = 8
STENCIL_WEIGHTS = (-205.0 / 72.0, 8.0 / 5.0, -1.0 / 5.0, 8.0 / 315.0, -1.0 / 560.0)
STEP_RATIO = 0.1
MESH = pl.DeviceIdType.MESH
NS, NTX, NTY = 16, 4, 8
CX, CY, CZ = 32, 8, 256
ROWS = CX * CY
SLAB = 32
NREC = 128
YH = CX * 4
XH = 4 * CY
HALO = 2 * YH + 2 * XH
LIMIT = 40 * 1024 * 1024


def stencil_constants():
    w = np.array(STENCIL_WEIGHTS)
    band = np.zeros(600)
    band[1:5] = w[1:]
    row = np.arange(ROWS)
    x, y = row // CY, row % CY
    dx, dy = np.abs(x[:, None] - x[None, :]), np.abs(y[:, None] - y[None, :])
    inner = band[dx] * (dy == 0) + band[dy] * (dx == 0) + 3.0 * w[0] * ((dx == 0) & (dy == 0))
    z = np.arange(CZ)
    depth = band[np.abs(z[:, None] - z[None, :])]
    pick = np.zeros((ROWS, ROWS))
    halo = np.zeros((ROWS, 2 * YH))
    for cx in range(CX):
        for q in range(4):
            pick[cx * 4 + q, cx * CY + CY - 4 + q] = 1.0
            pick[YH + cx * 4 + q, cx * CY + q] = 1.0
            for cy in range(CY):
                halo[cx * CY + cy, cx * 4 + q] = band[cy + 4 - q]
                halo[cx * CY + cy, YH + cx * 4 + q] = band[CY + q - cy]

    def parts(matrix):
        high = matrix.astype(np.float32).astype(ml_dtypes.bfloat16)
        low = (matrix - high.astype(np.float64)).astype(np.float32).astype(ml_dtypes.bfloat16)
        return [high, low]

    square = np.concatenate(parts(inner) + parts(depth) + parts(pick)[:1], axis=0)
    return square, np.concatenate(parts(halo), axis=0)


def mm(a, b):
    return jnp.dot(a, b, preferred_element_type=jnp.float32)


def kernel(
    f_prev, f_now, a_prev, a_now, velocity, aperture, source_cell, strength, receivers, traces,
    square_hbm, halo_hbm,
    prev, corr_in, hit_out,
    now, lap, high, low, edge, slab_b, slab, ids, cell_v, trace_v, square, halo_w,
    pick_send, halo, tables, wanted, wanted_by, blocks, arrived, speed, corr_send,
    hit,
    smem_tables, source_s, strength_s,
    load_sem, table_sem, id_sem, id_send, id_recv, halo_send, halo_recv, v_send, v_recv,
    c_send, c_recv, ready, go,
):
    me = lax.axis_index("shot")
    tx = lax.axis_index("tx")
    ty = lax.axis_index("ty")

    loads = [
        pltpu.make_async_copy(aperture.at[0], ids, load_sem.at[0]),
        pltpu.make_async_copy(f_now.at[0], now.at[0], load_sem.at[1]),
        pltpu.make_async_copy(a_now.at[0], now.at[1], load_sem.at[2]),
        pltpu.make_async_copy(square_hbm, square, load_sem.at[3]),
        pltpu.make_async_copy(velocity.at[0], slab_b, load_sem.at[4]),
        pltpu.make_async_copy(halo_hbm, halo_w, load_sem.at[5]),
        pltpu.make_async_copy(f_prev.at[0], prev.at[0], load_sem.at[6]),
        pltpu.make_async_copy(a_prev.at[0], prev.at[1], load_sem.at[7]),
        pltpu.make_async_copy(receivers.at[0], cell_v, load_sem.at[8]),
        pltpu.make_async_copy(traces, trace_v, load_sem.at[9]),
        pltpu.make_async_copy(source_cell, source_s, load_sem.at[10]),
        pltpu.make_async_copy(strength, strength_s, load_sem.at[11]),
    ]
    for n in (0, 1, 2, 4):
        loads[n].start()

    relayed = tx == 2
    home = tx + relayed.astype(jnp.int32)
    odd = lax.rem(tx, 2) == 1
    sides = [
        (ty < NTY - 1, "ty", ty + 1),
        (ty > 0, "ty", ty - 1),
        (tx < NTX - 1, "tx", tx + 1),
        (tx > 0, "tx", tx - 1),
    ]
    first = [ty < NTY - 1, None, tx == 1, tx == 1]

    barrier = pltpu.get_barrier_semaphore()

    @pl.loop(1 - relayed.astype(jnp.int32), NS)
    def _(d):
        pl.semaphore_signal(
            barrier,
            inc=1,
            device_id={"shot": lax.rem(me + d, NS), "tx": home},
            device_id_type=MESH,
        )

    @pl.when(first[0])
    def _():
        pl.semaphore_signal(
            barrier, inc=1, device_id={"tx": home, "ty": ty + 1}, device_id_type=MESH
        )

    for n in (2, 3):

        @pl.when(first[n])
        def _():
            pl.semaphore_signal(
                barrier, inc=1, device_id={"tx": sides[n][2]}, device_id_type=MESH
            )

    for n in (3, 5, 6, 7, 8, 9, 10, 11):
        loads[n].start()

    for present, start, size in (
        (ty > 0, 0, YH),
        (ty < NTY - 1, YH, YH),
        (tx > 0, 2 * YH, XH),
        (tx < NTX - 1, 2 * YH + XH, XH),
    ):

        @pl.when(jnp.logical_not(present))
        def _():
            halo[:, start : start + size, :] = jnp.zeros((2, size, CZ), jnp.bfloat16)

    def halo_copy(n, source=None):
        axis, other = sides[n][1], sides[n][2]
        start = (0, YH, 2 * YH, 2 * YH + XH)[n]
        size = YH if n < 2 else XH
        if source is None and n < 2:
            source = pick_send.at[n]
        elif source is None:
            source = high.at[:, pl.ds((CX - 4) * CY if n == 2 else 0, XH)]
        return pltpu.make_async_remote_copy(
            src_ref=source,
            dst_ref=halo.at[:, pl.ds(start, size)],
            send_sem=halo_send.at[n],
            recv_sem=halo_recv.at[n],
            device_id={axis: other},
            device_id_type=MESH,
        )

    def answer_first(n):
        axis, other = sides[n][1:]
        pl.semaphore_signal(
            ready.at[(1, 0, 3, 2)[n]], inc=1, device_id={axis: other}, device_id_type=MESH
        )

    def across():
        pl.semaphore_wait(barrier, 1)
        answer_first(3)
        halo_copy(3, edge).start()

    loads[1].wait()
    loads[2].wait()

    @pl.when(relayed)
    def _():
        edge[...] = now[:, 0:4].reshape(2, XH, CZ).astype(jnp.bfloat16)

    @pl.when(relayed & (ty < 6))
    def _():
        across()

    for field in range(2):
        u = now[field].reshape(ROWS, CZ)
        top = u.astype(jnp.bfloat16)
        high[field] = top
        low[field] = (u - top.astype(jnp.float32)).astype(jnp.bfloat16)

    loads[0].wait()
    row_l = lax.broadcasted_iota(jnp.int32, (CX, CX), 1)
    row_s = lax.broadcasted_iota(jnp.int32, (CX, CX), 0)
    ids_l = jnp.broadcast_to(ids[...], (CX, CX))
    ids_s = ids_l.T
    earlier = ((ids_s >> 5) == (ids_l >> 5)) & (row_s < row_l)
    rank = jnp.sum(earlier.astype(jnp.int32), axis=0, keepdims=True)
    slot = 2 * (ids[...] >> 5) + rank
    placed = jnp.broadcast_to(slot, (CX, CX)).T == row_l
    tables[0, :, 0:CX] = slot
    tables[1, :, 0:CX] = jnp.sum(jnp.where(placed, row_s, 0), axis=0, keepdims=True)
    wanted[me, :, 0:CX] = jnp.sum(jnp.where(placed, ids_s & (SLAB - 1), 0), axis=0, keepdims=True)
    table_copy = pltpu.make_async_copy(tables, smem_tables, table_sem)
    table_copy.start()

    loads[3].wait()
    for field in range(2):
        picked = mm(square[4 * ROWS : 5 * ROWS, :], high[field]).astype(jnp.bfloat16)
        pick_send[0, field] = picked[0:YH]
        pick_send[1, field] = picked[YH:]

    partners = NS - 1 + (ty > 0).astype(jnp.int32) + (tx == 0).astype(jnp.int32)
    partners = partners + jnp.where(tx == 3, NS + (ty > 0).astype(jnp.int32), 0)

    @pl.when(jnp.logical_not(relayed))
    def _():
        pl.semaphore_wait(barrier, partners)

    @pl.when(tx == 3)
    def _():
        pl.semaphore_signal(go, inc=1, device_id={"tx": 2}, device_id_type=MESH)

    @pl.when(relayed)
    def _():
        pl.semaphore_wait(go, 1)

    def id_copy(d):
        return pltpu.make_async_remote_copy(
            src_ref=wanted.at[me],
            dst_ref=wanted.at[me],
            send_sem=id_send,
            recv_sem=id_recv,
            device_id={"shot": lax.rem(me + d, NS)},
            device_id_type=MESH,
        )

    @pl.loop(1, NS)
    def _(d):
        id_copy(d).start()

    @pl.when(relayed & (ty >= 6))
    def _():
        across()

    @pl.when(ty > 0)
    def _():
        answer_first(1)

    @pl.when(tx == 0)
    def _():
        answer_first(2)

    @pl.when(jnp.logical_not(odd))
    def _():
        halo_copy(2).start()

    @pl.when(tx == 3)
    def _():
        halo_copy(3).start()

    @pl.when(ty > 0)
    def _():
        halo_copy(1).start()

    def answer(n):
        @pl.when(first[n])
        def _():
            pl.semaphore_wait(ready.at[n], 1)
            halo_copy(n).start()

    loads[4].wait()
    slab[...] = slab_b[...].astype(jnp.float32)

    depth_l = lax.broadcasted_iota(jnp.int32, (CY, ROWS), 1)
    same_y = (depth_l & (CY - 1)) == lax.broadcasted_iota(jnp.int32, (CY, ROWS), 0)
    block_l = jnp.where(same_y, depth_l >> 3, -1)

    def serve(shot):
        first = wanted_by[shot, 0, 2 * me]
        second = wanted_by[shot, 0, 2 * me + 1]
        pair = jnp.concatenate([slab[first], slab[second]], axis=0).astype(jnp.bfloat16)
        hits = jnp.concatenate([block_l == first, block_l == second], axis=0)
        hit[pl.ds(pl.multiple_of(shot * 16, 16), 16), :] = jnp.where(hits, 1.0, 0.0)
        return pair

    def block_copy(d):
        shot = lax.rem(me - d + NS, NS)
        return pltpu.make_async_remote_copy(
            src_ref=blocks.at[shot],
            dst_ref=arrived.at[me],
            send_sem=v_send,
            recv_sem=v_recv.at[d],
            device_id={"shot": shot},
            device_id_type=MESH,
        )

    all_but_one = pl.ds(0, NS - 1)
    pltpu.make_async_copy(wanted.at[all_but_one], wanted.at[all_but_one], id_recv).wait()
    id_local = pltpu.make_async_copy(wanted, wanted_by, id_sem)
    id_local.start()
    id_local.wait()

    @pl.loop(1, NS)
    def _(d):
        shot = lax.rem(me - d + NS, NS)
        blocks[shot] = serve(shot)
        block_copy(d).start()

    arrived[me] = serve(me)
    answer(0)

    @pl.when(ty >= 5)
    def _():
        answer(3)
        answer(2)

    for field in range(2):
        top, rest = high[field], low[field]
        lap[field] = (
            mm(square[0:ROWS, :], top)
            + mm(square[0:ROWS, :], rest)
            + mm(square[ROWS : 2 * ROWS, :], top)
            + mm(top, square[2 * ROWS : 3 * ROWS, :])
            + mm(rest, square[2 * ROWS : 3 * ROWS, :])
            + mm(top, square[3 * ROWS : 4 * ROWS, :])
        ).reshape(CX, CY, CZ)

    for load in loads[8:]:
        load.wait()
    row = lax.broadcasted_iota(jnp.int32, (ROWS, 1), 0)

    def local_row(along_x, along_y):
        inside = (along_x >= tx * CX) & (along_x < tx * CX + CX)
        inside = inside & (along_y >= ty * CY) & (along_y < ty * CY + CY)
        return jnp.where(inside, (along_x - tx * CX) * CY + along_y - ty * CY, -1)

    source_row = local_row(source_s[0, 0], source_s[0, 1])
    cell_row = local_row(cell_v[0:1, :], cell_v[1:2, :])
    injected = jnp.where(row == source_row, strength_s[0, 0], 0.0)
    recorded = jnp.sum(
        jnp.where(jnp.broadcast_to(row, (ROWS, NREC)) == cell_row, trace_v[...], 0.0),
        axis=1,
        keepdims=True,
    )
    surface = lax.broadcasted_iota(jnp.int32, (ROWS, CZ), 1) == SURFACE_DEPTH

    loads[5].wait()
    loads[6].wait()
    loads[7].wait()
    def halo_wait(n):
        @pl.when(sides[(1, 0, 3, 2)[n]][0])
        def _():
            halo_copy(n).wait_recv()

    halo_wait(0)
    halo_wait(1)
    for field, extra in ((0, injected), (1, recorded)):
        layers = halo[field, 0 : 2 * YH]
        beyond = mm(halo_w[0:ROWS, :], layers) + mm(halo_w[ROWS:, :], layers)
        beyond = beyond + jnp.where(surface, jnp.broadcast_to(extra, (ROWS, CZ)), 0.0)
        lap[field] = lap[field] + beyond.reshape(CX, CY, CZ)
        prev[field] = 2.0 * now[field] - prev[field]

    @pl.when(ty < 5)
    def _():
        answer(3)
        answer(2)

    halo_wait(2)
    halo_wait(3)
    for field in range(2):
        layers = halo[field, 2 * YH :].astype(jnp.float32).reshape(8, CY, CZ)
        for q in range(4):
            for x in range(4):
                if x <= q:
                    weight = STENCIL_WEIGHTS[x + 4 - q]
                    lap[field, x] = lap[field, x] + weight * layers[q]
                if x >= q:
                    weight = STENCIL_WEIGHTS[4 + q - x]
                    lap[field, CX - 4 + x] = lap[field, CX - 4 + x] + weight * layers[4 + q]

    table_copy.wait()

    def corr_copy(d):
        owner = lax.rem(me + d, NS)
        return pltpu.make_async_remote_copy(
            src_ref=corr_send.at[owner],
            dst_ref=corr_in.at[me],
            send_sem=c_send,
            recv_sem=c_recv,
            device_id={"shot": owner},
            device_id_type=MESH,
        )

    def contribute(owner):
        pair = arrived[owner].astype(jnp.float32)
        products = []
        for k in range(2):
            scaled = pair[k * CY : (k + 1) * CY] * STEP_RATIO
            courant = scaled * scaled
            speed[2 * owner + k] = courant
            r = smem_tables[1, 0, 2 * owner + k]
            products.append(
                (prev[0, r] + courant * lap[0, r]) * (prev[1, r] + courant * lap[1, r])
            )
        both = jnp.concatenate(products, axis=0)
        top = both.astype(jnp.bfloat16)
        return top, (both - top.astype(jnp.float32)).astype(jnp.bfloat16)

    corr_in[me, 0], corr_in[me, 1] = contribute(me)

    @pl.loop(1, NS)
    def _(d):
        block_copy(d).wait_recv()
        owner = lax.rem(me + d, NS)
        corr_send[owner, 0], corr_send[owner, 1] = contribute(owner)
        corr_copy(d).start()

    @pl.loop(0, CX)
    def _(r):
        courant = speed[smem_tables[0, 0, r]]
        for field in range(2):
            prev[field, r] = prev[field, r] + courant * lap[field, r]

    hit_out[...] = hit[...].T.astype(jnp.bfloat16)

    def all_sent(ref, sem):
        pltpu.make_async_copy(ref.at[all_but_one], ref.at[all_but_one], sem).wait()

    all_sent(wanted, id_send)
    all_sent(blocks, v_send)
    for n in range(4):

        @pl.when(sides[n][0])
        def _():
            halo_copy(n).wait_send()

    all_sent(corr_send, c_send)
    all_sent(corr_in, c_recv)


def finish(values, corr_in, hit, f_out, a_out, image_out, image, out_sem):
    outs = [
        pltpu.make_async_copy(values.at[0], f_out.at[0], out_sem.at[0]),
        pltpu.make_async_copy(values.at[1], a_out.at[0], out_sem.at[1]),
        pltpu.make_async_copy(image, image_out.at[0], out_sem.at[2]),
    ]
    outs[0].start()
    outs[1].start()
    tops = corr_in[:, 0].reshape(ROWS, CZ)
    rests = corr_in[:, 1].reshape(ROWS, CZ)
    image[...] = (mm(hit[...], tops) + mm(hit[...], rests)).reshape(SLAB, CY, CZ)
    outs[2].start()
    for out in outs:
        out.wait()


def on_device(*arrays):
    square, halo_w = stencil_constants()
    arrays = (
        *arrays[:7],
        arrays[7].reshape(1, 1),
        jnp.swapaxes(arrays[8], 1, 2),
        arrays[9],
        jnp.asarray(square),
        jnp.asarray(halo_w),
    )
    field = jax.ShapeDtypeStruct((1, CX, CY, CZ), jnp.float32)
    dma = pltpu.SemaphoreType.DMA
    bf, f32, i32 = jnp.bfloat16, jnp.float32, jnp.int32
    scratch = [
        pltpu.VMEM((2, CX, CY, CZ), f32),
        pltpu.VMEM((2, CX, CY, CZ), f32),
        pltpu.VMEM((2, ROWS, CZ), bf),
        pltpu.VMEM((2, ROWS, CZ), bf),
        pltpu.VMEM((2, XH, CZ), bf),
        pltpu.VMEM((SLAB, CY, CZ), bf),
        pltpu.VMEM((SLAB, CY, CZ), f32),
        pltpu.VMEM((1, CX), i32),
        pltpu.VMEM((2, NREC), i32),
        pltpu.VMEM((1, NREC), f32),
        pltpu.VMEM(square.shape, bf),
        pltpu.VMEM(halo_w.shape, bf),
        pltpu.VMEM((2, 2, YH, CZ), bf),
        pltpu.VMEM((2, HALO, CZ), bf),
        pltpu.VMEM((2, 1, 128), i32),
        pltpu.VMEM((NS, 1, 128), i32),
        pltpu.SMEM((NS, 1, 128), i32),
        pltpu.VMEM((NS, 2 * CY, CZ), bf),
        pltpu.VMEM((NS, 2 * CY, CZ), bf),
        pltpu.VMEM((2 * NS, CY, CZ), f32),
        pltpu.VMEM((NS, 2, 2 * CY, CZ), bf),
        pltpu.VMEM((ROWS, ROWS), f32),
        pltpu.SMEM((2, 1, 128), i32),
        pltpu.SMEM((1, 2), i32),
        pltpu.SMEM((1, 1), f32),
        dma((12,)),
        dma,
        dma,
        dma,
        dma,
        dma((4,)),
        dma((4,)),
        dma,
        dma((NS,)),
        dma,
        dma,
        pltpu.SemaphoreType.REGULAR((4,)),
        pltpu.SemaphoreType.REGULAR,
    ]
    anywhere = pl.BlockSpec(memory_space=pl.ANY)
    vmem = pl.BlockSpec(memory_space=pltpu.VMEM)
    values, corr_in, hit = pl.pallas_call(
        kernel,
        out_shape=(
            jax.ShapeDtypeStruct((2, CX, CY, CZ), f32),
            jax.ShapeDtypeStruct((NS, 2, 2 * CY, CZ), bf),
            jax.ShapeDtypeStruct((ROWS, ROWS), bf),
        ),
        in_specs=[anywhere] * 12,
        out_specs=(vmem,) * 3,
        scratch_shapes=scratch,
        compiler_params=pltpu.CompilerParams(
            collective_id=0, has_side_effects=True, vmem_limit_bytes=LIMIT
        ),
    )(*[a if a.size == 1 else pltpu.with_memory_space_constraint(a, pltpu.HBM) for a in arrays])
    return pl.pallas_call(
        finish,
        out_shape=(field, field, field),
        in_specs=[vmem] * 3,
        out_specs=(anywhere,) * 3,
        scratch_shapes=[pltpu.VMEM((SLAB, CY, CZ), f32), dma((3,))],
        compiler_params=pltpu.CompilerParams(vmem_limit_bytes=LIMIT),
    )(values, corr_in, hit)


def solution(mesh):
    in_specs = (
        P("shot", "tx", "ty", None),
        P("shot", "tx", "ty", None),
        P("shot", "tx", "ty", None),
        P("shot", "tx", "ty", None),
        P(("tx", "ty"), "shot", None, None),
        P("shot", ("tx", "ty"), None),
        P("shot", None),
        P("shot"),
        P("shot", None, None),
        P("shot", None),
    )
    out_specs = (
        P("shot", "tx", "ty", None),
        P("shot", "tx", "ty", None),
        P(("tx", "ty"), "shot", None, None),
    )
    return jax.shard_map(
        on_device, mesh=mesh, in_specs=in_specs, out_specs=out_specs, check_vma=False
    )
```

```python
import functools

import jax
import jax.numpy as jnp
import ml_dtypes
import numpy as np
from jax import lax
from jax.experimental import pallas as pl
from jax.experimental.pallas import tpu as pltpu
from jax.sharding import PartitionSpec as P

SURFACE_DEPTH = 8
STENCIL_WEIGHTS = (-205.0 / 72.0, 8.0 / 5.0, -1.0 / 5.0, 8.0 / 315.0, -1.0 / 560.0)
STEP_RATIO = 0.1
MESH = pl.DeviceIdType.MESH
NS, NTX, NTY = 16, 4, 8
CX, CY, CZ = 32, 8, 256
ROWS = CX * CY
SLAB = 32
NREC = 128
YH = CX * 4
XH = 4 * CY
HALO = 2 * YH + 2 * XH
STEPS = 32766.0
TINY = 1e-34
LIMIT = 40 * 1024 * 1024


def stencil_constants():
    w = np.array(STENCIL_WEIGHTS)
    band = np.zeros(600)
    band[1:5] = w[1:]
    row = np.arange(ROWS)
    x, y = row // CY, row % CY
    dx, dy = np.abs(x[:, None] - x[None, :]), np.abs(y[:, None] - y[None, :])
    inner = band[dx] * (dy == 0) + band[dy] * (dx == 0) + 3.0 * w[0] * ((dx == 0) & (dy == 0))
    z = np.arange(CZ)
    depth = band[np.abs(z[:, None] - z[None, :])]
    pick = np.zeros((ROWS, ROWS))
    halo = np.zeros((ROWS, 2 * YH))
    for cx in range(CX):
        for q in range(4):
            pick[cx * 4 + q, cx * CY + CY - 4 + q] = 1.0
            pick[YH + cx * 4 + q, cx * CY + q] = 1.0
            for cy in range(CY):
                halo[cx * CY + cy, cx * 4 + q] = band[cy + 4 - q]
                halo[cx * CY + cy, YH + cx * 4 + q] = band[CY + q - cy]

    def parts(matrix):
        high = matrix.astype(np.float32).astype(ml_dtypes.bfloat16)
        low = (matrix - high.astype(np.float64)).astype(np.float32).astype(ml_dtypes.bfloat16)
        return [high, low]

    square = np.concatenate(parts(inner) + parts(depth) + parts(pick)[:1], axis=0)
    return square, np.concatenate(parts(halo), axis=0)


def each_partner(body):
    @pl.loop(1, NS)
    def _(step):
        body(lax.rem(5 * step, NS))


def mm(a, b):
    return jnp.dot(a, b, preferred_element_type=jnp.float32)


def kernel(
    f_prev, f_now, a_prev, a_now, velocity, aperture, source_cell, strength, receivers, traces,
    square_hbm, halo_hbm,
    prev, peak_in, corr_in, hit_out,
    now, lap, high, low, edge_f, edge, slab_b, slab, ids, cell_v, trace_v, square, halo_w,
    pick_send, halo, tables, wanted, wanted_by, blocks, arrived, speed, peak_send, corr_send,
    hit,
    smem_tables, source_s, strength_s,
    load_sem, edge_sem, table_sem, id_sem, id_send, id_recv, halo_send, halo_recv, v_send, v_recv,
    c_send, c_recv, ready, go,
):
    me = lax.axis_index("shot")
    tx = lax.axis_index("tx")
    ty = lax.axis_index("ty")

    loads = [
        pltpu.make_async_copy(aperture.at[0], ids, load_sem.at[0]),
        pltpu.make_async_copy(f_now.at[0], now.at[0], load_sem.at[1]),
        pltpu.make_async_copy(a_now.at[0], now.at[1], load_sem.at[2]),
        pltpu.make_async_copy(square_hbm, square, load_sem.at[3]),
        pltpu.make_async_copy(velocity.at[0], slab_b, load_sem.at[4]),
        pltpu.make_async_copy(halo_hbm, halo_w, load_sem.at[5]),
        pltpu.make_async_copy(f_prev.at[0], prev.at[0], load_sem.at[6]),
        pltpu.make_async_copy(a_prev.at[0], prev.at[1], load_sem.at[7]),
        pltpu.make_async_copy(receivers.at[0], cell_v, load_sem.at[8]),
        pltpu.make_async_copy(traces, trace_v, load_sem.at[9]),
        pltpu.make_async_copy(source_cell, source_s, load_sem.at[10]),
        pltpu.make_async_copy(strength, strength_s, load_sem.at[11]),
    ]
    edge_loads = [
        pltpu.make_async_copy(now_hbm.at[0, 0:4], edge_f.at[field], edge_sem.at[field])
        for field, now_hbm in enumerate((f_now, a_now))
    ]

    @pl.when(lax.axis_index("tx") == 2)
    def _():
        edge_loads[0].start()
        edge_loads[1].start()

    for n in (0, 1, 2, 4):
        loads[n].start()

    relayed = tx == 2
    home = tx + relayed.astype(jnp.int32)
    odd = lax.rem(tx, 2) == 1
    sides = [
        (ty < NTY - 1, "ty", ty + 1),
        (ty > 0, "ty", ty - 1),
        (tx < NTX - 1, "tx", tx + 1),
        (tx > 0, "tx", tx - 1),
    ]
    first = [ty < NTY - 1, None, tx == 1, tx == 1]

    barrier = pltpu.get_barrier_semaphore()

    @pl.loop(1 - relayed.astype(jnp.int32), NS)
    def _(d):
        pl.semaphore_signal(
            barrier,
            inc=1,
            device_id={"shot": lax.rem(me + d, NS), "tx": home},
            device_id_type=MESH,
        )

    @pl.when(first[0])
    def _():
        pl.semaphore_signal(
            barrier, inc=1, device_id={"tx": home, "ty": ty + 1}, device_id_type=MESH
        )

    for n in (2, 3):

        @pl.when(first[n])
        def _():
            pl.semaphore_signal(
                barrier, inc=1, device_id={"tx": sides[n][2]}, device_id_type=MESH
            )

    for n in (3, 5, 6, 7, 8, 9, 10, 11):
        loads[n].start()

    for present, start, size in (
        (ty > 0, 0, YH),
        (ty < NTY - 1, YH, YH),
        (tx > 0, 2 * YH, XH),
        (tx < NTX - 1, 2 * YH + XH, XH),
    ):

        @pl.when(jnp.logical_not(present))
        def _():
            halo[:, start : start + size, :] = jnp.zeros((2, size, CZ), jnp.bfloat16)

    def halo_copy(n, source=None):
        axis, other = sides[n][1], sides[n][2]
        start = (0, YH, 2 * YH, 2 * YH + XH)[n]
        size = YH if n < 2 else XH
        if source is None and n < 2:
            source = pick_send.at[n]
        elif source is None:
            source = high.at[:, pl.ds((CX - 4) * CY if n == 2 else 0, XH)]
        return pltpu.make_async_remote_copy(
            src_ref=source,
            dst_ref=halo.at[:, pl.ds(start, size)],
            send_sem=halo_send.at[n],
            recv_sem=halo_recv.at[n],
            device_id={axis: other},
            device_id_type=MESH,
        )

    def answer_first(n):
        axis, other = sides[n][1:]
        pl.semaphore_signal(
            ready.at[(1, 0, 3, 2)[n]], inc=1, device_id={axis: other}, device_id_type=MESH
        )

    def across():
        pl.semaphore_wait(barrier, 1)
        answer_first(3)
        halo_copy(3, edge).start()

    @pl.when(relayed)
    def _():
        edge_loads[0].wait()
        edge_loads[1].wait()
        edge[...] = edge_f[...].reshape(2, XH, CZ).astype(jnp.bfloat16)

    @pl.when(relayed & (ty < 6))
    def _():
        across()

    loads[1].wait()
    loads[2].wait()
    for field in range(2):
        u = now[field].reshape(ROWS, CZ)
        top = u.astype(jnp.bfloat16)
        high[field] = top
        low[field] = (u - top.astype(jnp.float32)).astype(jnp.bfloat16)

    loads[0].wait()
    row_l = lax.broadcasted_iota(jnp.int32, (CX, CX), 1)
    row_s = lax.broadcasted_iota(jnp.int32, (CX, CX), 0)
    ids_l = jnp.broadcast_to(ids[...], (CX, CX))
    ids_s = ids_l.T
    earlier = ((ids_s >> 5) == (ids_l >> 5)) & (row_s < row_l)
    rank = jnp.sum(earlier.astype(jnp.int32), axis=0, keepdims=True)
    slot = 2 * (ids[...] >> 5) + rank
    placed = jnp.broadcast_to(slot, (CX, CX)).T == row_l
    tables[0, :, 0:CX] = slot
    tables[1, :, 0:CX] = jnp.sum(jnp.where(placed, row_s, 0), axis=0, keepdims=True)
    wanted[me, :, 0:CX] = jnp.sum(jnp.where(placed, ids_s & (SLAB - 1), 0), axis=0, keepdims=True)
    table_copy = pltpu.make_async_copy(tables, smem_tables, table_sem)
    table_copy.start()

    loads[3].wait()
    for field in range(2):
        picked = mm(square[4 * ROWS : 5 * ROWS, :], high[field]).astype(jnp.bfloat16)
        pick_send[0, field] = picked[0:YH]
        pick_send[1, field] = picked[YH:]

    partners = NS - 1 + (ty > 0).astype(jnp.int32) + (tx == 0).astype(jnp.int32)
    partners = partners + jnp.where(tx == 3, NS + (ty > 0).astype(jnp.int32), 0)

    @pl.when(jnp.logical_not(relayed))
    def _():
        pl.semaphore_wait(barrier, partners)

    @pl.when(tx == 3)
    def _():
        pl.semaphore_signal(go, inc=1, device_id={"tx": 2}, device_id_type=MESH)

    @pl.when(relayed)
    def _():
        pl.semaphore_wait(go, 1)

    def id_copy(d):
        return pltpu.make_async_remote_copy(
            src_ref=wanted.at[me],
            dst_ref=wanted.at[me],
            send_sem=id_send,
            recv_sem=id_recv,
            device_id={"shot": lax.rem(me + d, NS)},
            device_id_type=MESH,
        )

    each_partner(lambda d: id_copy(d).start())

    @pl.when(relayed & (ty >= 6))
    def _():
        across()

    @pl.when(ty > 0)
    def _():
        answer_first(1)

    @pl.when(tx == 0)
    def _():
        answer_first(2)

    @pl.when(jnp.logical_not(odd))
    def _():
        halo_copy(2).start()

    @pl.when(tx == 3)
    def _():
        halo_copy(3).start()

    @pl.when(ty > 0)
    def _():
        halo_copy(1).start()

    def answer(n):
        @pl.when(first[n])
        def _():
            pl.semaphore_wait(ready.at[n], 1)
            halo_copy(n).start()

    loads[4].wait()
    slab[...] = slab_b[...].astype(jnp.float32)

    def serve(shot):
        rows = [slab[wanted_by[shot, 0, 2 * me + k]] for k in range(2)]
        return jnp.concatenate(rows, axis=0).astype(jnp.bfloat16)

    def block_copy(d):
        shot = lax.rem(me - d + NS, NS)
        return pltpu.make_async_remote_copy(
            src_ref=blocks.at[shot],
            dst_ref=arrived.at[me],
            send_sem=v_send,
            recv_sem=v_recv.at[d],
            device_id={"shot": shot},
            device_id_type=MESH,
        )

    for field in range(2):
        top, rest = high[field], low[field]
        lap[field] = (
            mm(square[0:ROWS, :], top)
            + mm(square[0:ROWS, :], rest)
            + mm(square[ROWS : 2 * ROWS, :], top)
            + mm(top, square[2 * ROWS : 3 * ROWS, :])
            + mm(rest, square[2 * ROWS : 3 * ROWS, :])
            + mm(top, square[3 * ROWS : 4 * ROWS, :])
        ).reshape(CX, CY, CZ)

    for load in loads[8:]:
        load.wait()
    row = lax.broadcasted_iota(jnp.int32, (ROWS, 1), 0)

    def local_row(along_x, along_y):
        inside = (along_x >= tx * CX) & (along_x < tx * CX + CX)
        inside = inside & (along_y >= ty * CY) & (along_y < ty * CY + CY)
        return jnp.where(inside, (along_x - tx * CX) * CY + along_y - ty * CY, -1)

    source_row = local_row(source_s[0, 0], source_s[0, 1])
    cell_row = local_row(cell_v[0:1, :], cell_v[1:2, :])
    injected = jnp.where(row == source_row, strength_s[0, 0], 0.0)
    recorded = jnp.sum(
        jnp.where(jnp.broadcast_to(row, (ROWS, NREC)) == cell_row, trace_v[...], 0.0),
        axis=1,
        keepdims=True,
    )
    surface = lax.broadcasted_iota(jnp.int32, (ROWS, CZ), 1) == SURFACE_DEPTH

    loads[5].wait()
    loads[6].wait()
    loads[7].wait()
    all_but_one = pl.ds(0, NS - 1)
    pltpu.make_async_copy(wanted.at[all_but_one], wanted.at[all_but_one], id_recv).wait()
    id_local = pltpu.make_async_copy(wanted, wanted_by, id_sem)
    id_local.start()
    id_local.wait()

    @each_partner
    def _(d):
        shot = lax.rem(me - d + NS, NS)
        blocks[shot] = serve(shot)
        block_copy(d).start()

    arrived[me] = serve(me)
    answer(0)

    @pl.when(ty >= 5)
    def _():
        answer(3)
        answer(2)

    depth_l = lax.broadcasted_iota(jnp.int32, (CY, ROWS), 1)
    same_y = (depth_l & (CY - 1)) == lax.broadcasted_iota(jnp.int32, (CY, ROWS), 0)
    block_l = jnp.where(same_y, depth_l >> 3, -1)


    @pl.loop(0, NS)
    def _(shot):
        hits = [block_l == wanted_by[shot, 0, 2 * me + k] for k in range(2)]
        rows = pl.ds(pl.multiple_of(shot * 16, 16), 16)
        hit[rows, :] = jnp.where(jnp.concatenate(hits, axis=0), 1.0, 0.0)

    hit_out[...] = hit[...].T.astype(jnp.bfloat16)

    def halo_wait(n):
        @pl.when(sides[(1, 0, 3, 2)[n]][0])
        def _():
            halo_copy(n).wait_recv()

    halo_wait(0)
    halo_wait(1)
    for field, extra in ((0, injected), (1, recorded)):
        layers = halo[field, 0 : 2 * YH]
        beyond = mm(halo_w[0:ROWS, :], layers) + mm(halo_w[ROWS:, :], layers)
        beyond = beyond + jnp.where(surface, jnp.broadcast_to(extra, (ROWS, CZ)), 0.0)
        lap[field] = lap[field] + beyond.reshape(CX, CY, CZ)
        prev[field] = 2.0 * now[field] - prev[field]

    @pl.when(ty < 5)
    def _():
        answer(3)
        answer(2)

    halo_wait(2)
    halo_wait(3)
    for field in range(2):
        layers = halo[field, 2 * YH :].astype(jnp.float32).reshape(8, CY, CZ)
        for q in range(4):
            for x in range(4):
                if x <= q:
                    weight = STENCIL_WEIGHTS[x + 4 - q]
                    lap[field, x] = lap[field, x] + weight * layers[q]
                if x >= q:
                    weight = STENCIL_WEIGHTS[4 + q - x]
                    lap[field, CX - 4 + x] = lap[field, CX - 4 + x] + weight * layers[4 + q]

    table_copy.wait()

    def corr_copies(d):
        owner = lax.rem(me + d, NS)
        return [
            pltpu.make_async_remote_copy(
                src_ref=source.at[owner],
                dst_ref=target.at[me],
                send_sem=c_send.at[n],
                recv_sem=c_recv.at[n],
                device_id={"shot": owner},
                device_id_type=MESH,
            )
            for n, (source, target) in enumerate(((peak_send, peak_in), (corr_send, corr_in)))
        ]

    def contribute(owner):
        pair = arrived[owner].astype(jnp.float32)
        products = []
        for k in range(2):
            scaled = pair[k * CY : (k + 1) * CY] * STEP_RATIO
            courant = scaled * scaled
            speed[2 * owner + k] = courant
            r = smem_tables[1, 0, 2 * owner + k]
            products.append(
                (prev[0, r] + courant * lap[0, r]) * (prev[1, r] + courant * lap[1, r])
            )
        both = jnp.concatenate(products, axis=0)
        top = jnp.max(jnp.abs(both), axis=0, keepdims=True)
        top = jnp.maximum(jnp.maximum(top[:, : CZ // 2], top[:, CZ // 2 :]), TINY)
        scale = STEPS / top
        code = jnp.round(both * jnp.concatenate([scale, scale], axis=1))
        return top, code.astype(jnp.int32).astype(jnp.int16)

    peak_in[me], corr_in[me] = contribute(me)

    @each_partner
    def _(d):
        block_copy(d).wait_recv()
        owner = lax.rem(me + d, NS)
        peak_send[owner], corr_send[owner] = contribute(owner)
        for copy in corr_copies(d):
            copy.start()

    @pl.loop(0, CX)
    def _(r):
        courant = speed[smem_tables[0, 0, r]]
        for field in range(2):
            prev[field, r] = prev[field, r] + courant * lap[field, r]

    def all_sent(ref, sem):
        pltpu.make_async_copy(ref.at[all_but_one], ref.at[all_but_one], sem).wait()

    all_sent(wanted, id_send)
    all_sent(blocks, v_send)
    for n in range(4):

        @pl.when(sides[n][0])
        def _():
            halo_copy(n).wait_send()

    all_sent(peak_send, c_send.at[0])
    all_sent(corr_send, c_send.at[1])
    all_sent(peak_in, c_recv.at[0])
    all_sent(corr_in, c_recv.at[1])


def finish(values, peak_in, corr_in, hit, f_out, a_out, image_out, image, out_sem):
    outs = [
        pltpu.make_async_copy(values.at[0], f_out.at[0], out_sem.at[0]),
        pltpu.make_async_copy(values.at[1], a_out.at[0], out_sem.at[1]),
        pltpu.make_async_copy(image, image_out.at[0], out_sem.at[2]),
    ]
    outs[0].start()
    outs[1].start()
    peak = peak_in[...]
    peak = jnp.broadcast_to(jnp.concatenate([peak, peak], axis=2), (NS, 2 * CY, CZ))
    share = corr_in[...].astype(jnp.int32).astype(jnp.float32) * (1.0 / STEPS)
    rows = (share * peak).reshape(ROWS, CZ)
    top = rows.astype(jnp.bfloat16)
    rest = (rows - top.astype(jnp.float32)).astype(jnp.bfloat16)
    image[...] = (mm(hit[...], top) + mm(hit[...], rest)).reshape(SLAB, CY, CZ)
    outs[2].start()
    for out in outs:
        out.wait()


def on_device(*arrays):
    square, halo_w = stencil_constants()
    arrays = (
        *arrays[:7],
        arrays[7].reshape(1, 1),
        jnp.swapaxes(arrays[8], 1, 2),
        arrays[9],
        jnp.asarray(square),
        jnp.asarray(halo_w),
    )
    field = jax.ShapeDtypeStruct((1, CX, CY, CZ), jnp.float32)
    dma = pltpu.SemaphoreType.DMA
    bf, f32, i32 = jnp.bfloat16, jnp.float32, jnp.int32
    scratch = [
        pltpu.VMEM((2, CX, CY, CZ), f32),
        pltpu.VMEM((2, CX, CY, CZ), f32),
        pltpu.VMEM((2, ROWS, CZ), bf),
        pltpu.VMEM((2, ROWS, CZ), bf),
        pltpu.VMEM((2, 4, CY, CZ), f32),
        pltpu.VMEM((2, XH, CZ), bf),
        pltpu.VMEM((SLAB, CY, CZ), bf),
        pltpu.VMEM((SLAB, CY, CZ), f32),
        pltpu.VMEM((1, CX), i32),
        pltpu.VMEM((2, NREC), i32),
        pltpu.VMEM((1, NREC), f32),
        pltpu.VMEM(square.shape, bf),
        pltpu.VMEM(halo_w.shape, bf),
        pltpu.VMEM((2, 2, YH, CZ), bf),
        pltpu.VMEM((2, HALO, CZ), bf),
        pltpu.VMEM((2, 1, 128), i32),
        pltpu.VMEM((NS, 1, 128), i32),
        pltpu.SMEM((NS, 1, 128), i32),
        pltpu.VMEM((NS, 2 * CY, CZ), bf),
        pltpu.VMEM((NS, 2 * CY, CZ), bf),
        pltpu.VMEM((2 * NS, CY, CZ), f32),
        pltpu.VMEM((NS, 1, CZ // 2), f32),
        pltpu.VMEM((NS, 2 * CY, CZ), jnp.int16),
        pltpu.VMEM((ROWS, ROWS), f32),
        pltpu.SMEM((2, 1, 128), i32),
        pltpu.SMEM((1, 2), i32),
        pltpu.SMEM((1, 1), f32),
        dma((12,)),
        dma((2,)),
        dma,
        dma,
        dma,
        dma,
        dma((4,)),
        dma((4,)),
        dma,
        dma((NS,)),
        dma((2,)),
        dma((2,)),
        pltpu.SemaphoreType.REGULAR((4,)),
        pltpu.SemaphoreType.REGULAR,
    ]
    anywhere = pl.BlockSpec(memory_space=pl.ANY)
    vmem = pl.BlockSpec(memory_space=pltpu.VMEM)
    values, peak_in, corr_in, hit = pl.pallas_call(
        kernel,
        out_shape=(
            jax.ShapeDtypeStruct((2, CX, CY, CZ), f32),
            jax.ShapeDtypeStruct((NS, 1, CZ // 2), f32),
            jax.ShapeDtypeStruct((NS, 2 * CY, CZ), jnp.int16),
            jax.ShapeDtypeStruct((ROWS, ROWS), bf),
        ),
        in_specs=[anywhere] * 12,
        out_specs=(vmem,) * 4,
        scratch_shapes=scratch,
        compiler_params=pltpu.CompilerParams(
            collective_id=0, has_side_effects=True, vmem_limit_bytes=LIMIT
        ),
    )(*[a if a.size == 1 else pltpu.with_memory_space_constraint(a, pltpu.HBM) for a in arrays])
    return pl.pallas_call(
        finish,
        out_shape=(field, field, field),
        in_specs=[vmem] * 4,
        out_specs=(anywhere,) * 3,
        scratch_shapes=[pltpu.VMEM((SLAB, CY, CZ), f32), dma((3,))],
        compiler_params=pltpu.CompilerParams(vmem_limit_bytes=LIMIT),
    )(values, peak_in, corr_in, hit)


def solution(mesh):
    in_specs = (
        P("shot", "tx", "ty", None),
        P("shot", "tx", "ty", None),
        P("shot", "tx", "ty", None),
        P("shot", "tx", "ty", None),
        P(("tx", "ty"), "shot", None, None),
        P("shot", ("tx", "ty"), None),
        P("shot", None),
        P("shot"),
        P("shot", None, None),
        P("shot", None),
    )
    out_specs = (
        P("shot", "tx", "ty", None),
        P("shot", "tx", "ty", None),
        P(("tx", "ty"), "shot", None, None),
    )
    return jax.shard_map(
        on_device, mesh=mesh, in_specs=in_specs, out_specs=out_specs, check_vma=False
    )
```

```python
import functools

import jax
import jax.numpy as jnp
import ml_dtypes
import numpy as np
from jax import lax
from jax.experimental import pallas as pl
from jax.experimental.pallas import tpu as pltpu
from jax.sharding import PartitionSpec as P

SURFACE_DEPTH = 8
STENCIL_WEIGHTS = (-205.0 / 72.0, 8.0 / 5.0, -1.0 / 5.0, 8.0 / 315.0, -1.0 / 560.0)
STEP_RATIO = 0.1
MESH = pl.DeviceIdType.MESH
NS, NTX, NTY = 16, 4, 8
CX, CY, CZ = 32, 8, 256
ROWS = CX * CY
SLAB = 32
NREC = 128
YH = CX * 4
XH = 4 * CY
HALO = 2 * YH + 2 * XH
STEPS = 32766.0
TINY = 1e-34
DIRECT = 3
LATE = 6
LIMIT = 40 * 1024 * 1024


def stencil_constants():
    w = np.array(STENCIL_WEIGHTS)
    band = np.zeros(600)
    band[1:5] = w[1:]
    row = np.arange(ROWS)
    x, y = row // CY, row % CY
    dx, dy = np.abs(x[:, None] - x[None, :]), np.abs(y[:, None] - y[None, :])
    inner = band[dx] * (dy == 0) + band[dy] * (dx == 0) + 3.0 * w[0] * ((dx == 0) & (dy == 0))
    z = np.arange(CZ)
    depth = band[np.abs(z[:, None] - z[None, :])]
    pick = np.zeros((ROWS, ROWS))
    halo = np.zeros((ROWS, 2 * YH))
    for cx in range(CX):
        for q in range(4):
            pick[cx * 4 + q, cx * CY + CY - 4 + q] = 1.0
            pick[YH + cx * 4 + q, cx * CY + q] = 1.0
            for cy in range(CY):
                halo[cx * CY + cy, cx * 4 + q] = band[cy + 4 - q]
                halo[cx * CY + cy, YH + cx * 4 + q] = band[CY + q - cy]

    def parts(matrix):
        high = matrix.astype(np.float32).astype(ml_dtypes.bfloat16)
        low = (matrix - high.astype(np.float64)).astype(np.float32).astype(ml_dtypes.bfloat16)
        return [high, low]

    square = np.concatenate(parts(inner) + parts(depth) + parts(pick)[:1], axis=0)
    return square, np.concatenate(parts(halo), axis=0)


def each_partner(body):
    @pl.loop(1, NS)
    def _(step):
        body(lax.rem(5 * step, NS))


def mm(a, b):
    return jnp.dot(a, b, preferred_element_type=jnp.float32)


def kernel(
    f_prev, f_now, a_prev, a_now, velocity, aperture, source_cell, strength, receivers, traces,
    square_hbm, halo_hbm,
    prev, peak_in, corr_in, hit_out,
    now, lap, high, low, edge_f, edge, far, slab_b, slab, ids, cell_v, trace_v, square, halo_w,
    pick_send, halo, tables, wanted, wanted_by, blocks, arrived, speed, peak_send, corr_send,
    hit,
    smem_tables, source_s, strength_s,
    load_sem, edge_sem, far_send, far_recv, table_sem, id_sem, id_send, id_recv, halo_send, halo_recv, v_send, v_recv,
    c_send, c_recv, ready, go,
):
    me = lax.axis_index("shot")
    tx = lax.axis_index("tx")
    ty = lax.axis_index("ty")

    loads = [
        pltpu.make_async_copy(aperture.at[0], ids, load_sem.at[0]),
        pltpu.make_async_copy(f_now.at[0], now.at[0], load_sem.at[1]),
        pltpu.make_async_copy(a_now.at[0], now.at[1], load_sem.at[2]),
        pltpu.make_async_copy(square_hbm, square, load_sem.at[3]),
        pltpu.make_async_copy(velocity.at[0], slab_b, load_sem.at[4]),
        pltpu.make_async_copy(halo_hbm, halo_w, load_sem.at[5]),
        pltpu.make_async_copy(f_prev.at[0], prev.at[0], load_sem.at[6]),
        pltpu.make_async_copy(a_prev.at[0], prev.at[1], load_sem.at[7]),
        pltpu.make_async_copy(receivers.at[0], cell_v, load_sem.at[8]),
        pltpu.make_async_copy(traces, trace_v, load_sem.at[9]),
        pltpu.make_async_copy(source_cell, source_s, load_sem.at[10]),
        pltpu.make_async_copy(strength, strength_s, load_sem.at[11]),
    ]
    edge_loads = [
        pltpu.make_async_copy(now_hbm.at[0, 0:4], edge_f.at[field], edge_sem.at[field])
        for field, now_hbm in enumerate((f_now, a_now))
    ]

    direct = ty < DIRECT

    @pl.when((tx == 2) & jnp.logical_not(direct))
    def _():
        edge_loads[0].start()
        edge_loads[1].start()

    for n in (0, 1, 2, 4):
        loads[n].start()

    relayed = tx == 2
    home = tx + relayed.astype(jnp.int32)
    odd = lax.rem(tx, 2) == 1
    sides = [
        (ty < NTY - 1, "ty", ty + 1),
        (ty > 0, "ty", ty - 1),
        (tx < NTX - 1, "tx", tx + 1),
        (tx > 0, "tx", tx - 1),
    ]
    first = [ty < NTY - 1, None, tx == 1, tx == 1]

    barrier = pltpu.get_barrier_semaphore()

    @pl.loop(1 - relayed.astype(jnp.int32), NS)
    def _(d):
        pl.semaphore_signal(
            barrier,
            inc=1,
            device_id={"shot": lax.rem(me + d, NS), "tx": home},
            device_id_type=MESH,
        )

    @pl.when(first[0])
    def _():
        pl.semaphore_signal(
            barrier, inc=1, device_id={"tx": home, "ty": ty + 1}, device_id_type=MESH
        )

    for n in (2, 3):

        @pl.when(first[n])
        def _():
            pl.semaphore_signal(
                barrier, inc=1, device_id={"tx": sides[n][2]}, device_id_type=MESH
            )

    for n in (3, 5, 6, 7, 8, 9, 10, 11):
        loads[n].start()

    for present, start, size in (
        (ty > 0, 0, YH),
        (ty < NTY - 1, YH, YH),
        (tx > 0, 2 * YH, XH),
        (tx < NTX - 1, 2 * YH + XH, XH),
    ):

        @pl.when(jnp.logical_not(present))
        def _():
            halo[:, start : start + size, :] = jnp.zeros((2, size, CZ), jnp.bfloat16)

    def halo_copy(n, source=None):
        axis, other = sides[n][1], sides[n][2]
        start = (0, YH, 2 * YH, 2 * YH + XH)[n]
        size = YH if n < 2 else XH
        if source is None and n < 2:
            source = pick_send.at[n]
        elif source is None:
            source = high.at[:, pl.ds((CX - 4) * CY if n == 2 else 0, XH)]
        return pltpu.make_async_remote_copy(
            src_ref=source,
            dst_ref=halo.at[:, pl.ds(start, size)],
            send_sem=halo_send.at[n],
            recv_sem=halo_recv.at[n],
            device_id={axis: other},
            device_id_type=MESH,
        )

    def answer_first(n):
        axis, other = sides[n][1:]
        pl.semaphore_signal(
            ready.at[(1, 0, 3, 2)[n]], inc=1, device_id={axis: other}, device_id_type=MESH
        )

    def far_copy(field):
        return pltpu.make_async_remote_copy(
            src_ref=(f_now, a_now)[field].at[0, 0:4],
            dst_ref=far.at[field],
            send_sem=far_send.at[field],
            recv_sem=far_recv.at[field],
            device_id={"tx": tx - 1},
            device_id_type=MESH,
        )

    def across():
        pl.semaphore_wait(barrier, 1)
        answer_first(3)
        halo_copy(3, edge).start()

    @pl.when(relayed & direct)
    def _():
        pl.semaphore_wait(barrier, 1)
        answer_first(3)
        far_copy(0).start()
        far_copy(1).start()

    @pl.when(relayed & jnp.logical_not(direct))
    def _():
        edge_loads[0].wait()
        edge_loads[1].wait()
        edge[...] = edge_f[...].reshape(2, XH, CZ).astype(jnp.bfloat16)

    @pl.when(relayed & (ty >= DIRECT) & (ty < LATE))
    def _():
        across()

    loads[1].wait()
    loads[2].wait()
    for field in range(2):
        u = now[field].reshape(ROWS, CZ)
        top = u.astype(jnp.bfloat16)
        high[field] = top
        low[field] = (u - top.astype(jnp.float32)).astype(jnp.bfloat16)

    loads[0].wait()
    row_l = lax.broadcasted_iota(jnp.int32, (CX, CX), 1)
    row_s = lax.broadcasted_iota(jnp.int32, (CX, CX), 0)
    ids_l = jnp.broadcast_to(ids[...], (CX, CX))
    ids_s = ids_l.T
    earlier = ((ids_s >> 5) == (ids_l >> 5)) & (row_s < row_l)
    rank = jnp.sum(earlier.astype(jnp.int32), axis=0, keepdims=True)
    slot = 2 * (ids[...] >> 5) + rank
    placed = jnp.broadcast_to(slot, (CX, CX)).T == row_l
    tables[0, :, 0:CX] = slot
    tables[1, :, 0:CX] = jnp.sum(jnp.where(placed, row_s, 0), axis=0, keepdims=True)
    wanted[me, :, 0:CX] = jnp.sum(jnp.where(placed, ids_s & (SLAB - 1), 0), axis=0, keepdims=True)
    table_copy = pltpu.make_async_copy(tables, smem_tables, table_sem)
    table_copy.start()

    loads[3].wait()
    for field in range(2):
        picked = mm(square[4 * ROWS : 5 * ROWS, :], high[field]).astype(jnp.bfloat16)
        pick_send[0, field] = picked[0:YH]
        pick_send[1, field] = picked[YH:]

    partners = NS - 1 + (ty > 0).astype(jnp.int32) + (tx == 0).astype(jnp.int32)
    partners = partners + jnp.where(tx == 3, NS + (ty > 0).astype(jnp.int32), 0)

    @pl.when(jnp.logical_not(relayed))
    def _():
        pl.semaphore_wait(barrier, partners)

    @pl.when(tx == 3)
    def _():
        pl.semaphore_signal(go, inc=1, device_id={"tx": 2}, device_id_type=MESH)

    @pl.when(relayed & (ty >= LATE))
    def _():
        across()

    @pl.when(relayed)
    def _():
        pl.semaphore_wait(go, 1)

    def id_copy(d):
        return pltpu.make_async_remote_copy(
            src_ref=wanted.at[me],
            dst_ref=wanted.at[me],
            send_sem=id_send,
            recv_sem=id_recv,
            device_id={"shot": lax.rem(me + d, NS)},
            device_id_type=MESH,
        )

    each_partner(lambda d: id_copy(d).start())

    @pl.when(ty > 0)
    def _():
        answer_first(1)

    @pl.when(tx == 0)
    def _():
        answer_first(2)

    @pl.when(jnp.logical_not(odd))
    def _():
        halo_copy(2).start()

    @pl.when(tx == 3)
    def _():
        halo_copy(3).start()

    @pl.when(ty > 0)
    def _():
        halo_copy(1).start()

    def answer(n):
        @pl.when(first[n])
        def _():
            pl.semaphore_wait(ready.at[n], 1)
            halo_copy(n).start()

    loads[4].wait()
    slab[...] = slab_b[...].astype(jnp.float32)

    def serve(shot):
        rows = [slab[wanted_by[shot, 0, 2 * me + k]] for k in range(2)]
        return jnp.concatenate(rows, axis=0).astype(jnp.bfloat16)

    def block_copy(d):
        shot = lax.rem(me - d + NS, NS)
        return pltpu.make_async_remote_copy(
            src_ref=blocks.at[shot],
            dst_ref=arrived.at[me],
            send_sem=v_send,
            recv_sem=v_recv.at[d],
            device_id={"shot": shot},
            device_id_type=MESH,
        )

    for field in range(2):
        top, rest = high[field], low[field]
        lap[field] = (
            mm(square[0:ROWS, :], top)
            + mm(square[0:ROWS, :], rest)
            + mm(square[ROWS : 2 * ROWS, :], top)
            + mm(top, square[2 * ROWS : 3 * ROWS, :])
            + mm(rest, square[2 * ROWS : 3 * ROWS, :])
            + mm(top, square[3 * ROWS : 4 * ROWS, :])
        ).reshape(CX, CY, CZ)

    for load in loads[8:]:
        load.wait()
    row = lax.broadcasted_iota(jnp.int32, (ROWS, 1), 0)

    def local_row(along_x, along_y):
        inside = (along_x >= tx * CX) & (along_x < tx * CX + CX)
        inside = inside & (along_y >= ty * CY) & (along_y < ty * CY + CY)
        return jnp.where(inside, (along_x - tx * CX) * CY + along_y - ty * CY, -1)

    source_row = local_row(source_s[0, 0], source_s[0, 1])
    cell_row = local_row(cell_v[0:1, :], cell_v[1:2, :])
    injected = jnp.where(row == source_row, strength_s[0, 0], 0.0)
    recorded = jnp.sum(
        jnp.where(jnp.broadcast_to(row, (ROWS, NREC)) == cell_row, trace_v[...], 0.0),
        axis=1,
        keepdims=True,
    )
    surface = lax.broadcasted_iota(jnp.int32, (ROWS, CZ), 1) == SURFACE_DEPTH

    loads[5].wait()
    loads[6].wait()
    loads[7].wait()
    answer(0)

    all_but_one = pl.ds(0, NS - 1)
    pltpu.make_async_copy(wanted.at[all_but_one], wanted.at[all_but_one], id_recv).wait()
    id_local = pltpu.make_async_copy(wanted, wanted_by, id_sem)
    id_local.start()
    id_local.wait()

    @each_partner
    def _(d):
        shot = lax.rem(me - d + NS, NS)
        blocks[shot] = serve(shot)
        block_copy(d).start()

    arrived[me] = serve(me)
    @pl.when(ty >= 5)
    def _():
        answer(3)
        answer(2)

    depth_l = lax.broadcasted_iota(jnp.int32, (CY, ROWS), 1)
    same_y = (depth_l & (CY - 1)) == lax.broadcasted_iota(jnp.int32, (CY, ROWS), 0)
    block_l = jnp.where(same_y, depth_l >> 3, -1)


    @pl.loop(0, NS)
    def _(shot):
        hits = [block_l == wanted_by[shot, 0, 2 * me + k] for k in range(2)]
        rows = pl.ds(pl.multiple_of(shot * 16, 16), 16)
        hit[rows, :] = jnp.where(jnp.concatenate(hits, axis=0), 1.0, 0.0)

    hit_out[...] = hit[...].T.astype(jnp.bfloat16)

    def halo_wait(n):
        @pl.when(sides[(1, 0, 3, 2)[n]][0])
        def _():
            halo_copy(n).wait_recv()

    halo_wait(0)
    halo_wait(1)
    for field, extra in ((0, injected), (1, recorded)):
        layers = halo[field, 0 : 2 * YH]
        beyond = mm(halo_w[0:ROWS, :], layers) + mm(halo_w[ROWS:, :], layers)
        beyond = beyond + jnp.where(surface, jnp.broadcast_to(extra, (ROWS, CZ)), 0.0)
        lap[field] = lap[field] + beyond.reshape(CX, CY, CZ)
        prev[field] = 2.0 * now[field] - prev[field]

    @pl.when(ty < 5)
    def _():
        answer(3)
        answer(2)

    halo_wait(2)
    near = halo[:, 2 * YH : 2 * YH + XH].astype(jnp.float32).reshape(2, 4, CY, CZ)

    @pl.when((tx == 1) & direct)
    def _():
        far_copy(0).wait_recv()
        far_copy(1).wait_recv()

    @pl.when((tx < NTX - 1) & jnp.logical_not((tx == 1) & direct))
    def _():
        halo_copy(3).wait_recv()

    @pl.when(jnp.logical_not((tx == 1) & direct))
    def _():
        far[...] = halo[:, 2 * YH + XH :].astype(jnp.float32).reshape(2, 4, CY, CZ)

    for field in range(2):
        for q in range(4):
            for x in range(4):
                if x <= q:
                    weight = STENCIL_WEIGHTS[x + 4 - q]
                    lap[field, x] = lap[field, x] + weight * near[field, q]
                if x >= q:
                    weight = STENCIL_WEIGHTS[4 + q - x]
                    lap[field, CX - 4 + x] = lap[field, CX - 4 + x] + weight * far[field, q]

    table_copy.wait()

    def corr_copies(d):
        owner = lax.rem(me + d, NS)
        return [
            pltpu.make_async_remote_copy(
                src_ref=source.at[owner],
                dst_ref=target.at[me],
                send_sem=c_send.at[n],
                recv_sem=c_recv.at[n],
                device_id={"shot": owner},
                device_id_type=MESH,
            )
            for n, (source, target) in enumerate(((peak_send, peak_in), (corr_send, corr_in)))
        ]

    def contribute(owner):
        pair = arrived[owner].astype(jnp.float32)
        products = []
        for k in range(2):
            scaled = pair[k * CY : (k + 1) * CY] * STEP_RATIO
            courant = scaled * scaled
            speed[2 * owner + k] = courant
            r = smem_tables[1, 0, 2 * owner + k]
            products.append(
                (prev[0, r] + courant * lap[0, r]) * (prev[1, r] + courant * lap[1, r])
            )
        both = jnp.concatenate(products, axis=0)
        top = jnp.max(jnp.abs(both), axis=0, keepdims=True)
        top = jnp.maximum(jnp.maximum(top[:, : CZ // 2], top[:, CZ // 2 :]), TINY)
        scale = STEPS / top
        code = jnp.round(both * jnp.concatenate([scale, scale], axis=1))
        return top, code.astype(jnp.int32).astype(jnp.int16)

    peak_in[me], corr_in[me] = contribute(me)

    @each_partner
    def _(d):
        block_copy(d).wait_recv()
        owner = lax.rem(me + d, NS)
        peak_send[owner], corr_send[owner] = contribute(owner)
        for copy in corr_copies(d):
            copy.start()

    @pl.loop(0, CX)
    def _(r):
        courant = speed[smem_tables[0, 0, r]]
        for field in range(2):
            prev[field, r] = prev[field, r] + courant * lap[field, r]

    def all_sent(ref, sem):
        pltpu.make_async_copy(ref.at[all_but_one], ref.at[all_but_one], sem).wait()

    all_sent(wanted, id_send)
    all_sent(blocks, v_send)
    for n in range(3):

        @pl.when(sides[n][0])
        def _():
            halo_copy(n).wait_send()

    @pl.when((tx > 0) & jnp.logical_not(relayed & direct))
    def _():
        halo_copy(3).wait_send()

    @pl.when(relayed & direct)
    def _():
        far_copy(0).wait_send()
        far_copy(1).wait_send()

    all_sent(peak_send, c_send.at[0])
    all_sent(corr_send, c_send.at[1])
    all_sent(peak_in, c_recv.at[0])
    all_sent(corr_in, c_recv.at[1])


def finish(values, peak_in, corr_in, hit, f_out, a_out, image_out, image, out_sem):
    outs = [
        pltpu.make_async_copy(values.at[0], f_out.at[0], out_sem.at[0]),
        pltpu.make_async_copy(values.at[1], a_out.at[0], out_sem.at[1]),
        pltpu.make_async_copy(image, image_out.at[0], out_sem.at[2]),
    ]
    outs[0].start()
    outs[1].start()
    peak = peak_in[...]
    peak = jnp.broadcast_to(jnp.concatenate([peak, peak], axis=2), (NS, 2 * CY, CZ))
    share = corr_in[...].astype(jnp.int32).astype(jnp.float32) * (1.0 / STEPS)
    rows = (share * peak).reshape(ROWS, CZ)
    top = rows.astype(jnp.bfloat16)
    rest = (rows - top.astype(jnp.float32)).astype(jnp.bfloat16)
    image[...] = (mm(hit[...], top) + mm(hit[...], rest)).reshape(SLAB, CY, CZ)
    outs[2].start()
    for out in outs:
        out.wait()


def on_device(*arrays):
    square, halo_w = stencil_constants()
    arrays = (
        *arrays[:7],
        arrays[7].reshape(1, 1),
        jnp.swapaxes(arrays[8], 1, 2),
        arrays[9],
        jnp.asarray(square),
        jnp.asarray(halo_w),
    )
    field = jax.ShapeDtypeStruct((1, CX, CY, CZ), jnp.float32)
    dma = pltpu.SemaphoreType.DMA
    bf, f32, i32 = jnp.bfloat16, jnp.float32, jnp.int32
    scratch = [
        pltpu.VMEM((2, CX, CY, CZ), f32),
        pltpu.VMEM((2, CX, CY, CZ), f32),
        pltpu.VMEM((2, ROWS, CZ), bf),
        pltpu.VMEM((2, ROWS, CZ), bf),
        pltpu.VMEM((2, 4, CY, CZ), f32),
        pltpu.VMEM((2, XH, CZ), bf),
        pltpu.VMEM((2, 4, CY, CZ), f32),
        pltpu.VMEM((SLAB, CY, CZ), bf),
        pltpu.VMEM((SLAB, CY, CZ), f32),
        pltpu.VMEM((1, CX), i32),
        pltpu.VMEM((2, NREC), i32),
        pltpu.VMEM((1, NREC), f32),
        pltpu.VMEM(square.shape, bf),
        pltpu.VMEM(halo_w.shape, bf),
        pltpu.VMEM((2, 2, YH, CZ), bf),
        pltpu.VMEM((2, HALO, CZ), bf),
        pltpu.VMEM((2, 1, 128), i32),
        pltpu.VMEM((NS, 1, 128), i32),
        pltpu.SMEM((NS, 1, 128), i32),
        pltpu.VMEM((NS, 2 * CY, CZ), bf),
        pltpu.VMEM((NS, 2 * CY, CZ), bf),
        pltpu.VMEM((2 * NS, CY, CZ), f32),
        pltpu.VMEM((NS, 1, CZ // 2), f32),
        pltpu.VMEM((NS, 2 * CY, CZ), jnp.int16),
        pltpu.VMEM((ROWS, ROWS), f32),
        pltpu.SMEM((2, 1, 128), i32),
        pltpu.SMEM((1, 2), i32),
        pltpu.SMEM((1, 1), f32),
        dma((12,)),
        dma((2,)),
        dma((2,)),
        dma((2,)),
        dma,
        dma,
        dma,
        dma,
        dma((4,)),
        dma((4,)),
        dma,
        dma((NS,)),
        dma((2,)),
        dma((2,)),
        pltpu.SemaphoreType.REGULAR((4,)),
        pltpu.SemaphoreType.REGULAR,
    ]
    anywhere = pl.BlockSpec(memory_space=pl.ANY)
    vmem = pl.BlockSpec(memory_space=pltpu.VMEM)
    values, peak_in, corr_in, hit = pl.pallas_call(
        kernel,
        out_shape=(
            jax.ShapeDtypeStruct((2, CX, CY, CZ), f32),
            jax.ShapeDtypeStruct((NS, 1, CZ // 2), f32),
            jax.ShapeDtypeStruct((NS, 2 * CY, CZ), jnp.int16),
            jax.ShapeDtypeStruct((ROWS, ROWS), bf),
        ),
        in_specs=[anywhere] * 12,
        out_specs=(vmem,) * 4,
        scratch_shapes=scratch,
        compiler_params=pltpu.CompilerParams(
            collective_id=0, has_side_effects=True, vmem_limit_bytes=LIMIT
        ),
    )(*[a if a.size == 1 else pltpu.with_memory_space_constraint(a, pltpu.HBM) for a in arrays])
    return pl.pallas_call(
        finish,
        out_shape=(field, field, field),
        in_specs=[vmem] * 4,
        out_specs=(anywhere,) * 3,
        scratch_shapes=[pltpu.VMEM((SLAB, CY, CZ), f32), dma((3,))],
        compiler_params=pltpu.CompilerParams(vmem_limit_bytes=LIMIT),
    )(values, peak_in, corr_in, hit)


def solution(mesh):
    in_specs = (
        P("shot", "tx", "ty", None),
        P("shot", "tx", "ty", None),
        P("shot", "tx", "ty", None),
        P("shot", "tx", "ty", None),
        P(("tx", "ty"), "shot", None, None),
        P("shot", ("tx", "ty"), None),
        P("shot", None),
        P("shot"),
        P("shot", None, None),
        P("shot", None),
    )
    out_specs = (
        P("shot", "tx", "ty", None),
        P("shot", "tx", "ty", None),
        P(("tx", "ty"), "shot", None, None),
    )
    return jax.shard_map(
        on_device, mesh=mesh, in_specs=in_specs, out_specs=out_specs, check_vma=False
    )
```

```python
import functools

import jax
import jax.numpy as jnp
import ml_dtypes
import numpy as np
from jax import lax
from jax.experimental import pallas as pl
from jax.experimental.pallas import tpu as pltpu
from jax.sharding import PartitionSpec as P

SURFACE_DEPTH = 8
STENCIL_WEIGHTS = (-205.0 / 72.0, 8.0 / 5.0, -1.0 / 5.0, 8.0 / 315.0, -1.0 / 560.0)
STEP_RATIO = 0.1
MESH = pl.DeviceIdType.MESH
NS, NTX, NTY = 16, 4, 8
CX, CY, CZ = 32, 8, 256
ROWS = CX * CY
SLAB = 32
NREC = 128
YH = CX * 4
XH = 4 * CY
HALO = 2 * YH + 2 * XH
STEPS = 32766.0
TINY = 1e-34
DIRECT = 3
LATE = 6
LIMIT = 40 * 1024 * 1024


def stencil_constants():
    w = np.array(STENCIL_WEIGHTS)
    band = np.zeros(600)
    band[1:5] = w[1:]
    row = np.arange(ROWS)
    x, y = row // CY, row % CY
    dx, dy = np.abs(x[:, None] - x[None, :]), np.abs(y[:, None] - y[None, :])
    inner = band[dx] * (dy == 0) + band[dy] * (dx == 0) + 3.0 * w[0] * ((dx == 0) & (dy == 0))
    z = np.arange(CZ)
    depth = band[np.abs(z[:, None] - z[None, :])]
    pick = np.zeros((ROWS, ROWS))
    halo = np.zeros((ROWS, 2 * YH))
    for cx in range(CX):
        for q in range(4):
            pick[cx * 4 + q, cx * CY + CY - 4 + q] = 1.0
            pick[YH + cx * 4 + q, cx * CY + q] = 1.0
            for cy in range(CY):
                halo[cx * CY + cy, cx * 4 + q] = band[cy + 4 - q]
                halo[cx * CY + cy, YH + cx * 4 + q] = band[CY + q - cy]

    def parts(matrix):
        high = matrix.astype(np.float32).astype(ml_dtypes.bfloat16)
        low = (matrix - high.astype(np.float64)).astype(np.float32).astype(ml_dtypes.bfloat16)
        return [high, low]

    square = np.concatenate(parts(inner) + parts(depth) + parts(pick)[:1], axis=0)
    return square, np.concatenate(parts(halo), axis=0)


def each_partner(body, near=0):
    me = lax.axis_index("shot")
    x, y = me // 4, lax.rem(me, 4)
    turn_x, turn_y = (x < 2).astype(jnp.int32), (y < 2).astype(jnp.int32)

    @pl.loop(0, NS)
    def _(step):
        step = step + near * (NS - 1 - 2 * step)
        i, j = step // 4, lax.rem(step, 4)
        other = 4 * (i + turn_x * (3 - 2 * i)) + j + turn_y * (3 - 2 * j)
        d = lax.rem(other - me + NS, NS)

        @pl.when(d > 0)
        def _():
            body(d)


def mm(a, b):
    return jnp.dot(a, b, preferred_element_type=jnp.float32)


def kernel(
    f_prev, f_now, a_prev, a_now, velocity, aperture, source_cell, strength, receivers, traces,
    square_hbm, halo_hbm,
    prev, peak_in, corr_in, hit_out,
    now, lap, high, low, edge_f, edge, far, slab_b, slab, ids, cell_v, trace_v, square, halo_w,
    pick_send, halo, tables, wanted, wanted_by, blocks, arrived, speed, peak_send, corr_send,
    hit,
    smem_tables, source_s, strength_s,
    load_sem, edge_sem, far_send, far_recv, table_sem, id_sem, id_send, id_recv, halo_send, halo_recv, v_send, v_recv,
    c_send, c_recv, ready, go,
):
    me = lax.axis_index("shot")
    tx = lax.axis_index("tx")
    ty = lax.axis_index("ty")

    loads = [
        pltpu.make_async_copy(aperture.at[0], ids, load_sem.at[0]),
        pltpu.make_async_copy(f_now.at[0], now.at[0], load_sem.at[1]),
        pltpu.make_async_copy(a_now.at[0], now.at[1], load_sem.at[2]),
        pltpu.make_async_copy(square_hbm, square, load_sem.at[3]),
        pltpu.make_async_copy(velocity.at[0], slab_b, load_sem.at[4]),
        pltpu.make_async_copy(halo_hbm, halo_w, load_sem.at[5]),
        pltpu.make_async_copy(f_prev.at[0], prev.at[0], load_sem.at[6]),
        pltpu.make_async_copy(a_prev.at[0], prev.at[1], load_sem.at[7]),
        pltpu.make_async_copy(receivers.at[0], cell_v, load_sem.at[8]),
        pltpu.make_async_copy(traces, trace_v, load_sem.at[9]),
        pltpu.make_async_copy(source_cell, source_s, load_sem.at[10]),
        pltpu.make_async_copy(strength, strength_s, load_sem.at[11]),
    ]
    edge_loads = [
        pltpu.make_async_copy(now_hbm.at[0, 0:4], edge_f.at[field], edge_sem.at[field])
        for field, now_hbm in enumerate((f_now, a_now))
    ]

    direct = ty < DIRECT

    @pl.when((tx == 2) & jnp.logical_not(direct))
    def _():
        edge_loads[0].start()
        edge_loads[1].start()

    for n in (0, 1, 2, 4):
        loads[n].start()

    relayed = tx == 2
    home = tx + relayed.astype(jnp.int32)
    odd = lax.rem(tx, 2) == 1
    sides = [
        (ty < NTY - 1, "ty", ty + 1),
        (ty > 0, "ty", ty - 1),
        (tx < NTX - 1, "tx", tx + 1),
        (tx > 0, "tx", tx - 1),
    ]
    first = [ty < NTY - 1, None, tx == 1, tx == 1]

    barrier = pltpu.get_barrier_semaphore()

    @pl.loop(1 - relayed.astype(jnp.int32), NS)
    def _(d):
        pl.semaphore_signal(
            barrier,
            inc=1,
            device_id={"shot": lax.rem(me + d, NS), "tx": home},
            device_id_type=MESH,
        )

    @pl.when(first[0])
    def _():
        pl.semaphore_signal(
            barrier, inc=1, device_id={"tx": home, "ty": ty + 1}, device_id_type=MESH
        )

    for n in (2, 3):

        @pl.when(first[n])
        def _():
            pl.semaphore_signal(
                barrier, inc=1, device_id={"tx": sides[n][2]}, device_id_type=MESH
            )

    for n in (3, 5, 6, 7, 8, 9, 10, 11):
        loads[n].start()

    for present, start, size in (
        (ty > 0, 0, YH),
        (ty < NTY - 1, YH, YH),
        (tx > 0, 2 * YH, XH),
        (tx < NTX - 1, 2 * YH + XH, XH),
    ):

        @pl.when(jnp.logical_not(present))
        def _():
            halo[:, start : start + size, :] = jnp.zeros((2, size, CZ), jnp.bfloat16)

    def halo_copy(n, source=None):
        axis, other = sides[n][1], sides[n][2]
        start = (0, YH, 2 * YH, 2 * YH + XH)[n]
        size = YH if n < 2 else XH
        if source is None and n < 2:
            source = pick_send.at[n]
        elif source is None:
            source = high.at[:, pl.ds((CX - 4) * CY if n == 2 else 0, XH)]
        return pltpu.make_async_remote_copy(
            src_ref=source,
            dst_ref=halo.at[:, pl.ds(start, size)],
            send_sem=halo_send.at[n],
            recv_sem=halo_recv.at[n],
            device_id={axis: other},
            device_id_type=MESH,
        )

    def answer_first(n):
        axis, other = sides[n][1:]
        pl.semaphore_signal(
            ready.at[(1, 0, 3, 2)[n]], inc=1, device_id={axis: other}, device_id_type=MESH
        )

    def far_copy(field):
        return pltpu.make_async_remote_copy(
            src_ref=(f_now, a_now)[field].at[0, 0:4],
            dst_ref=far.at[field],
            send_sem=far_send.at[field],
            recv_sem=far_recv.at[field],
            device_id={"tx": tx - 1},
            device_id_type=MESH,
        )

    def across():
        pl.semaphore_wait(barrier, 1)
        answer_first(3)
        halo_copy(3, edge).start()

    @pl.when(relayed & direct)
    def _():
        pl.semaphore_wait(barrier, 1)
        answer_first(3)
        far_copy(0).start()
        far_copy(1).start()

    @pl.when(relayed & jnp.logical_not(direct))
    def _():
        edge_loads[0].wait()
        edge_loads[1].wait()
        edge[...] = edge_f[...].reshape(2, XH, CZ).astype(jnp.bfloat16)

    @pl.when(relayed & (ty >= DIRECT) & (ty < LATE))
    def _():
        across()

    loads[1].wait()
    loads[2].wait()
    for field in range(2):
        u = now[field].reshape(ROWS, CZ)
        top = u.astype(jnp.bfloat16)
        high[field] = top
        low[field] = (u - top.astype(jnp.float32)).astype(jnp.bfloat16)

    loads[0].wait()
    row_l = lax.broadcasted_iota(jnp.int32, (CX, CX), 1)
    row_s = lax.broadcasted_iota(jnp.int32, (CX, CX), 0)
    ids_l = jnp.broadcast_to(ids[...], (CX, CX))
    ids_s = ids_l.T
    earlier = ((ids_s >> 5) == (ids_l >> 5)) & (row_s < row_l)
    rank = jnp.sum(earlier.astype(jnp.int32), axis=0, keepdims=True)
    slot = 2 * (ids[...] >> 5) + rank
    placed = jnp.broadcast_to(slot, (CX, CX)).T == row_l
    tables[0, :, 0:CX] = slot
    tables[1, :, 0:CX] = jnp.sum(jnp.where(placed, row_s, 0), axis=0, keepdims=True)
    wanted[me, :, 0:CX] = jnp.sum(jnp.where(placed, ids_s & (SLAB - 1), 0), axis=0, keepdims=True)
    table_copy = pltpu.make_async_copy(tables, smem_tables, table_sem)
    table_copy.start()

    loads[3].wait()
    for field in range(2):
        picked = mm(square[4 * ROWS : 5 * ROWS, :], high[field]).astype(jnp.bfloat16)
        pick_send[0, field] = picked[0:YH]
        pick_send[1, field] = picked[YH:]

    partners = NS - 1 + (ty > 0).astype(jnp.int32) + (tx == 0).astype(jnp.int32)
    partners = partners + jnp.where(tx == 3, NS + (ty > 0).astype(jnp.int32), 0)

    @pl.when(jnp.logical_not(relayed))
    def _():
        pl.semaphore_wait(barrier, partners)

    @pl.when(tx == 3)
    def _():
        pl.semaphore_signal(go, inc=1, device_id={"tx": 2}, device_id_type=MESH)

    upper = me // 4 + lax.rem(me, 4) >= 2

    @pl.when(relayed & (ty >= LATE) & jnp.logical_not(upper))
    def _():
        across()

    @pl.when(relayed)
    def _():
        pl.semaphore_wait(go, 1)

    def id_copy(d):
        return pltpu.make_async_remote_copy(
            src_ref=wanted.at[me],
            dst_ref=wanted.at[me],
            send_sem=id_send,
            recv_sem=id_recv,
            device_id={"shot": lax.rem(me + d, NS)},
            device_id_type=MESH,
        )

    each_partner(lambda d: id_copy(d).start())

    @pl.when(relayed & (ty >= LATE) & upper)
    def _():
        across()

    @pl.when(ty > 0)
    def _():
        answer_first(1)

    @pl.when(tx == 0)
    def _():
        answer_first(2)

    @pl.when(jnp.logical_not(odd))
    def _():
        halo_copy(2).start()

    @pl.when(tx == 3)
    def _():
        halo_copy(3).start()

    @pl.when(ty > 0)
    def _():
        halo_copy(1).start()

    def answer(n):
        @pl.when(first[n])
        def _():
            pl.semaphore_wait(ready.at[n], 1)
            halo_copy(n).start()

    loads[4].wait()
    slab[...] = slab_b[...].astype(jnp.float32)

    def serve(shot):
        rows = [slab[wanted_by[shot, 0, 2 * me + k]] for k in range(2)]
        return jnp.concatenate(rows, axis=0).astype(jnp.bfloat16)

    def block_copy(d):
        shot = lax.rem(me - d + NS, NS)
        return pltpu.make_async_remote_copy(
            src_ref=blocks.at[shot],
            dst_ref=arrived.at[me],
            send_sem=v_send,
            recv_sem=v_recv.at[d],
            device_id={"shot": shot},
            device_id_type=MESH,
        )

    for field in range(2):
        top, rest = high[field], low[field]
        lap[field] = (
            mm(square[0:ROWS, :], top)
            + mm(square[0:ROWS, :], rest)
            + mm(square[ROWS : 2 * ROWS, :], top)
            + mm(top, square[2 * ROWS : 3 * ROWS, :])
            + mm(rest, square[2 * ROWS : 3 * ROWS, :])
            + mm(top, square[3 * ROWS : 4 * ROWS, :])
        ).reshape(CX, CY, CZ)

    for load in loads[8:]:
        load.wait()
    row = lax.broadcasted_iota(jnp.int32, (ROWS, 1), 0)

    def local_row(along_x, along_y):
        inside = (along_x >= tx * CX) & (along_x < tx * CX + CX)
        inside = inside & (along_y >= ty * CY) & (along_y < ty * CY + CY)
        return jnp.where(inside, (along_x - tx * CX) * CY + along_y - ty * CY, -1)

    source_row = local_row(source_s[0, 0], source_s[0, 1])
    cell_row = local_row(cell_v[0:1, :], cell_v[1:2, :])
    injected = jnp.where(row == source_row, strength_s[0, 0], 0.0)
    recorded = jnp.sum(
        jnp.where(jnp.broadcast_to(row, (ROWS, NREC)) == cell_row, trace_v[...], 0.0),
        axis=1,
        keepdims=True,
    )
    surface = lax.broadcasted_iota(jnp.int32, (ROWS, CZ), 1) == SURFACE_DEPTH

    loads[5].wait()
    loads[6].wait()
    loads[7].wait()
    answer(0)

    all_but_one = pl.ds(0, NS - 1)
    pltpu.make_async_copy(wanted.at[all_but_one], wanted.at[all_but_one], id_recv).wait()
    id_local = pltpu.make_async_copy(wanted, wanted_by, id_sem)
    id_local.start()
    id_local.wait()

    @each_partner
    def _(ahead):
        shot = lax.rem(me + ahead, NS)
        blocks[shot] = serve(shot)
        block_copy(NS - ahead).start()

    arrived[me] = serve(me)
    @pl.when(ty >= 5)
    def _():
        answer(3)
        answer(2)

    depth_l = lax.broadcasted_iota(jnp.int32, (CY, ROWS), 1)
    same_y = (depth_l & (CY - 1)) == lax.broadcasted_iota(jnp.int32, (CY, ROWS), 0)
    block_l = jnp.where(same_y, depth_l >> 3, -1)


    @pl.loop(0, NS)
    def _(shot):
        hits = [block_l == wanted_by[shot, 0, 2 * me + k] for k in range(2)]
        rows = pl.ds(pl.multiple_of(shot * 16, 16), 16)
        hit[rows, :] = jnp.where(jnp.concatenate(hits, axis=0), 1.0, 0.0)

    hit_out[...] = hit[...].T.astype(jnp.bfloat16)

    def halo_wait(n):
        @pl.when(sides[(1, 0, 3, 2)[n]][0])
        def _():
            halo_copy(n).wait_recv()

    halo_wait(0)
    halo_wait(1)
    for field, extra in ((0, injected), (1, recorded)):
        layers = halo[field, 0 : 2 * YH]
        beyond = mm(halo_w[0:ROWS, :], layers) + mm(halo_w[ROWS:, :], layers)
        beyond = beyond + jnp.where(surface, jnp.broadcast_to(extra, (ROWS, CZ)), 0.0)
        lap[field] = lap[field] + beyond.reshape(CX, CY, CZ)
        prev[field] = 2.0 * now[field] - prev[field]

    @pl.when(ty < 5)
    def _():
        answer(3)
        answer(2)

    halo_wait(2)
    near = halo[:, 2 * YH : 2 * YH + XH].astype(jnp.float32).reshape(2, 4, CY, CZ)

    @pl.when((tx == 1) & direct)
    def _():
        far_copy(0).wait_recv()
        far_copy(1).wait_recv()

    @pl.when((tx < NTX - 1) & jnp.logical_not((tx == 1) & direct))
    def _():
        halo_copy(3).wait_recv()

    @pl.when(jnp.logical_not((tx == 1) & direct))
    def _():
        far[...] = halo[:, 2 * YH + XH :].astype(jnp.float32).reshape(2, 4, CY, CZ)

    for field in range(2):
        for q in range(4):
            for x in range(4):
                if x <= q:
                    weight = STENCIL_WEIGHTS[x + 4 - q]
                    lap[field, x] = lap[field, x] + weight * near[field, q]
                if x >= q:
                    weight = STENCIL_WEIGHTS[4 + q - x]
                    lap[field, CX - 4 + x] = lap[field, CX - 4 + x] + weight * far[field, q]

    table_copy.wait()

    def corr_copies(d):
        owner = lax.rem(me + d, NS)
        return [
            pltpu.make_async_remote_copy(
                src_ref=source.at[owner],
                dst_ref=target.at[me],
                send_sem=c_send.at[n],
                recv_sem=c_recv.at[n],
                device_id={"shot": owner},
                device_id_type=MESH,
            )
            for n, (source, target) in enumerate(((peak_send, peak_in), (corr_send, corr_in)))
        ]

    def contribute(owner):
        pair = arrived[owner].astype(jnp.float32)
        products = []
        for k in range(2):
            scaled = pair[k * CY : (k + 1) * CY] * STEP_RATIO
            courant = scaled * scaled
            speed[2 * owner + k] = courant
            r = smem_tables[1, 0, 2 * owner + k]
            products.append(
                (prev[0, r] + courant * lap[0, r]) * (prev[1, r] + courant * lap[1, r])
            )
        both = jnp.concatenate(products, axis=0)
        top = jnp.max(jnp.abs(both), axis=0, keepdims=True)
        top = jnp.maximum(jnp.maximum(top[:, : CZ // 2], top[:, CZ // 2 :]), TINY)
        scale = STEPS / top
        code = jnp.round(both * jnp.concatenate([scale, scale], axis=1))
        return top, code.astype(jnp.int32).astype(jnp.int16)

    peak_in[me], corr_in[me] = contribute(me)

    def one_owner(d):
        block_copy(d).wait_recv()
        owner = lax.rem(me + d, NS)
        peak_send[owner], corr_send[owner] = contribute(owner)
        for copy in corr_copies(d):
            copy.start()

    each_partner(one_owner, near=((tx == 0) | (tx == 3)).astype(jnp.int32))

    @pl.loop(0, CX)
    def _(r):
        courant = speed[smem_tables[0, 0, r]]
        for field in range(2):
            prev[field, r] = prev[field, r] + courant * lap[field, r]

    def all_sent(ref, sem):
        pltpu.make_async_copy(ref.at[all_but_one], ref.at[all_but_one], sem).wait()

    all_sent(wanted, id_send)
    all_sent(blocks, v_send)
    for n in range(3):

        @pl.when(sides[n][0])
        def _():
            halo_copy(n).wait_send()

    @pl.when((tx > 0) & jnp.logical_not(relayed & direct))
    def _():
        halo_copy(3).wait_send()

    @pl.when(relayed & direct)
    def _():
        far_copy(0).wait_send()
        far_copy(1).wait_send()

    all_sent(peak_send, c_send.at[0])
    all_sent(corr_send, c_send.at[1])
    all_sent(peak_in, c_recv.at[0])
    all_sent(corr_in, c_recv.at[1])


def finish(values, peak_in, corr_in, hit, f_out, a_out, image_out, image, out_sem):
    outs = [
        pltpu.make_async_copy(values.at[0], f_out.at[0], out_sem.at[0]),
        pltpu.make_async_copy(values.at[1], a_out.at[0], out_sem.at[1]),
        pltpu.make_async_copy(image, image_out.at[0], out_sem.at[2]),
    ]
    outs[0].start()
    outs[1].start()
    peak = peak_in[...]
    peak = jnp.broadcast_to(jnp.concatenate([peak, peak], axis=2), (NS, 2 * CY, CZ))
    share = corr_in[...].astype(jnp.int32).astype(jnp.float32) * (1.0 / STEPS)
    rows = (share * peak).reshape(ROWS, CZ)
    top = rows.astype(jnp.bfloat16)
    rest = (rows - top.astype(jnp.float32)).astype(jnp.bfloat16)
    image[...] = (mm(hit[...], top) + mm(hit[...], rest)).reshape(SLAB, CY, CZ)
    outs[2].start()
    for out in outs:
        out.wait()


def on_device(*arrays):
    square, halo_w = stencil_constants()
    arrays = (
        *arrays[:7],
        arrays[7].reshape(1, 1),
        jnp.swapaxes(arrays[8], 1, 2),
        arrays[9],
        jnp.asarray(square),
        jnp.asarray(halo_w),
    )
    field = jax.ShapeDtypeStruct((1, CX, CY, CZ), jnp.float32)
    dma = pltpu.SemaphoreType.DMA
    bf, f32, i32 = jnp.bfloat16, jnp.float32, jnp.int32
    scratch = [
        pltpu.VMEM((2, CX, CY, CZ), f32),
        pltpu.VMEM((2, CX, CY, CZ), f32),
        pltpu.VMEM((2, ROWS, CZ), bf),
        pltpu.VMEM((2, ROWS, CZ), bf),
        pltpu.VMEM((2, 4, CY, CZ), f32),
        pltpu.VMEM((2, XH, CZ), bf),
        pltpu.VMEM((2, 4, CY, CZ), f32),
        pltpu.VMEM((SLAB, CY, CZ), bf),
        pltpu.VMEM((SLAB, CY, CZ), f32),
        pltpu.VMEM((1, CX), i32),
        pltpu.VMEM((2, NREC), i32),
        pltpu.VMEM((1, NREC), f32),
        pltpu.VMEM(square.shape, bf),
        pltpu.VMEM(halo_w.shape, bf),
        pltpu.VMEM((2, 2, YH, CZ), bf),
        pltpu.VMEM((2, HALO, CZ), bf),
        pltpu.VMEM((2, 1, 128), i32),
        pltpu.VMEM((NS, 1, 128), i32),
        pltpu.SMEM((NS, 1, 128), i32),
        pltpu.VMEM((NS, 2 * CY, CZ), bf),
        pltpu.VMEM((NS, 2 * CY, CZ), bf),
        pltpu.VMEM((2 * NS, CY, CZ), f32),
        pltpu.VMEM((NS, 1, CZ // 2), f32),
        pltpu.VMEM((NS, 2 * CY, CZ), jnp.int16),
        pltpu.VMEM((ROWS, ROWS), f32),
        pltpu.SMEM((2, 1, 128), i32),
        pltpu.SMEM((1, 2), i32),
        pltpu.SMEM((1, 1), f32),
        dma((12,)),
        dma((2,)),
        dma((2,)),
        dma((2,)),
        dma,
        dma,
        dma,
        dma,
        dma((4,)),
        dma((4,)),
        dma,
        dma((NS,)),
        dma((2,)),
        dma((2,)),
        pltpu.SemaphoreType.REGULAR((4,)),
        pltpu.SemaphoreType.REGULAR,
    ]
    anywhere = pl.BlockSpec(memory_space=pl.ANY)
    vmem = pl.BlockSpec(memory_space=pltpu.VMEM)
    values, peak_in, corr_in, hit = pl.pallas_call(
        kernel,
        out_shape=(
            jax.ShapeDtypeStruct((2, CX, CY, CZ), f32),
            jax.ShapeDtypeStruct((NS, 1, CZ // 2), f32),
            jax.ShapeDtypeStruct((NS, 2 * CY, CZ), jnp.int16),
            jax.ShapeDtypeStruct((ROWS, ROWS), bf),
        ),
        in_specs=[anywhere] * 12,
        out_specs=(vmem,) * 4,
        scratch_shapes=scratch,
        compiler_params=pltpu.CompilerParams(
            collective_id=0, has_side_effects=True, vmem_limit_bytes=LIMIT
        ),
    )(*[a if a.size == 1 else pltpu.with_memory_space_constraint(a, pltpu.HBM) for a in arrays])
    return pl.pallas_call(
        finish,
        out_shape=(field, field, field),
        in_specs=[vmem] * 4,
        out_specs=(anywhere,) * 3,
        scratch_shapes=[pltpu.VMEM((SLAB, CY, CZ), f32), dma((3,))],
        compiler_params=pltpu.CompilerParams(vmem_limit_bytes=LIMIT),
    )(values, peak_in, corr_in, hit)


def solution(mesh):
    in_specs = (
        P("shot", "tx", "ty", None),
        P("shot", "tx", "ty", None),
        P("shot", "tx", "ty", None),
        P("shot", "tx", "ty", None),
        P(("tx", "ty"), "shot", None, None),
        P("shot", ("tx", "ty"), None),
        P("shot", None),
        P("shot"),
        P("shot", None, None),
        P("shot", None),
    )
    out_specs = (
        P("shot", "tx", "ty", None),
        P("shot", "tx", "ty", None),
        P(("tx", "ty"), "shot", None, None),
    )
    return jax.shard_map(
        on_device, mesh=mesh, in_specs=in_specs, out_specs=out_specs, check_vma=False
    )
```

```python
import functools

import jax
import jax.numpy as jnp
import ml_dtypes
import numpy as np
from jax import lax
from jax.experimental import pallas as pl
from jax.experimental.pallas import tpu as pltpu
from jax.sharding import PartitionSpec as P

SURFACE_DEPTH = 8
STENCIL_WEIGHTS = (-205.0 / 72.0, 8.0 / 5.0, -1.0 / 5.0, 8.0 / 315.0, -1.0 / 560.0)
STEP_RATIO = 0.1
MESH = pl.DeviceIdType.MESH
NS, NTX, NTY = 16, 4, 8
CX, CY, CZ = 32, 8, 256
ROWS = CX * CY
SLAB = 32
NREC = 128
YH = CX * 4
XH = 4 * CY
HALO = 2 * YH + 2 * XH
STEPS = 32766.0
TINY = 1e-34
DIRECT = 1
LATE = 6
LIMIT = 40 * 1024 * 1024


def stencil_constants():
    w = np.array(STENCIL_WEIGHTS)
    band = np.zeros(600)
    band[1:5] = w[1:]
    row = np.arange(ROWS)
    x, y = row // CY, row % CY
    dx, dy = np.abs(x[:, None] - x[None, :]), np.abs(y[:, None] - y[None, :])
    inner = band[dx] * (dy == 0) + band[dy] * (dx == 0) + 3.0 * w[0] * ((dx == 0) & (dy == 0))
    z = np.arange(CZ)
    depth = band[np.abs(z[:, None] - z[None, :])]
    pick = np.zeros((ROWS, ROWS))
    halo = np.zeros((ROWS, 2 * YH))
    for cx in range(CX):
        for q in range(4):
            pick[cx * 4 + q, cx * CY + CY - 4 + q] = 1.0
            pick[YH + cx * 4 + q, cx * CY + q] = 1.0
            for cy in range(CY):
                halo[cx * CY + cy, cx * 4 + q] = band[cy + 4 - q]
                halo[cx * CY + cy, YH + cx * 4 + q] = band[CY + q - cy]

    def parts(matrix):
        high = matrix.astype(np.float32).astype(ml_dtypes.bfloat16)
        low = (matrix - high.astype(np.float64)).astype(np.float32).astype(ml_dtypes.bfloat16)
        return [high, low]

    square = np.concatenate(parts(inner) + parts(depth) + parts(pick)[:1], axis=0)
    return square, np.concatenate(parts(halo), axis=0)


def each_partner(body, near=0):
    me = lax.axis_index("shot")
    turn_x = (me < NS // 2).astype(jnp.int32)
    turn_y = (lax.rem(me, 4) < 2).astype(jnp.int32)
    turn_x = turn_x + near * (1 - 2 * turn_x)
    turn_y = turn_y + near * (1 - 2 * turn_y)
    corner, step_x, step_y = 12 * turn_x + 3 * turn_y, 4 - 8 * turn_x, 1 - 2 * turn_y

    @pl.loop(0, 4)
    def _(i):
        for j in range(4):
            other = corner + step_x * i + step_y * j

            @pl.when(other != me)
            def _():
                body(other)


def mm(a, b):
    return jnp.dot(a, b, preferred_element_type=jnp.float32)


def kernel(
    f_prev, f_now, a_prev, a_now, velocity, aperture, source_cell, strength, receivers, traces,
    square_hbm, halo_hbm,
    prev, peak_in, corr_in, hit_out,
    now, lap, high, low, edge_f, edge, far, slab_b, slab, ids, cell_v, trace_v, square, halo_w,
    pick_send, halo, tables, wanted, wanted_by, blocks, arrived, speed, peak_send, corr_send,
    hit,
    smem_tables, source_s, strength_s,
    load_sem, edge_sem, far_send, far_recv, table_sem, id_sem, id_send, id_recv, halo_send, halo_recv, v_send, v_recv,
    c_send, c_recv, ready, go,
):
    me = lax.axis_index("shot")
    tx = lax.axis_index("tx")
    ty = lax.axis_index("ty")

    loads = [
        pltpu.make_async_copy(aperture.at[0], ids, load_sem.at[0]),
        pltpu.make_async_copy(f_now.at[0], now.at[0], load_sem.at[1]),
        pltpu.make_async_copy(a_now.at[0], now.at[1], load_sem.at[2]),
        pltpu.make_async_copy(square_hbm, square, load_sem.at[3]),
        pltpu.make_async_copy(velocity.at[0], slab_b, load_sem.at[4]),
        pltpu.make_async_copy(halo_hbm, halo_w, load_sem.at[5]),
        pltpu.make_async_copy(f_prev.at[0], prev.at[0], load_sem.at[6]),
        pltpu.make_async_copy(a_prev.at[0], prev.at[1], load_sem.at[7]),
        pltpu.make_async_copy(receivers.at[0], cell_v, load_sem.at[8]),
        pltpu.make_async_copy(traces, trace_v, load_sem.at[9]),
        pltpu.make_async_copy(source_cell, source_s, load_sem.at[10]),
        pltpu.make_async_copy(strength, strength_s, load_sem.at[11]),
    ]
    edge_loads = [
        pltpu.make_async_copy(now_hbm.at[0, 0:4], edge_f.at[field], edge_sem.at[field])
        for field, now_hbm in enumerate((f_now, a_now))
    ]

    direct = ty < DIRECT

    @pl.when((tx == 2) & jnp.logical_not(direct))
    def _():
        edge_loads[0].start()
        edge_loads[1].start()

    for n in (0, 1, 2, 4):
        loads[n].start()

    relayed = tx == 2
    home = tx + relayed.astype(jnp.int32)
    odd = lax.rem(tx, 2) == 1
    sides = [
        (ty < NTY - 1, "ty", ty + 1),
        (ty > 0, "ty", ty - 1),
        (tx < NTX - 1, "tx", tx + 1),
        (tx > 0, "tx", tx - 1),
    ]
    first = [ty < NTY - 1, None, tx == 1, tx == 1]

    barrier = pltpu.get_barrier_semaphore()

    @pl.loop(1 - relayed.astype(jnp.int32), NS)
    def _(d):
        pl.semaphore_signal(
            barrier,
            inc=1,
            device_id={"shot": lax.rem(me + d, NS), "tx": home},
            device_id_type=MESH,
        )

    @pl.when(first[0])
    def _():
        pl.semaphore_signal(
            barrier, inc=1, device_id={"tx": home, "ty": ty + 1}, device_id_type=MESH
        )

    mutual = ty >= LATE
    for n, says in ((2, first[2]), (3, first[3] | (relayed & mutual))):

        @pl.when(says)
        def _():
            pl.semaphore_signal(
                barrier, inc=1, device_id={"tx": sides[n][2]}, device_id_type=MESH
            )

    for n in (3, 5, 6, 7, 8, 9, 10, 11):
        loads[n].start()

    for present, start, size in (
        (ty > 0, 0, YH),
        (ty < NTY - 1, YH, YH),
        (tx > 0, 2 * YH, XH),
        (tx < NTX - 1, 2 * YH + XH, XH),
    ):

        @pl.when(jnp.logical_not(present))
        def _():
            halo[:, start : start + size, :] = jnp.zeros((2, size, CZ), jnp.bfloat16)

    def halo_copy(n, source=None):
        axis, other = sides[n][1], sides[n][2]
        start = (0, YH, 2 * YH, 2 * YH + XH)[n]
        size = YH if n < 2 else XH
        if source is None and n < 2:
            source = pick_send.at[n]
        elif source is None:
            source = high.at[:, pl.ds((CX - 4) * CY if n == 2 else 0, XH)]
        return pltpu.make_async_remote_copy(
            src_ref=source,
            dst_ref=halo.at[:, pl.ds(start, size)],
            send_sem=halo_send.at[n],
            recv_sem=halo_recv.at[n],
            device_id={axis: other},
            device_id_type=MESH,
        )

    def answer_first(n):
        axis, other = sides[n][1:]
        pl.semaphore_signal(
            ready.at[(1, 0, 3, 2)[n]], inc=1, device_id={axis: other}, device_id_type=MESH
        )

    def far_copy(field):
        return pltpu.make_async_remote_copy(
            src_ref=(f_now, a_now)[field].at[0, 0:4],
            dst_ref=far.at[field],
            send_sem=far_send.at[field],
            recv_sem=far_recv.at[field],
            device_id={"tx": tx - 1},
            device_id_type=MESH,
        )

    def across():
        pl.semaphore_wait(barrier, 1)

        @pl.when(jnp.logical_not(mutual))
        def _():
            answer_first(3)

        halo_copy(3, edge).start()

    @pl.when(relayed & direct)
    def _():
        pl.semaphore_wait(barrier, 1)
        answer_first(3)
        far_copy(0).start()
        far_copy(1).start()

    @pl.when(relayed & jnp.logical_not(direct))
    def _():
        edge_loads[0].wait()
        edge_loads[1].wait()
        edge[...] = edge_f[...].reshape(2, XH, CZ).astype(jnp.bfloat16)

    @pl.when(relayed & (ty >= DIRECT) & jnp.logical_not(mutual))
    def _():
        across()

    loads[1].wait()
    loads[2].wait()
    for field in range(2):
        u = now[field].reshape(ROWS, CZ)
        top = u.astype(jnp.bfloat16)
        high[field] = top
        low[field] = (u - top.astype(jnp.float32)).astype(jnp.bfloat16)

    loads[0].wait()
    row_l = lax.broadcasted_iota(jnp.int32, (CX, CX), 1)
    row_s = lax.broadcasted_iota(jnp.int32, (CX, CX), 0)
    ids_l = jnp.broadcast_to(ids[...], (CX, CX))
    ids_s = ids_l.T
    earlier = ((ids_s >> 5) == (ids_l >> 5)) & (row_s < row_l)
    rank = jnp.sum(earlier.astype(jnp.int32), axis=0, keepdims=True)
    slot = 2 * (ids[...] >> 5) + rank
    placed = jnp.broadcast_to(slot, (CX, CX)).T == row_l
    tables[0, :, 0:CX] = slot
    tables[1, :, 0:CX] = jnp.sum(jnp.where(placed, row_s, 0), axis=0, keepdims=True)
    wanted[me, :, 0:CX] = jnp.sum(jnp.where(placed, ids_s & (SLAB - 1), 0), axis=0, keepdims=True)
    table_copy = pltpu.make_async_copy(tables, smem_tables, table_sem)
    table_copy.start()

    loads[3].wait()
    for field in range(2):
        picked = mm(square[4 * ROWS : 5 * ROWS, :], high[field]).astype(jnp.bfloat16)
        pick_send[0, field] = picked[0:YH]
        pick_send[1, field] = picked[YH:]

    partners = NS - 1 + (ty > 0).astype(jnp.int32) + (tx == 0).astype(jnp.int32)
    partners = partners + ((tx == 1) & mutual).astype(jnp.int32)
    partners = partners + jnp.where(tx == 3, NS + (ty > 0).astype(jnp.int32), 0)

    @pl.when(jnp.logical_not(relayed))
    def _():
        pl.semaphore_wait(barrier, partners)

    @pl.when(tx == 3)
    def _():
        pl.semaphore_signal(go, inc=1, device_id={"tx": 2}, device_id_type=MESH)

    upper = me // 4 + lax.rem(me, 4) >= 2

    @pl.when(relayed & mutual & jnp.logical_not(upper))
    def _():
        across()

    @pl.when(relayed)
    def _():
        pl.semaphore_wait(go, 1)

    def id_copy(other):
        return pltpu.make_async_remote_copy(
            src_ref=wanted.at[me],
            dst_ref=wanted.at[me],
            send_sem=id_send,
            recv_sem=id_recv,
            device_id={"shot": other},
            device_id_type=MESH,
        )

    each_partner(lambda other: id_copy(other).start())

    @pl.when(relayed & mutual & upper)
    def _():
        across()

    @pl.when(ty > 0)
    def _():
        answer_first(1)

    @pl.when(tx == 0)
    def _():
        answer_first(2)

    @pl.when(jnp.logical_not(odd) | ((tx == 1) & mutual))
    def _():
        halo_copy(2).start()

    @pl.when(tx == 3)
    def _():
        halo_copy(3).start()

    @pl.when(ty > 0)
    def _():
        halo_copy(1).start()

    def answer(n):
        @pl.when(first[n])
        def _():
            pl.semaphore_wait(ready.at[n], 1)
            halo_copy(n).start()

    loads[4].wait()
    slab[...] = slab_b[...].astype(jnp.float32)

    def serve(shot):
        rows = [slab[wanted_by[shot, 0, 2 * me + k]] for k in range(2)]
        return jnp.concatenate(rows, axis=0).astype(jnp.bfloat16)

    def block_copy(owner, shot):
        return pltpu.make_async_remote_copy(
            src_ref=blocks.at[shot],
            dst_ref=arrived.at[owner],
            send_sem=v_send,
            recv_sem=v_recv.at[owner],
            device_id={"shot": shot},
            device_id_type=MESH,
        )

    for field in range(2):
        top, rest = high[field], low[field]
        lap[field] = (
            mm(square[0:ROWS, :], top)
            + mm(square[0:ROWS, :], rest)
            + mm(square[ROWS : 2 * ROWS, :], top)
            + mm(top, square[2 * ROWS : 3 * ROWS, :])
            + mm(rest, square[2 * ROWS : 3 * ROWS, :])
            + mm(top, square[3 * ROWS : 4 * ROWS, :])
        ).reshape(CX, CY, CZ)

    for load in loads[8:]:
        load.wait()
    row = lax.broadcasted_iota(jnp.int32, (ROWS, 1), 0)

    def local_row(along_x, along_y):
        inside = (along_x >= tx * CX) & (along_x < tx * CX + CX)
        inside = inside & (along_y >= ty * CY) & (along_y < ty * CY + CY)
        return jnp.where(inside, (along_x - tx * CX) * CY + along_y - ty * CY, -1)

    source_row = local_row(source_s[0, 0], source_s[0, 1])
    cell_row = local_row(cell_v[0:1, :], cell_v[1:2, :])
    injected = jnp.where(row == source_row, strength_s[0, 0], 0.0)
    recorded = jnp.sum(
        jnp.where(jnp.broadcast_to(row, (ROWS, NREC)) == cell_row, trace_v[...], 0.0),
        axis=1,
        keepdims=True,
    )
    surface = lax.broadcasted_iota(jnp.int32, (ROWS, CZ), 1) == SURFACE_DEPTH

    loads[5].wait()
    loads[6].wait()
    loads[7].wait()
    answer(0)

    all_but_one = pl.ds(0, NS - 1)
    pltpu.make_async_copy(wanted.at[all_but_one], wanted.at[all_but_one], id_recv).wait()
    id_local = pltpu.make_async_copy(wanted, wanted_by, id_sem)
    id_local.start()
    id_local.wait()

    @each_partner
    def _(shot):
        blocks[shot] = serve(shot)
        block_copy(me, shot).start()

    arrived[me] = serve(me)
    @pl.when(ty >= 5)
    def _():
        answer(3)

        @pl.when(jnp.logical_not(mutual))
        def _():
            answer(2)

    depth_l = lax.broadcasted_iota(jnp.int32, (CY, ROWS), 1)
    same_y = (depth_l & (CY - 1)) == lax.broadcasted_iota(jnp.int32, (CY, ROWS), 0)
    block_l = jnp.where(same_y, depth_l >> 3, -1)


    @pl.loop(0, NS)
    def _(shot):
        hits = [block_l == wanted_by[shot, 0, 2 * me + k] for k in range(2)]
        rows = pl.ds(pl.multiple_of(shot * 16, 16), 16)
        hit[rows, :] = jnp.where(jnp.concatenate(hits, axis=0), 1.0, 0.0)

    hit_out[...] = hit[...].T.astype(jnp.bfloat16)

    def halo_wait(n):
        @pl.when(sides[(1, 0, 3, 2)[n]][0])
        def _():
            halo_copy(n).wait_recv()

    halo_wait(0)
    halo_wait(1)
    for field, extra in ((0, injected), (1, recorded)):
        layers = halo[field, 0 : 2 * YH]
        beyond = mm(halo_w[0:ROWS, :], layers) + mm(halo_w[ROWS:, :], layers)
        beyond = beyond + jnp.where(surface, jnp.broadcast_to(extra, (ROWS, CZ)), 0.0)
        lap[field] = lap[field] + beyond.reshape(CX, CY, CZ)
        prev[field] = 2.0 * now[field] - prev[field]

    @pl.when(ty < 5)
    def _():
        answer(3)
        answer(2)

    halo_wait(2)
    near = halo[:, 2 * YH : 2 * YH + XH].astype(jnp.float32).reshape(2, 4, CY, CZ)

    @pl.when((tx == 1) & direct)
    def _():
        far_copy(0).wait_recv()
        far_copy(1).wait_recv()

    @pl.when((tx < NTX - 1) & jnp.logical_not((tx == 1) & direct))
    def _():
        halo_copy(3).wait_recv()

    @pl.when(jnp.logical_not((tx == 1) & direct))
    def _():
        far[...] = halo[:, 2 * YH + XH :].astype(jnp.float32).reshape(2, 4, CY, CZ)

    for field in range(2):
        for q in range(4):
            for x in range(4):
                if x <= q:
                    weight = STENCIL_WEIGHTS[x + 4 - q]
                    lap[field, x] = lap[field, x] + weight * near[field, q]
                if x >= q:
                    weight = STENCIL_WEIGHTS[4 + q - x]
                    lap[field, CX - 4 + x] = lap[field, CX - 4 + x] + weight * far[field, q]

    table_copy.wait()

    def corr_copies(owner):
        return [
            pltpu.make_async_remote_copy(
                src_ref=source.at[owner],
                dst_ref=target.at[me],
                send_sem=c_send.at[n],
                recv_sem=c_recv.at[n],
                device_id={"shot": owner},
                device_id_type=MESH,
            )
            for n, (source, target) in enumerate(((peak_send, peak_in), (corr_send, corr_in)))
        ]

    def contribute(owner):
        pair = arrived[owner].astype(jnp.float32)
        products = []
        for k in range(2):
            scaled = pair[k * CY : (k + 1) * CY] * STEP_RATIO
            courant = scaled * scaled
            speed[2 * owner + k] = courant
            r = smem_tables[1, 0, 2 * owner + k]
            products.append(
                (prev[0, r] + courant * lap[0, r]) * (prev[1, r] + courant * lap[1, r])
            )
        both = jnp.concatenate(products, axis=0)
        top = jnp.max(jnp.abs(both), axis=0, keepdims=True)
        top = jnp.maximum(jnp.maximum(top[:, : CZ // 2], top[:, CZ // 2 :]), TINY)
        scale = STEPS / top
        code = jnp.round(both * jnp.concatenate([scale, scale], axis=1))
        return top, code.astype(jnp.int32).astype(jnp.int16)

    peak_in[me], corr_in[me] = contribute(me)

    def one_owner(owner):
        block_copy(owner, me).wait_recv()
        peak_send[owner], corr_send[owner] = contribute(owner)
        for copy in corr_copies(owner):
            copy.start()

    each_partner(one_owner, near=((tx == 0) | (tx == 3)).astype(jnp.int32))

    @pl.loop(0, CX)
    def _(r):
        courant = speed[smem_tables[0, 0, r]]
        for field in range(2):
            prev[field, r] = prev[field, r] + courant * lap[field, r]

    def all_sent(ref, sem):
        pltpu.make_async_copy(ref.at[all_but_one], ref.at[all_but_one], sem).wait()

    all_sent(wanted, id_send)
    all_sent(blocks, v_send)
    for n in range(3):

        @pl.when(sides[n][0])
        def _():
            halo_copy(n).wait_send()

    @pl.when((tx > 0) & jnp.logical_not(relayed & direct))
    def _():
        halo_copy(3).wait_send()

    @pl.when(relayed & direct)
    def _():
        far_copy(0).wait_send()
        far_copy(1).wait_send()

    all_sent(peak_send, c_send.at[0])
    all_sent(corr_send, c_send.at[1])
    all_sent(peak_in, c_recv.at[0])
    all_sent(corr_in, c_recv.at[1])


def finish(values, peak_in, corr_in, hit, f_out, a_out, image_out, image, out_sem):
    outs = [
        pltpu.make_async_copy(values.at[0], f_out.at[0], out_sem.at[0]),
        pltpu.make_async_copy(values.at[1], a_out.at[0], out_sem.at[1]),
        pltpu.make_async_copy(image, image_out.at[0], out_sem.at[2]),
    ]
    outs[0].start()
    outs[1].start()
    peak = peak_in[...]
    peak = jnp.broadcast_to(jnp.concatenate([peak, peak], axis=2), (NS, 2 * CY, CZ))
    share = corr_in[...].astype(jnp.int32).astype(jnp.float32) * (1.0 / STEPS)
    rows = (share * peak).reshape(ROWS, CZ)
    top = rows.astype(jnp.bfloat16)
    rest = (rows - top.astype(jnp.float32)).astype(jnp.bfloat16)
    image[...] = (mm(hit[...], top) + mm(hit[...], rest)).reshape(SLAB, CY, CZ)
    outs[2].start()
    for out in outs:
        out.wait()


def on_device(*arrays):
    square, halo_w = stencil_constants()
    arrays = (
        *arrays[:7],
        arrays[7].reshape(1, 1),
        jnp.swapaxes(arrays[8], 1, 2),
        arrays[9],
        jnp.asarray(square),
        jnp.asarray(halo_w),
    )
    field = jax.ShapeDtypeStruct((1, CX, CY, CZ), jnp.float32)
    dma = pltpu.SemaphoreType.DMA
    bf, f32, i32 = jnp.bfloat16, jnp.float32, jnp.int32
    scratch = [
        pltpu.VMEM((2, CX, CY, CZ), f32),
        pltpu.VMEM((2, CX, CY, CZ), f32),
        pltpu.VMEM((2, ROWS, CZ), bf),
        pltpu.VMEM((2, ROWS, CZ), bf),
        pltpu.VMEM((2, 4, CY, CZ), f32),
        pltpu.VMEM((2, XH, CZ), bf),
        pltpu.VMEM((2, 4, CY, CZ), f32),
        pltpu.VMEM((SLAB, CY, CZ), bf),
        pltpu.VMEM((SLAB, CY, CZ), f32),
        pltpu.VMEM((1, CX), i32),
        pltpu.VMEM((2, NREC), i32),
        pltpu.VMEM((1, NREC), f32),
        pltpu.VMEM(square.shape, bf),
        pltpu.VMEM(halo_w.shape, bf),
        pltpu.VMEM((2, 2, YH, CZ), bf),
        pltpu.VMEM((2, HALO, CZ), bf),
        pltpu.VMEM((2, 1, 128), i32),
        pltpu.VMEM((NS, 1, 128), i32),
        pltpu.SMEM((NS, 1, 128), i32),
        pltpu.VMEM((NS, 2 * CY, CZ), bf),
        pltpu.VMEM((NS, 2 * CY, CZ), bf),
        pltpu.VMEM((2 * NS, CY, CZ), f32),
        pltpu.VMEM((NS, 1, CZ // 2), f32),
        pltpu.VMEM((NS, 2 * CY, CZ), jnp.int16),
        pltpu.VMEM((ROWS, ROWS), f32),
        pltpu.SMEM((2, 1, 128), i32),
        pltpu.SMEM((1, 2), i32),
        pltpu.SMEM((1, 1), f32),
        dma((12,)),
        dma((2,)),
        dma((2,)),
        dma((2,)),
        dma,
        dma,
        dma,
        dma,
        dma((4,)),
        dma((4,)),
        dma,
        dma((NS,)),
        dma((2,)),
        dma((2,)),
        pltpu.SemaphoreType.REGULAR((4,)),
        pltpu.SemaphoreType.REGULAR,
    ]
    anywhere = pl.BlockSpec(memory_space=pl.ANY)
    vmem = pl.BlockSpec(memory_space=pltpu.VMEM)
    values, peak_in, corr_in, hit = pl.pallas_call(
        kernel,
        out_shape=(
            jax.ShapeDtypeStruct((2, CX, CY, CZ), f32),
            jax.ShapeDtypeStruct((NS, 1, CZ // 2), f32),
            jax.ShapeDtypeStruct((NS, 2 * CY, CZ), jnp.int16),
            jax.ShapeDtypeStruct((ROWS, ROWS), bf),
        ),
        in_specs=[anywhere] * 12,
        out_specs=(vmem,) * 4,
        scratch_shapes=scratch,
        compiler_params=pltpu.CompilerParams(
            collective_id=0, has_side_effects=True, vmem_limit_bytes=LIMIT
        ),
    )(*[a if a.size == 1 else pltpu.with_memory_space_constraint(a, pltpu.HBM) for a in arrays])
    return pl.pallas_call(
        finish,
        out_shape=(field, field, field),
        in_specs=[vmem] * 4,
        out_specs=(anywhere,) * 3,
        scratch_shapes=[pltpu.VMEM((SLAB, CY, CZ), f32), dma((3,))],
        compiler_params=pltpu.CompilerParams(vmem_limit_bytes=LIMIT),
    )(values, peak_in, corr_in, hit)


def solution(mesh):
    in_specs = (
        P("shot", "tx", "ty", None),
        P("shot", "tx", "ty", None),
        P("shot", "tx", "ty", None),
        P("shot", "tx", "ty", None),
        P(("tx", "ty"), "shot", None, None),
        P("shot", ("tx", "ty"), None),
        P("shot", None),
        P("shot"),
        P("shot", None, None),
        P("shot", None),
    )
    out_specs = (
        P("shot", "tx", "ty", None),
        P("shot", "tx", "ty", None),
        P(("tx", "ty"), "shot", None, None),
    )
    return jax.shard_map(
        on_device, mesh=mesh, in_specs=in_specs, out_specs=out_specs, check_vma=False
    )
```

```python
import functools

import jax
import jax.numpy as jnp
import ml_dtypes
import numpy as np
from jax import lax
from jax.experimental import pallas as pl
from jax.experimental.pallas import tpu as pltpu
from jax.sharding import PartitionSpec as P

SURFACE_DEPTH = 8
STENCIL_WEIGHTS = (-205.0 / 72.0, 8.0 / 5.0, -1.0 / 5.0, 8.0 / 315.0, -1.0 / 560.0)
STEP_RATIO = 0.1
MESH = pl.DeviceIdType.MESH
NS, NTX, NTY = 16, 4, 8
CX, CY, CZ = 32, 8, 256
ROWS = CX * CY
SLAB = 32
NREC = 128
YH = CX * 4
XH = 4 * CY
HALO = 2 * YH + 2 * XH
STEPS = 32766.0
TINY = 1e-34
DIRECT = 1
LATE = 6
LIMIT = 40 * 1024 * 1024


def stencil_constants():
    w = np.array(STENCIL_WEIGHTS)
    band = np.zeros(600)
    band[1:5] = w[1:]
    row = np.arange(ROWS)
    x, y = row // CY, row % CY
    dx, dy = np.abs(x[:, None] - x[None, :]), np.abs(y[:, None] - y[None, :])
    inner = band[dx] * (dy == 0) + band[dy] * (dx == 0) + 3.0 * w[0] * ((dx == 0) & (dy == 0))
    z = np.arange(CZ)
    depth = band[np.abs(z[:, None] - z[None, :])]
    pick = np.zeros((ROWS, ROWS))
    halo = np.zeros((ROWS, 2 * YH))
    for cx in range(CX):
        for q in range(4):
            pick[cx * 4 + q, cx * CY + CY - 4 + q] = 1.0
            pick[YH + cx * 4 + q, cx * CY + q] = 1.0
            for cy in range(CY):
                halo[cx * CY + cy, cx * 4 + q] = band[cy + 4 - q]
                halo[cx * CY + cy, YH + cx * 4 + q] = band[CY + q - cy]

    def parts(matrix):
        high = matrix.astype(np.float32).astype(ml_dtypes.bfloat16)
        low = (matrix - high.astype(np.float64)).astype(np.float32).astype(ml_dtypes.bfloat16)
        return [high, low]

    square = np.concatenate(parts(inner) + parts(depth) + parts(pick)[:1], axis=0)
    return square, np.concatenate(parts(halo), axis=0)


def each_partner(body, near=0):
    me = lax.axis_index("shot")
    turn_x = (me < NS // 2).astype(jnp.int32)
    turn_y = (lax.rem(me, 4) < 2).astype(jnp.int32)
    turn_x = turn_x + near * (1 - 2 * turn_x)
    turn_y = turn_y + near * (1 - 2 * turn_y)
    corner, step_x, step_y = 12 * turn_x + 3 * turn_y, 4 - 8 * turn_x, 1 - 2 * turn_y

    @pl.loop(0, 4)
    def _(i):
        @pl.loop(0, 4)
        def _(j):
            other = corner + step_x * i + step_y * j

            @pl.when(other != me)
            def _():
                body(other)


def mm(a, b):
    return jnp.dot(a, b, preferred_element_type=jnp.float32)


def kernel(
    f_prev, f_now, a_prev, a_now, velocity, aperture, source_cell, strength, receivers, traces,
    square_hbm, halo_hbm,
    prev, peak_in, corr_in, hit_out,
    now, lap, high, low, edge_f, edge, far, slab_b, slab, ids, cell_v, trace_v, square, halo_w,
    pick_send, halo, tables, wanted, wanted_by, blocks, arrived, speed, peak_send, corr_send,
    hit,
    smem_tables, source_s, strength_s,
    load_sem, edge_sem, far_send, far_recv, table_sem, id_sem, id_send, id_recv, halo_send, halo_recv, v_send, v_recv,
    c_send, c_recv, ready, go,
):
    me = lax.axis_index("shot")
    tx = lax.axis_index("tx")
    ty = lax.axis_index("ty")

    loads = [
        pltpu.make_async_copy(aperture.at[0], ids, load_sem.at[0]),
        pltpu.make_async_copy(f_now.at[0], now.at[0], load_sem.at[1]),
        pltpu.make_async_copy(a_now.at[0], now.at[1], load_sem.at[2]),
        pltpu.make_async_copy(square_hbm, square, load_sem.at[3]),
        pltpu.make_async_copy(velocity.at[0], slab_b, load_sem.at[4]),
        pltpu.make_async_copy(halo_hbm, halo_w, load_sem.at[5]),
        pltpu.make_async_copy(f_prev.at[0], prev.at[0], load_sem.at[6]),
        pltpu.make_async_copy(a_prev.at[0], prev.at[1], load_sem.at[7]),
        pltpu.make_async_copy(receivers.at[0], cell_v, load_sem.at[8]),
        pltpu.make_async_copy(traces, trace_v, load_sem.at[9]),
        pltpu.make_async_copy(source_cell, source_s, load_sem.at[10]),
        pltpu.make_async_copy(strength, strength_s, load_sem.at[11]),
    ]
    edge_loads = [
        pltpu.make_async_copy(now_hbm.at[0, 0:4], edge_f.at[field], edge_sem.at[field])
        for field, now_hbm in enumerate((f_now, a_now))
    ]

    direct = ty < DIRECT

    @pl.when((tx == 2) & jnp.logical_not(direct))
    def _():
        edge_loads[0].start()
        edge_loads[1].start()

    for n in (0, 1, 2, 4):
        loads[n].start()

    relayed = tx == 2
    home = tx + relayed.astype(jnp.int32)
    odd = lax.rem(tx, 2) == 1
    sides = [
        (ty < NTY - 1, "ty", ty + 1),
        (ty > 0, "ty", ty - 1),
        (tx < NTX - 1, "tx", tx + 1),
        (tx > 0, "tx", tx - 1),
    ]
    first = [ty < NTY - 1, None, tx == 1, tx == 1]

    barrier = pltpu.get_barrier_semaphore()

    mutual = ty >= LATE
    for n, says in ((2, first[2]), (3, first[3] | (relayed & mutual))):

        @pl.when(says)
        def _():
            pl.semaphore_signal(
                barrier, inc=1, device_id={"tx": sides[n][2]}, device_id_type=MESH
            )

    def answer_first(n):
        axis, other = sides[n][1:]
        pl.semaphore_signal(
            ready.at[(1, 0, 3, 2)[n]], inc=1, device_id={axis: other}, device_id_type=MESH
        )

    def far_copy(field):
        return pltpu.make_async_remote_copy(
            src_ref=(f_now, a_now)[field].at[0, 0:4],
            dst_ref=far.at[field],
            send_sem=far_send.at[field],
            recv_sem=far_recv.at[field],
            device_id={"tx": tx - 1},
            device_id_type=MESH,
        )

    @pl.when(relayed & direct)
    def _():
        pl.semaphore_wait(barrier, 1)
        far_copy(0).start()
        far_copy(1).start()
        answer_first(3)

    @pl.loop(1 - relayed.astype(jnp.int32), NS)
    def _(d):
        pl.semaphore_signal(
            barrier,
            inc=1,
            device_id={"shot": lax.rem(me + d, NS), "tx": home},
            device_id_type=MESH,
        )

    @pl.when(first[0])
    def _():
        pl.semaphore_signal(
            barrier, inc=1, device_id={"tx": home, "ty": ty + 1}, device_id_type=MESH
        )

    for n in (3, 5, 6, 7, 8, 9, 10, 11):
        loads[n].start()

    for present, start, size in (
        (ty > 0, 0, YH),
        (ty < NTY - 1, YH, YH),
        (tx > 0, 2 * YH, XH),
        (tx < NTX - 1, 2 * YH + XH, XH),
    ):

        @pl.when(jnp.logical_not(present))
        def _():
            halo[:, start : start + size, :] = jnp.zeros((2, size, CZ), jnp.bfloat16)

    def halo_copy(n, source=None):
        axis, other = sides[n][1], sides[n][2]
        start = (0, YH, 2 * YH, 2 * YH + XH)[n]
        size = YH if n < 2 else XH
        if source is None and n < 2:
            source = pick_send.at[n]
        elif source is None:
            source = high.at[:, pl.ds((CX - 4) * CY if n == 2 else 0, XH)]
        return pltpu.make_async_remote_copy(
            src_ref=source,
            dst_ref=halo.at[:, pl.ds(start, size)],
            send_sem=halo_send.at[n],
            recv_sem=halo_recv.at[n],
            device_id={axis: other},
            device_id_type=MESH,
        )

    def across():
        pl.semaphore_wait(barrier, 1)

        @pl.when(jnp.logical_not(mutual))
        def _():
            answer_first(3)

        halo_copy(3, edge).start()

    @pl.when(relayed & jnp.logical_not(direct))
    def _():
        edge_loads[0].wait()
        edge_loads[1].wait()
        edge[...] = edge_f[...].reshape(2, XH, CZ).astype(jnp.bfloat16)

    @pl.when(relayed & (ty >= DIRECT) & jnp.logical_not(mutual))
    def _():
        across()

    loads[1].wait()
    loads[2].wait()

    @pl.loop(0, 2)
    def _(field):
        u = now[field].reshape(ROWS, CZ)
        top = u.astype(jnp.bfloat16)
        high[field] = top
        low[field] = (u - top.astype(jnp.float32)).astype(jnp.bfloat16)

    loads[0].wait()
    row_l = lax.broadcasted_iota(jnp.int32, (CX, CX), 1)
    row_s = lax.broadcasted_iota(jnp.int32, (CX, CX), 0)
    ids_l = jnp.broadcast_to(ids[...], (CX, CX))
    ids_s = ids_l.T
    earlier = ((ids_s >> 5) == (ids_l >> 5)) & (row_s < row_l)
    rank = jnp.sum(earlier.astype(jnp.int32), axis=0, keepdims=True)
    slot = 2 * (ids[...] >> 5) + rank
    placed = jnp.broadcast_to(slot, (CX, CX)).T == row_l
    tables[0, :, 0:CX] = slot
    tables[1, :, 0:CX] = jnp.sum(jnp.where(placed, row_s, 0), axis=0, keepdims=True)
    wanted[me, :, 0:CX] = jnp.sum(jnp.where(placed, ids_s & (SLAB - 1), 0), axis=0, keepdims=True)
    table_copy = pltpu.make_async_copy(tables, smem_tables, table_sem)
    table_copy.start()

    loads[3].wait()

    @pl.loop(0, 2)
    def _(field):
        picked = mm(square[4 * ROWS : 5 * ROWS, :], high[field]).astype(jnp.bfloat16)
        pick_send[0, field] = picked[0:YH]
        pick_send[1, field] = picked[YH:]

    partners = NS - 1 + (ty > 0).astype(jnp.int32) + (tx == 0).astype(jnp.int32)
    partners = partners + ((tx == 1) & mutual).astype(jnp.int32)
    partners = partners + jnp.where(tx == 3, NS + (ty > 0).astype(jnp.int32), 0)

    @pl.when(jnp.logical_not(relayed))
    def _():
        pl.semaphore_wait(barrier, partners)

    @pl.when(tx == 3)
    def _():
        pl.semaphore_signal(go, inc=1, device_id={"tx": 2}, device_id_type=MESH)

    upper = me // 4 + lax.rem(me, 4) >= 2

    @pl.when(relayed & mutual & jnp.logical_not(upper))
    def _():
        across()

    @pl.when(relayed)
    def _():
        pl.semaphore_wait(go, 1)

    def id_copy(other):
        return pltpu.make_async_remote_copy(
            src_ref=wanted.at[me],
            dst_ref=wanted.at[me],
            send_sem=id_send,
            recv_sem=id_recv,
            device_id={"shot": other},
            device_id_type=MESH,
        )

    each_partner(lambda other: id_copy(other).start())

    @pl.when(relayed & mutual & upper)
    def _():
        across()

    @pl.when(ty > 0)
    def _():
        answer_first(1)

    @pl.when(tx == 0)
    def _():
        answer_first(2)

    @pl.when(jnp.logical_not(odd) | ((tx == 1) & mutual))
    def _():
        halo_copy(2).start()

    @pl.when(tx == 3)
    def _():
        halo_copy(3).start()

    @pl.when(ty > 0)
    def _():
        halo_copy(1).start()

    def answer(n):
        @pl.when(first[n])
        def _():
            pl.semaphore_wait(ready.at[n], 1)
            halo_copy(n).start()

    loads[4].wait()
    slab[...] = slab_b[...].astype(jnp.float32)

    def serve(shot):
        rows = [slab[wanted_by[shot, 0, 2 * me + k]] for k in range(2)]
        return jnp.concatenate(rows, axis=0).astype(jnp.bfloat16)

    def block_copy(owner, shot):
        return pltpu.make_async_remote_copy(
            src_ref=blocks.at[shot],
            dst_ref=arrived.at[owner],
            send_sem=v_send,
            recv_sem=v_recv.at[owner],
            device_id={"shot": shot},
            device_id_type=MESH,
        )

    @pl.loop(0, 2)
    def _(field):
        top, rest = high[field], low[field]
        lap[field] = (
            mm(square[0:ROWS, :], top)
            + mm(square[0:ROWS, :], rest)
            + mm(square[ROWS : 2 * ROWS, :], top)
            + mm(top, square[2 * ROWS : 3 * ROWS, :])
            + mm(rest, square[2 * ROWS : 3 * ROWS, :])
            + mm(top, square[3 * ROWS : 4 * ROWS, :])
        ).reshape(CX, CY, CZ)

    for load in loads[8:]:
        load.wait()
    row = lax.broadcasted_iota(jnp.int32, (ROWS, 1), 0)

    def local_row(along_x, along_y):
        inside = (along_x >= tx * CX) & (along_x < tx * CX + CX)
        inside = inside & (along_y >= ty * CY) & (along_y < ty * CY + CY)
        return jnp.where(inside, (along_x - tx * CX) * CY + along_y - ty * CY, -1)

    source_row = local_row(source_s[0, 0], source_s[0, 1])
    cell_row = local_row(cell_v[0:1, :], cell_v[1:2, :])
    injected = jnp.where(row == source_row, strength_s[0, 0], 0.0)
    recorded = jnp.sum(
        jnp.where(jnp.broadcast_to(row, (ROWS, NREC)) == cell_row, trace_v[...], 0.0),
        axis=1,
        keepdims=True,
    )
    surface = lax.broadcasted_iota(jnp.int32, (ROWS, CZ), 1) == SURFACE_DEPTH

    loads[5].wait()
    loads[6].wait()
    loads[7].wait()
    answer(0)

    all_but_one = pl.ds(0, NS - 1)
    pltpu.make_async_copy(wanted.at[all_but_one], wanted.at[all_but_one], id_recv).wait()
    id_local = pltpu.make_async_copy(wanted, wanted_by, id_sem)
    id_local.start()
    id_local.wait()

    @each_partner
    def _(shot):
        blocks[shot] = serve(shot)
        block_copy(me, shot).start()

    arrived[me] = serve(me)
    @pl.when(ty >= 5)
    def _():
        answer(3)

        @pl.when(jnp.logical_not(mutual))
        def _():
            answer(2)

    depth_l = lax.broadcasted_iota(jnp.int32, (CY, ROWS), 1)
    same_y = (depth_l & (CY - 1)) == lax.broadcasted_iota(jnp.int32, (CY, ROWS), 0)
    block_l = jnp.where(same_y, depth_l >> 3, -1)


    @pl.loop(0, NS)
    def _(shot):
        hits = [block_l == wanted_by[shot, 0, 2 * me + k] for k in range(2)]
        rows = pl.ds(pl.multiple_of(shot * 16, 16), 16)
        hit[rows, :] = jnp.where(jnp.concatenate(hits, axis=0), 1.0, 0.0)

    hit_out[...] = hit[...].T.astype(jnp.bfloat16)

    def halo_wait(n):
        @pl.when(sides[(1, 0, 3, 2)[n]][0])
        def _():
            halo_copy(n).wait_recv()

    halo_wait(0)
    halo_wait(1)
    @pl.loop(0, 2)
    def _(field):
        extra = jnp.where(field == 0, injected, recorded)
        layers = halo[field, 0 : 2 * YH]
        beyond = mm(halo_w[0:ROWS, :], layers) + mm(halo_w[ROWS:, :], layers)
        beyond = beyond + jnp.where(surface, jnp.broadcast_to(extra, (ROWS, CZ)), 0.0)
        lap[field] = lap[field] + beyond.reshape(CX, CY, CZ)
        prev[field] = 2.0 * now[field] - prev[field]

    @pl.when(ty < 5)
    def _():
        answer(3)
        answer(2)

    halo_wait(2)

    @pl.when((tx == 1) & direct)
    def _():
        far_copy(0).wait_recv()
        far_copy(1).wait_recv()

    @pl.when((tx < NTX - 1) & jnp.logical_not((tx == 1) & direct))
    def _():
        halo_copy(3).wait_recv()

    @pl.when(jnp.logical_not((tx == 1) & direct))
    def _():
        far[...] = halo[:, 2 * YH + XH :].astype(jnp.float32).reshape(2, 4, CY, CZ)

    @pl.loop(0, 2)
    def _(field):
        near = halo[field, 2 * YH : 2 * YH + XH].astype(jnp.float32).reshape(4, CY, CZ)
        for q in range(4):
            for x in range(4):
                if x <= q:
                    weight = STENCIL_WEIGHTS[x + 4 - q]
                    lap[field, x] = lap[field, x] + weight * near[q]
                if x >= q:
                    weight = STENCIL_WEIGHTS[4 + q - x]
                    lap[field, CX - 4 + x] = lap[field, CX - 4 + x] + weight * far[field, q]

    table_copy.wait()

    def corr_copies(owner):
        return [
            pltpu.make_async_remote_copy(
                src_ref=source.at[owner],
                dst_ref=target.at[me],
                send_sem=c_send.at[n],
                recv_sem=c_recv.at[n],
                device_id={"shot": owner},
                device_id_type=MESH,
            )
            for n, (source, target) in enumerate(((peak_send, peak_in), (corr_send, corr_in)))
        ]

    def contribute(owner):
        pair = arrived[owner].astype(jnp.float32)
        products = []
        for k in range(2):
            scaled = pair[k * CY : (k + 1) * CY] * STEP_RATIO
            courant = scaled * scaled
            speed[2 * owner + k] = courant
            r = smem_tables[1, 0, 2 * owner + k]
            products.append(
                (prev[0, r] + courant * lap[0, r]) * (prev[1, r] + courant * lap[1, r])
            )
        both = jnp.concatenate(products, axis=0)
        top = jnp.max(jnp.abs(both), axis=0, keepdims=True)
        top = jnp.maximum(jnp.maximum(top[:, : CZ // 2], top[:, CZ // 2 :]), TINY)
        scale = STEPS / top
        code = jnp.round(both * jnp.concatenate([scale, scale], axis=1))
        return top, code.astype(jnp.int32).astype(jnp.int16)

    peak_in[me], corr_in[me] = contribute(me)

    def one_owner(owner):
        block_copy(owner, me).wait_recv()
        peak_send[owner], corr_send[owner] = contribute(owner)
        for copy in corr_copies(owner):
            copy.start()

    each_partner(one_owner, near=((tx == 0) | (tx == 3)).astype(jnp.int32))

    @pl.loop(0, CX)
    def _(r):
        courant = speed[smem_tables[0, 0, r]]
        for field in range(2):
            prev[field, r] = prev[field, r] + courant * lap[field, r]

    def all_sent(ref, sem):
        pltpu.make_async_copy(ref.at[all_but_one], ref.at[all_but_one], sem).wait()

    all_sent(wanted, id_send)
    all_sent(blocks, v_send)
    for n in range(3):

        @pl.when(sides[n][0])
        def _():
            halo_copy(n).wait_send()

    @pl.when((tx > 0) & jnp.logical_not(relayed & direct))
    def _():
        halo_copy(3).wait_send()

    @pl.when(relayed & direct)
    def _():
        far_copy(0).wait_send()
        far_copy(1).wait_send()

    all_sent(peak_send, c_send.at[0])
    all_sent(corr_send, c_send.at[1])
    all_sent(peak_in, c_recv.at[0])
    all_sent(corr_in, c_recv.at[1])


def finish(values, peak_in, corr_in, hit, f_out, a_out, image_out, image, out_sem):
    outs = [
        pltpu.make_async_copy(values.at[0], f_out.at[0], out_sem.at[0]),
        pltpu.make_async_copy(values.at[1], a_out.at[0], out_sem.at[1]),
        pltpu.make_async_copy(image, image_out.at[0], out_sem.at[2]),
    ]
    outs[0].start()
    outs[1].start()
    peak = peak_in[...]
    peak = jnp.broadcast_to(jnp.concatenate([peak, peak], axis=2), (NS, 2 * CY, CZ))
    share = corr_in[...].astype(jnp.int32).astype(jnp.float32) * (1.0 / STEPS)
    rows = (share * peak).reshape(ROWS, CZ)
    top = rows.astype(jnp.bfloat16)
    rest = (rows - top.astype(jnp.float32)).astype(jnp.bfloat16)
    image[...] = (mm(hit[...], top) + mm(hit[...], rest)).reshape(SLAB, CY, CZ)
    outs[2].start()
    for out in outs:
        out.wait()


def on_device(*arrays):
    square, halo_w = stencil_constants()
    arrays = (
        *arrays[:7],
        arrays[7].reshape(1, 1),
        jnp.swapaxes(arrays[8], 1, 2),
        arrays[9],
        jnp.asarray(square),
        jnp.asarray(halo_w),
    )
    field = jax.ShapeDtypeStruct((1, CX, CY, CZ), jnp.float32)
    dma = pltpu.SemaphoreType.DMA
    bf, f32, i32 = jnp.bfloat16, jnp.float32, jnp.int32
    scratch = [
        pltpu.VMEM((2, CX, CY, CZ), f32),
        pltpu.VMEM((2, CX, CY, CZ), f32),
        pltpu.VMEM((2, ROWS, CZ), bf),
        pltpu.VMEM((2, ROWS, CZ), bf),
        pltpu.VMEM((2, 4, CY, CZ), f32),
        pltpu.VMEM((2, XH, CZ), bf),
        pltpu.VMEM((2, 4, CY, CZ), f32),
        pltpu.VMEM((SLAB, CY, CZ), bf),
        pltpu.VMEM((SLAB, CY, CZ), f32),
        pltpu.VMEM((1, CX), i32),
        pltpu.VMEM((2, NREC), i32),
        pltpu.VMEM((1, NREC), f32),
        pltpu.VMEM(square.shape, bf),
        pltpu.VMEM(halo_w.shape, bf),
        pltpu.VMEM((2, 2, YH, CZ), bf),
        pltpu.VMEM((2, HALO, CZ), bf),
        pltpu.VMEM((2, 1, 128), i32),
        pltpu.VMEM((NS, 1, 128), i32),
        pltpu.SMEM((NS, 1, 128), i32),
        pltpu.VMEM((NS, 2 * CY, CZ), bf),
        pltpu.VMEM((NS, 2 * CY, CZ), bf),
        pltpu.VMEM((2 * NS, CY, CZ), f32),
        pltpu.VMEM((NS, 1, CZ // 2), f32),
        pltpu.VMEM((NS, 2 * CY, CZ), jnp.int16),
        pltpu.VMEM((ROWS, ROWS), f32),
        pltpu.SMEM((2, 1, 128), i32),
        pltpu.SMEM((1, 2), i32),
        pltpu.SMEM((1, 1), f32),
        dma((12,)),
        dma((2,)),
        dma((2,)),
        dma((2,)),
        dma,
        dma,
        dma,
        dma,
        dma((4,)),
        dma((4,)),
        dma,
        dma((NS,)),
        dma((2,)),
        dma((2,)),
        pltpu.SemaphoreType.REGULAR((4,)),
        pltpu.SemaphoreType.REGULAR,
    ]
    anywhere = pl.BlockSpec(memory_space=pl.ANY)
    vmem = pl.BlockSpec(memory_space=pltpu.VMEM)
    values, peak_in, corr_in, hit = pl.pallas_call(
        kernel,
        out_shape=(
            jax.ShapeDtypeStruct((2, CX, CY, CZ), f32),
            jax.ShapeDtypeStruct((NS, 1, CZ // 2), f32),
            jax.ShapeDtypeStruct((NS, 2 * CY, CZ), jnp.int16),
            jax.ShapeDtypeStruct((ROWS, ROWS), bf),
        ),
        in_specs=[anywhere] * 12,
        out_specs=(vmem,) * 4,
        scratch_shapes=scratch,
        compiler_params=pltpu.CompilerParams(
            collective_id=0, has_side_effects=True, vmem_limit_bytes=LIMIT
        ),
    )(*[a if a.size == 1 else pltpu.with_memory_space_constraint(a, pltpu.HBM) for a in arrays])
    return pl.pallas_call(
        finish,
        out_shape=(field, field, field),
        in_specs=[vmem] * 4,
        out_specs=(anywhere,) * 3,
        scratch_shapes=[pltpu.VMEM((SLAB, CY, CZ), f32), dma((3,))],
        compiler_params=pltpu.CompilerParams(vmem_limit_bytes=LIMIT),
    )(values, peak_in, corr_in, hit)


def solution(mesh):
    in_specs = (
        P("shot", "tx", "ty", None),
        P("shot", "tx", "ty", None),
        P("shot", "tx", "ty", None),
        P("shot", "tx", "ty", None),
        P(("tx", "ty"), "shot", None, None),
        P("shot", ("tx", "ty"), None),
        P("shot", None),
        P("shot"),
        P("shot", None, None),
        P("shot", None),
    )
    out_specs = (
        P("shot", "tx", "ty", None),
        P("shot", "tx", "ty", None),
        P(("tx", "ty"), "shot", None, None),
    )
    return jax.shard_map(
        on_device, mesh=mesh, in_specs=in_specs, out_specs=out_specs, check_vma=False
    )
```

```python
import functools

import jax
import jax.numpy as jnp
import ml_dtypes
import numpy as np
from jax import lax
from jax.experimental import pallas as pl
from jax.experimental.pallas import tpu as pltpu
from jax.sharding import PartitionSpec as P

SURFACE_DEPTH = 8
STENCIL_WEIGHTS = (-205.0 / 72.0, 8.0 / 5.0, -1.0 / 5.0, 8.0 / 315.0, -1.0 / 560.0)
STEP_RATIO = 0.1
MESH = pl.DeviceIdType.MESH
NS, NTX, NTY = 16, 4, 8
CX, CY, CZ = 32, 8, 256
ROWS = CX * CY
SLAB = 32
NREC = 128
YH = CX * 4
XH = 4 * CY
HALO = 2 * YH + 2 * XH
STEPS = 32766.0
TINY = 1e-34
DIRECT = 1
LATE = 6
LIMIT = 40 * 1024 * 1024


def stencil_constants():
    w = np.array(STENCIL_WEIGHTS)
    band = np.zeros(600)
    band[1:5] = w[1:]
    row = np.arange(ROWS)
    x, y = row // CY, row % CY
    dx, dy = np.abs(x[:, None] - x[None, :]), np.abs(y[:, None] - y[None, :])
    inner = band[dx] * (dy == 0) + band[dy] * (dx == 0) + 3.0 * w[0] * ((dx == 0) & (dy == 0))
    z = np.arange(CZ)
    depth = band[np.abs(z[:, None] - z[None, :])]
    pick = np.zeros((ROWS, ROWS))
    halo = np.zeros((ROWS, 2 * YH))
    for cx in range(CX):
        for q in range(4):
            pick[cx * 4 + q, cx * CY + CY - 4 + q] = 1.0
            pick[YH + cx * 4 + q, cx * CY + q] = 1.0
            for cy in range(CY):
                halo[cx * CY + cy, cx * 4 + q] = band[cy + 4 - q]
                halo[cx * CY + cy, YH + cx * 4 + q] = band[CY + q - cy]

    def parts(matrix):
        high = matrix.astype(np.float32).astype(ml_dtypes.bfloat16)
        low = (matrix - high.astype(np.float64)).astype(np.float32).astype(ml_dtypes.bfloat16)
        return [high, low]

    square = np.concatenate(parts(inner) + parts(depth) + parts(pick)[:1], axis=0)
    return square, np.concatenate(parts(halo), axis=0)


def each_partner(body, near=0, row=None):
    me = lax.axis_index("shot")
    turn_x = (me < NS // 2).astype(jnp.int32)
    turn_y = (lax.rem(me, 4) < 2).astype(jnp.int32)
    turn_x = turn_x + near * (1 - 2 * turn_x)
    turn_y = turn_y + near * (1 - 2 * turn_y)
    corner, step_x, step_y = 12 * turn_x + 3 * turn_y, 4 - 8 * turn_x, 1 - 2 * turn_y

    @pl.loop(0, 4)
    def _(i):
        if row is not None:
            row(3 * turn_x + (1 - 2 * turn_x) * i)

        @pl.loop(0, 4)
        def _(j):
            other = corner + step_x * i + step_y * j

            @pl.when(other != me)
            def _():
                body(other)


def mm(a, b):
    return jnp.dot(a, b, preferred_element_type=jnp.float32)


def kernel(
    f_prev, f_now, a_prev, a_now, velocity, aperture, source_cell, strength, receivers, traces,
    square_hbm, halo_hbm,
    prev, peak_in, corr_in, hit_out,
    now, lap, high, low, edge_f, edge, far, slab_b, slab, ids, cell_v, trace_v, square, halo_w,
    pick_send, halo, tables, wanted, wanted_by, blocks, arrived, speed, peak_send, corr_send,
    hit,
    smem_tables, source_s, strength_s,
    load_sem, edge_sem, far_sem, table_sem, id_sem, id_send, id_recv, halo_send, halo_recv, v_send, v_recv,
    c_send, c_recv, ready, go,
):
    me = lax.axis_index("shot")
    tx = lax.axis_index("tx")
    ty = lax.axis_index("ty")

    loads = [
        pltpu.make_async_copy(aperture.at[0], ids, load_sem.at[0]),
        pltpu.make_async_copy(f_now.at[0], now.at[0], load_sem.at[1]),
        pltpu.make_async_copy(a_now.at[0], now.at[1], load_sem.at[1]),
        pltpu.make_async_copy(square_hbm, square, load_sem.at[3]),
        pltpu.make_async_copy(velocity.at[0], slab_b, load_sem.at[4]),
        pltpu.make_async_copy(halo_hbm, halo_w, load_sem.at[5]),
        pltpu.make_async_copy(f_prev.at[0], prev.at[0], load_sem.at[6]),
        pltpu.make_async_copy(a_prev.at[0], prev.at[1], load_sem.at[6]),
        pltpu.make_async_copy(receivers.at[0], cell_v, load_sem.at[8]),
        pltpu.make_async_copy(traces, trace_v, load_sem.at[9]),
        pltpu.make_async_copy(source_cell, source_s, load_sem.at[2]),
        pltpu.make_async_copy(strength, strength_s, load_sem.at[7]),
    ]
    edge_loads = [
        pltpu.make_async_copy(now_hbm.at[0, 0:4], edge_f.at[field], edge_sem)
        for field, now_hbm in enumerate((f_now, a_now))
    ]

    direct = ty < DIRECT

    @pl.when((tx == 2) & jnp.logical_not(direct))
    def _():
        edge_loads[0].start()
        edge_loads[1].start()

    for n in (0, 1, 2, 4):
        loads[n].start()

    relayed = tx == 2
    home = tx + relayed.astype(jnp.int32)
    odd = lax.rem(tx, 2) == 1
    sides = [
        (ty < NTY - 1, "ty", ty + 1),
        (ty > 0, "ty", ty - 1),
        (tx < NTX - 1, "tx", tx + 1),
        (tx > 0, "tx", tx - 1),
    ]
    first = [ty < NTY - 1, None, tx == 1, tx == 1]

    barrier = pltpu.get_barrier_semaphore()

    mutual = ty >= LATE
    for n, says in ((2, first[2]), (3, first[3] | (relayed & mutual))):

        @pl.when(says)
        def _():
            pl.semaphore_signal(
                barrier, inc=1, device_id={"tx": sides[n][2]}, device_id_type=MESH
            )

    def answer_first(n):
        axis, other = sides[n][1:]
        pl.semaphore_signal(
            ready.at[(1, 0, 3, 2)[n]], inc=1, device_id={axis: other}, device_id_type=MESH
        )

    def far_copy(field, x):
        return pltpu.make_async_remote_copy(
            src_ref=(f_now, a_now)[field].at[0, x],
            dst_ref=far.at[field, x],
            send_sem=far_sem.at[0],
            recv_sem=far_sem.at[1],
            device_id={"tx": tx - 1},
            device_id_type=MESH,
        )

    @pl.when(relayed & direct)
    def _():
        pl.semaphore_wait(barrier, 1)
        for x in range(4):
            far_copy(0, x).start()
            far_copy(1, x).start()
        answer_first(3)

    @pl.loop(1 - relayed.astype(jnp.int32), NS)
    def _(d):
        pl.semaphore_signal(
            barrier,
            inc=1,
            device_id={"shot": lax.rem(me + d, NS), "tx": home},
            device_id_type=MESH,
        )

    @pl.when(first[0])
    def _():
        pl.semaphore_signal(
            barrier, inc=1, device_id={"tx": home, "ty": ty + 1}, device_id_type=MESH
        )

    for n in (3, 5, 6, 7, 8, 9, 10, 11):
        loads[n].start()

    for present, start, size in (
        (ty > 0, 0, YH),
        (ty < NTY - 1, YH, YH),
        (tx > 0, 2 * YH, XH),
        (tx < NTX - 1, 2 * YH + XH, XH),
    ):

        @pl.when(jnp.logical_not(present))
        def _():
            halo[:, start : start + size, :] = jnp.zeros((2, size, CZ), jnp.bfloat16)

    def halo_copy(n, source=None):
        axis, other = sides[n][1], sides[n][2]
        start = (0, YH, 2 * YH, 2 * YH + XH)[n]
        size = YH if n < 2 else XH
        if source is None and n < 2:
            source = pick_send.at[n]
        elif source is None:
            source = high.at[:, pl.ds((CX - 4) * CY if n == 2 else 0, XH)]
        return pltpu.make_async_remote_copy(
            src_ref=source,
            dst_ref=halo.at[:, pl.ds(start, size)],
            send_sem=halo_send.at[n],
            recv_sem=halo_recv.at[n],
            device_id={axis: other},
            device_id_type=MESH,
        )

    def across():
        pl.semaphore_wait(barrier, 1)

        @pl.when(jnp.logical_not(mutual))
        def _():
            answer_first(3)

        halo_copy(3, edge).start()

    @pl.when(relayed & jnp.logical_not(direct))
    def _():
        pltpu.make_async_copy(edge_f, edge_f, edge_sem).wait()
        edge[...] = edge_f[...].reshape(2, XH, CZ).astype(jnp.bfloat16)

    @pl.when(relayed & (ty >= DIRECT) & jnp.logical_not(mutual))
    def _():
        across()

    pltpu.make_async_copy(now, now, load_sem.at[1]).wait()

    @pl.loop(0, 2)
    def _(field):
        u = now[field].reshape(ROWS, CZ)
        top = u.astype(jnp.bfloat16)
        high[field] = top
        low[field] = (u - top.astype(jnp.float32)).astype(jnp.bfloat16)

    loads[0].wait()
    row_l = lax.broadcasted_iota(jnp.int32, (CX, CX), 1)
    row_s = lax.broadcasted_iota(jnp.int32, (CX, CX), 0)
    ids_l = jnp.broadcast_to(ids[...], (CX, CX))
    ids_s = ids_l.T
    earlier = ((ids_s >> 5) == (ids_l >> 5)) & (row_s < row_l)
    rank = jnp.sum(earlier.astype(jnp.int32), axis=0, keepdims=True)
    slot = 2 * (ids[...] >> 5) + rank
    placed = jnp.broadcast_to(slot, (CX, CX)).T == row_l
    tables[0, :, 0:CX] = slot
    tables[1, :, 0:CX] = jnp.sum(jnp.where(placed, row_s, 0), axis=0, keepdims=True)
    wanted[me, :, 0:CX] = jnp.sum(jnp.where(placed, ids_s & (SLAB - 1), 0), axis=0, keepdims=True)
    table_copy = pltpu.make_async_copy(tables, smem_tables, table_sem)
    table_copy.start()

    loads[3].wait()

    @pl.loop(0, 2)
    def _(field):
        picked = mm(square[4 * ROWS : 5 * ROWS, :], high[field]).astype(jnp.bfloat16)
        pick_send[0, field] = picked[0:YH]
        pick_send[1, field] = picked[YH:]

    partners = NS - 1 + (ty > 0).astype(jnp.int32) + (tx == 0).astype(jnp.int32)
    partners = partners + ((tx == 1) & mutual).astype(jnp.int32)
    partners = partners + jnp.where(tx == 3, NS + (ty > 0).astype(jnp.int32), 0)

    @pl.when(jnp.logical_not(relayed))
    def _():
        pl.semaphore_wait(barrier, partners)

    @pl.when(tx == 3)
    def _():
        pl.semaphore_signal(go, inc=1, device_id={"tx": 2}, device_id_type=MESH)

    upper = me // 4 + lax.rem(me, 4) >= 2

    @pl.when(relayed & mutual & jnp.logical_not(upper))
    def _():
        across()

    @pl.when(relayed)
    def _():
        pl.semaphore_wait(go, 1)

    def id_copy(other):
        return pltpu.make_async_remote_copy(
            src_ref=wanted.at[me],
            dst_ref=wanted.at[me],
            send_sem=id_send,
            recv_sem=id_recv,
            device_id={"shot": other},
            device_id_type=MESH,
        )

    each_partner(lambda other: id_copy(other).start())

    @pl.when(relayed & mutual & upper)
    def _():
        across()

    @pl.when(ty > 0)
    def _():
        answer_first(1)

    @pl.when(tx == 0)
    def _():
        answer_first(2)

    @pl.when(jnp.logical_not(odd) | ((tx == 1) & mutual))
    def _():
        halo_copy(2).start()

    @pl.when(tx == 3)
    def _():
        halo_copy(3).start()

    @pl.when(ty > 0)
    def _():
        halo_copy(1).start()

    def answer(n):
        @pl.when(first[n])
        def _():
            pl.semaphore_wait(ready.at[n], 1)
            halo_copy(n).start()

    loads[4].wait()
    slab[...] = slab_b[...].astype(jnp.float32)

    def serve(shot):
        rows = [slab[wanted_by[shot, 0, 2 * me + k]] for k in range(2)]
        return jnp.concatenate(rows, axis=0).astype(jnp.bfloat16)

    def block_copy(owner, shot):
        return pltpu.make_async_remote_copy(
            src_ref=blocks.at[shot],
            dst_ref=arrived.at[owner],
            send_sem=v_send,
            recv_sem=v_recv.at[me // 4],
            device_id={"shot": shot},
            device_id_type=MESH,
        )

    @pl.loop(0, 2)
    def _(field):
        top, rest = high[field], low[field]
        lap[field] = (
            mm(square[0:ROWS, :], top)
            + mm(square[0:ROWS, :], rest)
            + mm(square[ROWS : 2 * ROWS, :], top)
            + mm(top, square[2 * ROWS : 3 * ROWS, :])
            + mm(rest, square[2 * ROWS : 3 * ROWS, :])
            + mm(top, square[3 * ROWS : 4 * ROWS, :])
        ).reshape(CX, CY, CZ)

    for load in loads[8:]:
        load.wait()
    row = lax.broadcasted_iota(jnp.int32, (ROWS, 1), 0)

    def local_row(along_x, along_y):
        inside = (along_x >= tx * CX) & (along_x < tx * CX + CX)
        inside = inside & (along_y >= ty * CY) & (along_y < ty * CY + CY)
        return jnp.where(inside, (along_x - tx * CX) * CY + along_y - ty * CY, -1)

    source_row = local_row(source_s[0, 0], source_s[0, 1])
    cell_row = local_row(cell_v[0:1, :], cell_v[1:2, :])
    injected = jnp.where(row == source_row, strength_s[0, 0], 0.0)
    recorded = jnp.sum(
        jnp.where(jnp.broadcast_to(row, (ROWS, NREC)) == cell_row, trace_v[...], 0.0),
        axis=1,
        keepdims=True,
    )
    surface = lax.broadcasted_iota(jnp.int32, (ROWS, CZ), 1) == SURFACE_DEPTH

    loads[5].wait()
    pltpu.make_async_copy(prev, prev, load_sem.at[6]).wait()
    answer(0)

    all_but_one = pl.ds(0, NS - 1)
    pltpu.make_async_copy(wanted.at[all_but_one], wanted.at[all_but_one], id_recv).wait()
    id_local = pltpu.make_async_copy(wanted, wanted_by, id_sem)
    id_local.start()
    id_local.wait()

    @each_partner
    def _(shot):
        blocks[shot] = serve(shot)
        block_copy(me, shot).start()

    arrived[me] = serve(me)
    @pl.when(ty >= 5)
    def _():
        answer(3)

        @pl.when(jnp.logical_not(mutual))
        def _():
            answer(2)

    depth_l = lax.broadcasted_iota(jnp.int32, (CY, ROWS), 1)
    same_y = (depth_l & (CY - 1)) == lax.broadcasted_iota(jnp.int32, (CY, ROWS), 0)
    block_l = jnp.where(same_y, depth_l >> 3, -1)


    @pl.loop(0, NS)
    def _(shot):
        hits = [block_l == wanted_by[shot, 0, 2 * me + k] for k in range(2)]
        rows = pl.ds(pl.multiple_of(shot * 16, 16), 16)
        hit[rows, :] = jnp.where(jnp.concatenate(hits, axis=0), 1.0, 0.0)

    hit_out[...] = hit[...].T.astype(jnp.bfloat16)

    def halo_wait(n):
        @pl.when(sides[(1, 0, 3, 2)[n]][0])
        def _():
            halo_copy(n).wait_recv()

    halo_wait(0)
    halo_wait(1)
    @pl.loop(0, 2)
    def _(field):
        extra = jnp.where(field == 0, injected, recorded)
        layers = halo[field, 0 : 2 * YH]
        beyond = mm(halo_w[0:ROWS, :], layers) + mm(halo_w[ROWS:, :], layers)
        beyond = beyond + jnp.where(surface, jnp.broadcast_to(extra, (ROWS, CZ)), 0.0)
        lap[field] = lap[field] + beyond.reshape(CX, CY, CZ)
        prev[field] = 2.0 * now[field] - prev[field]

    @pl.when(ty < 5)
    def _():
        answer(3)
        answer(2)

    halo_wait(2)

    @pl.when((tx == 1) & direct)
    def _():
        pltpu.make_async_copy(far, far, far_sem.at[1]).wait()

    @pl.when((tx < NTX - 1) & jnp.logical_not((tx == 1) & direct))
    def _():
        halo_copy(3).wait_recv()

    @pl.when(jnp.logical_not((tx == 1) & direct))
    def _():
        far[...] = halo[:, 2 * YH + XH :].astype(jnp.float32).reshape(2, 4, CY, CZ)

    @pl.loop(0, 2)
    def _(field):
        near = halo[field, 2 * YH : 2 * YH + XH].astype(jnp.float32).reshape(4, CY, CZ)
        for q in range(4):
            for x in range(4):
                if x <= q:
                    weight = STENCIL_WEIGHTS[x + 4 - q]
                    lap[field, x] = lap[field, x] + weight * near[q]
                if x >= q:
                    weight = STENCIL_WEIGHTS[4 + q - x]
                    lap[field, CX - 4 + x] = lap[field, CX - 4 + x] + weight * far[field, q]

    table_copy.wait()

    def corr_copies(owner):
        return [
            pltpu.make_async_remote_copy(
                src_ref=source.at[owner],
                dst_ref=target.at[me],
                send_sem=c_send.at[n],
                recv_sem=c_recv.at[n],
                device_id={"shot": owner},
                device_id_type=MESH,
            )
            for n, (source, target) in enumerate(((peak_send, peak_in), (corr_send, corr_in)))
        ]

    def contribute(owner):
        pair = arrived[owner].astype(jnp.float32)
        products = []
        for k in range(2):
            scaled = pair[k * CY : (k + 1) * CY] * STEP_RATIO
            courant = scaled * scaled
            speed[2 * owner + k] = courant
            r = smem_tables[1, 0, 2 * owner + k]
            products.append(
                (prev[0, r] + courant * lap[0, r]) * (prev[1, r] + courant * lap[1, r])
            )
        both = jnp.concatenate(products, axis=0)
        top = jnp.max(jnp.abs(both), axis=0, keepdims=True)
        top = jnp.maximum(jnp.maximum(top[:, : CZ // 2], top[:, CZ // 2 :]), TINY)
        scale = STEPS / top
        code = jnp.round(both * jnp.concatenate([scale, scale], axis=1))
        return top, code.astype(jnp.int32).astype(jnp.int16)

    peak_in[me], corr_in[me] = contribute(me)

    def one_owner(owner):
        peak_send[owner], corr_send[owner] = contribute(owner)
        for copy in corr_copies(owner):
            copy.start()

    def row_of_blocks(x):
        for mine, count in ((x == me // 4, 3), (x != me // 4, 4)):

            @pl.when(mine)
            def _():
                four = arrived.at[pl.ds(4 * x, count)]
                pltpu.make_async_copy(four, four, v_recv.at[x]).wait()

    each_partner(one_owner, ((tx == 0) | (tx == 3)).astype(jnp.int32), row_of_blocks)

    @pl.loop(0, CX)
    def _(r):
        courant = speed[smem_tables[0, 0, r]]
        for field in range(2):
            prev[field, r] = prev[field, r] + courant * lap[field, r]

    def all_sent(ref, sem):
        pltpu.make_async_copy(ref.at[all_but_one], ref.at[all_but_one], sem).wait()

    all_sent(wanted, id_send)
    all_sent(blocks, v_send)
    for n in range(3):

        @pl.when(sides[n][0])
        def _():
            halo_copy(n).wait_send()

    @pl.when((tx > 0) & jnp.logical_not(relayed & direct))
    def _():
        halo_copy(3).wait_send()

    @pl.when(relayed & direct)
    def _():
        pltpu.make_async_copy(far, far, far_sem.at[0]).wait()

    all_sent(peak_send, c_send.at[0])
    all_sent(corr_send, c_send.at[1])
    all_sent(peak_in, c_recv.at[0])
    all_sent(corr_in, c_recv.at[1])


def finish(values, peak_in, corr_in, hit, f_out, a_out, image_out, image, out_sem):
    outs = [
        pltpu.make_async_copy(values.at[0], f_out.at[0], out_sem.at[0]),
        pltpu.make_async_copy(values.at[1], a_out.at[0], out_sem.at[1]),
        pltpu.make_async_copy(image, image_out.at[0], out_sem.at[2]),
    ]
    outs[0].start()
    outs[1].start()
    peak = peak_in[...]
    peak = jnp.broadcast_to(jnp.concatenate([peak, peak], axis=2), (NS, 2 * CY, CZ))
    share = corr_in[...].astype(jnp.int32).astype(jnp.float32) * (1.0 / STEPS)
    rows = (share * peak).reshape(ROWS, CZ)
    top = rows.astype(jnp.bfloat16)
    rest = (rows - top.astype(jnp.float32)).astype(jnp.bfloat16)
    image[...] = (mm(hit[...], top) + mm(hit[...], rest)).reshape(SLAB, CY, CZ)
    outs[2].start()
    for out in outs:
        out.wait()


def on_device(*arrays):
    square, halo_w = stencil_constants()
    arrays = (
        *arrays[:7],
        arrays[7].reshape(1, 1),
        jnp.swapaxes(arrays[8], 1, 2),
        arrays[9],
        jnp.asarray(square),
        jnp.asarray(halo_w),
    )
    field = jax.ShapeDtypeStruct((1, CX, CY, CZ), jnp.float32)
    dma = pltpu.SemaphoreType.DMA
    bf, f32, i32 = jnp.bfloat16, jnp.float32, jnp.int32
    scratch = [
        pltpu.VMEM((2, CX, CY, CZ), f32),
        pltpu.VMEM((2, CX, CY, CZ), f32),
        pltpu.VMEM((2, ROWS, CZ), bf),
        pltpu.VMEM((2, ROWS, CZ), bf),
        pltpu.VMEM((2, 4, CY, CZ), f32),
        pltpu.VMEM((2, XH, CZ), bf),
        pltpu.VMEM((2, 4, CY, CZ), f32),
        pltpu.VMEM((SLAB, CY, CZ), bf),
        pltpu.VMEM((SLAB, CY, CZ), f32),
        pltpu.VMEM((1, CX), i32),
        pltpu.VMEM((2, NREC), i32),
        pltpu.VMEM((1, NREC), f32),
        pltpu.VMEM(square.shape, bf),
        pltpu.VMEM(halo_w.shape, bf),
        pltpu.VMEM((2, 2, YH, CZ), bf),
        pltpu.VMEM((2, HALO, CZ), bf),
        pltpu.VMEM((2, 1, 128), i32),
        pltpu.VMEM((NS, 1, 128), i32),
        pltpu.SMEM((NS, 1, 128), i32),
        pltpu.VMEM((NS, 2 * CY, CZ), bf),
        pltpu.VMEM((NS, 2 * CY, CZ), bf),
        pltpu.VMEM((2 * NS, CY, CZ), f32),
        pltpu.VMEM((NS, 1, CZ // 2), f32),
        pltpu.VMEM((NS, 2 * CY, CZ), jnp.int16),
        pltpu.VMEM((ROWS, ROWS), f32),
        pltpu.SMEM((2, 1, 128), i32),
        pltpu.SMEM((1, 2), i32),
        pltpu.SMEM((1, 1), f32),
        dma((10,)),
        dma,
        dma((2,)),
        dma,
        dma,
        dma,
        dma,
        dma((4,)),
        dma((4,)),
        dma,
        dma((4,)),
        dma((2,)),
        dma((2,)),
        pltpu.SemaphoreType.REGULAR((4,)),
        pltpu.SemaphoreType.REGULAR,
    ]
    anywhere = pl.BlockSpec(memory_space=pl.ANY)
    vmem = pl.BlockSpec(memory_space=pltpu.VMEM)
    values, peak_in, corr_in, hit = pl.pallas_call(
        kernel,
        out_shape=(
            jax.ShapeDtypeStruct((2, CX, CY, CZ), f32),
            jax.ShapeDtypeStruct((NS, 1, CZ // 2), f32),
            jax.ShapeDtypeStruct((NS, 2 * CY, CZ), jnp.int16),
            jax.ShapeDtypeStruct((ROWS, ROWS), bf),
        ),
        in_specs=[anywhere] * 12,
        out_specs=(vmem,) * 4,
        scratch_shapes=scratch,
        compiler_params=pltpu.CompilerParams(
            collective_id=0, has_side_effects=True, vmem_limit_bytes=LIMIT
        ),
    )(*[a if a.size == 1 else pltpu.with_memory_space_constraint(a, pltpu.HBM) for a in arrays])
    return pl.pallas_call(
        finish,
        out_shape=(field, field, field),
        in_specs=[vmem] * 4,
        out_specs=(anywhere,) * 3,
        scratch_shapes=[pltpu.VMEM((SLAB, CY, CZ), f32), dma((3,))],
        compiler_params=pltpu.CompilerParams(vmem_limit_bytes=LIMIT),
    )(values, peak_in, corr_in, hit)


def solution(mesh):
    in_specs = (
        P("shot", "tx", "ty", None),
        P("shot", "tx", "ty", None),
        P("shot", "tx", "ty", None),
        P("shot", "tx", "ty", None),
        P(("tx", "ty"), "shot", None, None),
        P("shot", ("tx", "ty"), None),
        P("shot", None),
        P("shot"),
        P("shot", None, None),
        P("shot", None),
    )
    out_specs = (
        P("shot", "tx", "ty", None),
        P("shot", "tx", "ty", None),
        P(("tx", "ty"), "shot", None, None),
    )
    return jax.shard_map(
        on_device, mesh=mesh, in_specs=in_specs, out_specs=out_specs, check_vma=False
    )
```

```python
import functools

import jax
import jax.numpy as jnp
import ml_dtypes
import numpy as np
from jax import lax
from jax.experimental import pallas as pl
from jax.experimental.pallas import tpu as pltpu
from jax.sharding import PartitionSpec as P

SURFACE_DEPTH = 8
STENCIL_WEIGHTS = (-205.0 / 72.0, 8.0 / 5.0, -1.0 / 5.0, 8.0 / 315.0, -1.0 / 560.0)
STEP_RATIO = 0.1
MESH = pl.DeviceIdType.MESH
NS, NTX, NTY = 16, 4, 8
CX, CY, CZ = 32, 8, 256
ROWS = CX * CY
SLAB = 32
NREC = 128
YH = CX * 4
XH = 4 * CY
HALO = 2 * YH + 2 * XH
STEPS = 32766.0
TINY = 1e-34
DIRECT = 1
LATE = 6
LIMIT = 40 * 1024 * 1024


def stencil_constants():
    w = np.array(STENCIL_WEIGHTS)
    band = np.zeros(600)
    band[1:5] = w[1:]
    row = np.arange(ROWS)
    x, y = row // CY, row % CY
    dx, dy = np.abs(x[:, None] - x[None, :]), np.abs(y[:, None] - y[None, :])
    inner = band[dx] * (dy == 0) + band[dy] * (dx == 0) + 3.0 * w[0] * ((dx == 0) & (dy == 0))
    z = np.arange(CZ)
    depth = band[np.abs(z[:, None] - z[None, :])]
    pick = np.zeros((ROWS, ROWS))
    halo = np.zeros((ROWS, 2 * YH))
    for cx in range(CX):
        for q in range(4):
            pick[cx * 4 + q, cx * CY + CY - 4 + q] = 1.0
            pick[YH + cx * 4 + q, cx * CY + q] = 1.0
            for cy in range(CY):
                halo[cx * CY + cy, cx * 4 + q] = band[cy + 4 - q]
                halo[cx * CY + cy, YH + cx * 4 + q] = band[CY + q - cy]

    def parts(matrix):
        high = matrix.astype(np.float32).astype(ml_dtypes.bfloat16)
        low = (matrix - high.astype(np.float64)).astype(np.float32).astype(ml_dtypes.bfloat16)
        return [high, low]

    square = np.concatenate(parts(inner) + parts(depth) + parts(pick)[:1], axis=0)
    return square, np.concatenate(parts(halo), axis=0)


def each_partner(body, near=0, row=None, up=0):
    me = lax.axis_index("shot")
    turn_x = (me < NS // 2).astype(jnp.int32)
    turn_y = (lax.rem(me, 4) < 2).astype(jnp.int32)
    turn_x = turn_x + near * (1 - 2 * turn_x)
    turn_y = turn_y + near * (1 - 2 * turn_y)
    turn_x, turn_y = turn_x * (1 - up), turn_y * (1 - up)
    corner, step_x, step_y = 12 * turn_x + 3 * turn_y, 4 - 8 * turn_x, 1 - 2 * turn_y

    @pl.loop(0, 4)
    def _(i):
        if row is not None:
            row(3 * turn_x + (1 - 2 * turn_x) * i)

        @pl.loop(0, 4)
        def _(j):
            other = corner + step_x * i + step_y * j

            @pl.when(other != me)
            def _():
                body(other)


def mm(a, b):
    return jnp.dot(a, b, preferred_element_type=jnp.float32)


def kernel(
    f_prev, f_now, a_prev, a_now, velocity, aperture, source_cell, strength, receivers, traces,
    square_hbm, halo_hbm,
    prev, peak_in, corr_in, hit_out,
    now, lap, high, low, edge_f, edge, far, slab_b, slab, ids, cell_v, trace_v, square, halo_w,
    pick_send, halo, tables, wanted, wanted_by, blocks, arrived, speed, peak_send, corr_send,
    hit,
    smem_tables, source_s, strength_s,
    load_sem, edge_sem, far_sem, table_sem, id_sem, id_send, id_recv, halo_send, halo_recv, v_send, v_recv,
    c_send, c_recv, ready, go,
):
    me = lax.axis_index("shot")
    tx = lax.axis_index("tx")
    ty = lax.axis_index("ty")

    loads = [
        pltpu.make_async_copy(aperture.at[0], ids, load_sem.at[0]),
        pltpu.make_async_copy(f_now.at[0], now.at[0], load_sem.at[1]),
        pltpu.make_async_copy(a_now.at[0], now.at[1], load_sem.at[1]),
        pltpu.make_async_copy(square_hbm, square, load_sem.at[3]),
        pltpu.make_async_copy(velocity.at[0], slab_b, load_sem.at[4]),
        pltpu.make_async_copy(halo_hbm, halo_w, load_sem.at[5]),
        pltpu.make_async_copy(f_prev.at[0], prev.at[0], load_sem.at[6]),
        pltpu.make_async_copy(a_prev.at[0], prev.at[1], load_sem.at[6]),
        pltpu.make_async_copy(receivers.at[0], cell_v, load_sem.at[8]),
        pltpu.make_async_copy(traces, trace_v, load_sem.at[9]),
        pltpu.make_async_copy(source_cell, source_s, load_sem.at[2]),
        pltpu.make_async_copy(strength, strength_s, load_sem.at[7]),
    ]
    edge_loads = [
        pltpu.make_async_copy(now_hbm.at[0, 0:4], edge_f.at[field], edge_sem)
        for field, now_hbm in enumerate((f_now, a_now))
    ]

    direct = ty < DIRECT

    @pl.when((tx == 2) & jnp.logical_not(direct))
    def _():
        edge_loads[0].start()
        edge_loads[1].start()

    for n in (0, 1, 2, 4):
        loads[n].start()

    relayed = tx == 2
    home = tx + relayed.astype(jnp.int32)
    odd = lax.rem(tx, 2) == 1
    sides = [
        (ty < NTY - 1, "ty", ty + 1),
        (ty > 0, "ty", ty - 1),
        (tx < NTX - 1, "tx", tx + 1),
        (tx > 0, "tx", tx - 1),
    ]
    first = [ty < NTY - 1, None, tx == 1, tx == 1]

    barrier = pltpu.get_barrier_semaphore()

    mutual = ty >= LATE
    for n, says in ((2, first[2]), (3, first[3] | (relayed & mutual))):

        @pl.when(says)
        def _():
            pl.semaphore_signal(
                barrier, inc=1, device_id={"tx": sides[n][2]}, device_id_type=MESH
            )

    def answer_first(n):
        axis, other = sides[n][1:]
        pl.semaphore_signal(
            ready.at[(1, 0, 3, 2)[n]], inc=1, device_id={axis: other}, device_id_type=MESH
        )

    def far_copy(field, x):
        return pltpu.make_async_remote_copy(
            src_ref=(f_now, a_now)[field].at[0, x],
            dst_ref=far.at[field, x],
            send_sem=far_sem.at[0],
            recv_sem=far_sem.at[1],
            device_id={"tx": tx - 1},
            device_id_type=MESH,
        )

    @pl.when(relayed & direct)
    def _():
        pl.semaphore_wait(barrier, 1)
        for x in range(4):
            far_copy(0, x).start()
            far_copy(1, x).start()
        answer_first(3)

    @pl.loop(1 - relayed.astype(jnp.int32), NS)
    def _(d):
        pl.semaphore_signal(
            barrier,
            inc=1,
            device_id={"shot": lax.rem(me + d, NS), "tx": home},
            device_id_type=MESH,
        )

    @pl.when(first[0])
    def _():
        pl.semaphore_signal(
            barrier, inc=1, device_id={"tx": home, "ty": ty + 1}, device_id_type=MESH
        )

    for n in (3, 5, 6, 7, 8, 9, 10, 11):
        loads[n].start()

    for present, start, size in (
        (ty > 0, 0, YH),
        (ty < NTY - 1, YH, YH),
        (tx > 0, 2 * YH, XH),
        (tx < NTX - 1, 2 * YH + XH, XH),
    ):

        @pl.when(jnp.logical_not(present))
        def _():
            halo[:, start : start + size, :] = jnp.zeros((2, size, CZ), jnp.bfloat16)

    def halo_copy(n, source=None):
        axis, other = sides[n][1], sides[n][2]
        start = (0, YH, 2 * YH, 2 * YH + XH)[n]
        size = YH if n < 2 else XH
        if source is None and n < 2:
            source = pick_send.at[n]
        elif source is None:
            source = high.at[:, pl.ds((CX - 4) * CY if n == 2 else 0, XH)]
        return pltpu.make_async_remote_copy(
            src_ref=source,
            dst_ref=halo.at[:, pl.ds(start, size)],
            send_sem=halo_send.at[n],
            recv_sem=halo_recv.at[n],
            device_id={axis: other},
            device_id_type=MESH,
        )

    def across():
        pl.semaphore_wait(barrier, 1)

        @pl.when(jnp.logical_not(mutual))
        def _():
            answer_first(3)

        halo_copy(3, edge).start()

    @pl.when(relayed & jnp.logical_not(direct))
    def _():
        pltpu.make_async_copy(edge_f, edge_f, edge_sem).wait()
        edge[...] = edge_f[...].reshape(2, XH, CZ).astype(jnp.bfloat16)

    @pl.when(relayed & (ty >= DIRECT) & jnp.logical_not(mutual))
    def _():
        across()

    pltpu.make_async_copy(now, now, load_sem.at[1]).wait()

    @pl.loop(0, 2)
    def _(field):
        u = now[field].reshape(ROWS, CZ)
        top = u.astype(jnp.bfloat16)
        high[field] = top
        low[field] = (u - top.astype(jnp.float32)).astype(jnp.bfloat16)

    loads[0].wait()
    row_l = lax.broadcasted_iota(jnp.int32, (CX, CX), 1)
    row_s = lax.broadcasted_iota(jnp.int32, (CX, CX), 0)
    ids_l = jnp.broadcast_to(ids[...], (CX, CX))
    ids_s = ids_l.T
    earlier = ((ids_s >> 5) == (ids_l >> 5)) & (row_s < row_l)
    rank = jnp.sum(earlier.astype(jnp.int32), axis=0, keepdims=True)
    slot = 2 * (ids[...] >> 5) + rank
    placed = jnp.broadcast_to(slot, (CX, CX)).T == row_l
    tables[0, :, 0:CX] = slot
    tables[1, :, 0:CX] = jnp.sum(jnp.where(placed, row_s, 0), axis=0, keepdims=True)
    wanted[me, :, 0:CX] = jnp.sum(jnp.where(placed, ids_s & (SLAB - 1), 0), axis=0, keepdims=True)
    table_copy = pltpu.make_async_copy(tables, smem_tables, table_sem)
    table_copy.start()

    loads[3].wait()

    @pl.loop(0, 2)
    def _(field):
        picked = mm(square[4 * ROWS : 5 * ROWS, :], high[field]).astype(jnp.bfloat16)
        pick_send[0, field] = picked[0:YH]
        pick_send[1, field] = picked[YH:]

    partners = NS - 1 + (ty > 0).astype(jnp.int32) + (tx == 0).astype(jnp.int32)
    partners = partners + ((tx == 1) & mutual).astype(jnp.int32)
    partners = partners + jnp.where(tx == 3, NS + (ty > 0).astype(jnp.int32), 0)

    @pl.when(jnp.logical_not(relayed))
    def _():
        pl.semaphore_wait(barrier, partners)

    @pl.when(tx == 3)
    def _():
        pl.semaphore_signal(go, inc=1, device_id={"tx": 2}, device_id_type=MESH)

    upper = me // 4 + lax.rem(me, 4) >= 2

    @pl.when(relayed & mutual & jnp.logical_not(upper))
    def _():
        across()

    @pl.when(relayed)
    def _():
        pl.semaphore_wait(go, 1)

    def id_copy(other):
        return pltpu.make_async_remote_copy(
            src_ref=wanted.at[me],
            dst_ref=wanted.at[me],
            send_sem=id_send,
            recv_sem=id_recv,
            device_id={"shot": other},
            device_id_type=MESH,
        )

    each_partner(lambda other: id_copy(other).start())

    @pl.when(relayed & mutual & upper)
    def _():
        across()

    @pl.when(ty > 0)
    def _():
        answer_first(1)

    @pl.when(tx == 0)
    def _():
        answer_first(2)

    @pl.when(jnp.logical_not(odd) | ((tx == 1) & mutual))
    def _():
        halo_copy(2).start()

    @pl.when(tx == 3)
    def _():
        halo_copy(3).start()

    later = (tx < 2) & (ty >= 4)

    @pl.when((ty > 0) & jnp.logical_not(later))
    def _():
        halo_copy(1).start()

    def answer(n):
        @pl.when(first[n])
        def _():
            pl.semaphore_wait(ready.at[n], 1)
            halo_copy(n).start()

    loads[4].wait()
    slab[...] = slab_b[...].astype(jnp.float32)

    def serve(shot):
        rows = [slab[wanted_by[shot, 0, 2 * me + k]] for k in range(2)]
        return jnp.concatenate(rows, axis=0).astype(jnp.bfloat16)

    def block_copy(owner, shot):
        return pltpu.make_async_remote_copy(
            src_ref=blocks.at[shot],
            dst_ref=arrived.at[owner],
            send_sem=v_send,
            recv_sem=v_recv.at[me // 4],
            device_id={"shot": shot},
            device_id_type=MESH,
        )

    @pl.loop(0, 2)
    def _(field):
        top, rest = high[field], low[field]
        lap[field] = (
            mm(square[0:ROWS, :], top)
            + mm(square[0:ROWS, :], rest)
            + mm(square[ROWS : 2 * ROWS, :], top)
            + mm(top, square[2 * ROWS : 3 * ROWS, :])
            + mm(rest, square[2 * ROWS : 3 * ROWS, :])
            + mm(top, square[3 * ROWS : 4 * ROWS, :])
        ).reshape(CX, CY, CZ)

    for load in loads[8:]:
        load.wait()
    row = lax.broadcasted_iota(jnp.int32, (ROWS, 1), 0)

    def local_row(along_x, along_y):
        inside = (along_x >= tx * CX) & (along_x < tx * CX + CX)
        inside = inside & (along_y >= ty * CY) & (along_y < ty * CY + CY)
        return jnp.where(inside, (along_x - tx * CX) * CY + along_y - ty * CY, -1)

    source_row = local_row(source_s[0, 0], source_s[0, 1])
    cell_row = local_row(cell_v[0:1, :], cell_v[1:2, :])
    injected = jnp.where(row == source_row, strength_s[0, 0], 0.0)
    recorded = jnp.sum(
        jnp.where(jnp.broadcast_to(row, (ROWS, NREC)) == cell_row, trace_v[...], 0.0),
        axis=1,
        keepdims=True,
    )
    surface = lax.broadcasted_iota(jnp.int32, (ROWS, CZ), 1) == SURFACE_DEPTH

    loads[5].wait()
    pltpu.make_async_copy(prev, prev, load_sem.at[6]).wait()
    answer(0)

    all_but_one = pl.ds(0, NS - 1)
    pltpu.make_async_copy(wanted.at[all_but_one], wanted.at[all_but_one], id_recv).wait()
    id_local = pltpu.make_async_copy(wanted, wanted_by, id_sem)
    id_local.start()
    id_local.wait()

    @each_partner
    def _(shot):
        blocks[shot] = serve(shot)
        block_copy(me, shot).start()

    @pl.when(later)
    def _():
        halo_copy(1).start()

    arrived[me] = serve(me)
    @pl.when(ty >= 5)
    def _():
        answer(3)

        @pl.when(jnp.logical_not(mutual))
        def _():
            answer(2)

    depth_l = lax.broadcasted_iota(jnp.int32, (CY, ROWS), 1)
    same_y = (depth_l & (CY - 1)) == lax.broadcasted_iota(jnp.int32, (CY, ROWS), 0)
    block_l = jnp.where(same_y, depth_l >> 3, -1)


    @pl.loop(0, NS)
    def _(shot):
        hits = [block_l == wanted_by[shot, 0, 2 * me + k] for k in range(2)]
        rows = pl.ds(pl.multiple_of(shot * 16, 16), 16)
        hit[rows, :] = jnp.where(jnp.concatenate(hits, axis=0), 1.0, 0.0)

    hit_out[...] = hit[...].T.astype(jnp.bfloat16)

    def halo_wait(n):
        @pl.when(sides[(1, 0, 3, 2)[n]][0])
        def _():
            halo_copy(n).wait_recv()

    halo_wait(0)
    halo_wait(1)
    @pl.loop(0, 2)
    def _(field):
        extra = jnp.where(field == 0, injected, recorded)
        layers = halo[field, 0 : 2 * YH]
        beyond = mm(halo_w[0:ROWS, :], layers) + mm(halo_w[ROWS:, :], layers)
        beyond = beyond + jnp.where(surface, jnp.broadcast_to(extra, (ROWS, CZ)), 0.0)
        lap[field] = lap[field] + beyond.reshape(CX, CY, CZ)
        prev[field] = 2.0 * now[field] - prev[field]

    @pl.when(ty < 5)
    def _():
        answer(3)
        answer(2)

    halo_wait(2)

    @pl.when((tx == 1) & direct)
    def _():
        pltpu.make_async_copy(far, far, far_sem.at[1]).wait()

    @pl.when((tx < NTX - 1) & jnp.logical_not((tx == 1) & direct))
    def _():
        halo_copy(3).wait_recv()

    @pl.when(jnp.logical_not((tx == 1) & direct))
    def _():
        far[...] = halo[:, 2 * YH + XH :].astype(jnp.float32).reshape(2, 4, CY, CZ)

    @pl.loop(0, 2)
    def _(field):
        near = halo[field, 2 * YH : 2 * YH + XH].astype(jnp.float32).reshape(4, CY, CZ)
        for q in range(4):
            for x in range(4):
                if x <= q:
                    weight = STENCIL_WEIGHTS[x + 4 - q]
                    lap[field, x] = lap[field, x] + weight * near[q]
                if x >= q:
                    weight = STENCIL_WEIGHTS[4 + q - x]
                    lap[field, CX - 4 + x] = lap[field, CX - 4 + x] + weight * far[field, q]

    table_copy.wait()

    def corr_copies(owner):
        return [
            pltpu.make_async_remote_copy(
                src_ref=source.at[owner],
                dst_ref=target.at[me],
                send_sem=c_send.at[n],
                recv_sem=c_recv.at[n],
                device_id={"shot": owner},
                device_id_type=MESH,
            )
            for n, (source, target) in enumerate(((peak_send, peak_in), (corr_send, corr_in)))
        ]

    def contribute(owner):
        pair = arrived[owner].astype(jnp.float32)
        products = []
        for k in range(2):
            scaled = pair[k * CY : (k + 1) * CY] * STEP_RATIO
            courant = scaled * scaled
            speed[2 * owner + k] = courant
            r = smem_tables[1, 0, 2 * owner + k]
            products.append(
                (prev[0, r] + courant * lap[0, r]) * (prev[1, r] + courant * lap[1, r])
            )
        both = jnp.concatenate(products, axis=0)
        top = jnp.max(jnp.abs(both), axis=0, keepdims=True)
        top = jnp.maximum(jnp.maximum(top[:, : CZ // 2], top[:, CZ // 2 :]), TINY)
        scale = STEPS / top
        code = jnp.round(both * jnp.concatenate([scale, scale], axis=1))
        return top, code.astype(jnp.int32).astype(jnp.int16)

    peak_in[me], corr_in[me] = contribute(me)

    def one_owner(owner):
        peak_send[owner], corr_send[owner] = contribute(owner)
        for copy in corr_copies(owner):
            copy.start()

    def row_of_blocks(x):
        for mine, count in ((x == me // 4, 3), (x != me // 4, 4)):

            @pl.when(mine)
            def _():
                four = arrived.at[pl.ds(4 * x, count)]
                pltpu.make_async_copy(four, four, v_recv.at[x]).wait()

    near = ((tx == 0) | (tx == 3)).astype(jnp.int32)
    each_partner(one_owner, near, row_of_blocks, ((tx == 1) & direct).astype(jnp.int32))

    @pl.loop(0, CX)
    def _(r):
        courant = speed[smem_tables[0, 0, r]]
        for field in range(2):
            prev[field, r] = prev[field, r] + courant * lap[field, r]

    def all_sent(ref, sem):
        pltpu.make_async_copy(ref.at[all_but_one], ref.at[all_but_one], sem).wait()

    all_sent(wanted, id_send)
    all_sent(blocks, v_send)
    for n in range(3):

        @pl.when(sides[n][0])
        def _():
            halo_copy(n).wait_send()

    @pl.when((tx > 0) & jnp.logical_not(relayed & direct))
    def _():
        halo_copy(3).wait_send()

    @pl.when(relayed & direct)
    def _():
        pltpu.make_async_copy(far, far, far_sem.at[0]).wait()

    all_sent(peak_send, c_send.at[0])
    all_sent(corr_send, c_send.at[1])
    all_sent(peak_in, c_recv.at[0])
    all_sent(corr_in, c_recv.at[1])


def finish(values, peak_in, corr_in, hit, f_out, a_out, image_out, image, out_sem):
    outs = [
        pltpu.make_async_copy(values.at[0], f_out.at[0], out_sem.at[0]),
        pltpu.make_async_copy(values.at[1], a_out.at[0], out_sem.at[1]),
        pltpu.make_async_copy(image, image_out.at[0], out_sem.at[2]),
    ]
    outs[0].start()
    outs[1].start()
    peak = peak_in[...]
    peak = jnp.broadcast_to(jnp.concatenate([peak, peak], axis=2), (NS, 2 * CY, CZ))
    share = corr_in[...].astype(jnp.int32).astype(jnp.float32) * (1.0 / STEPS)
    rows = (share * peak).reshape(ROWS, CZ)
    top = rows.astype(jnp.bfloat16)
    rest = (rows - top.astype(jnp.float32)).astype(jnp.bfloat16)
    image[...] = (mm(hit[...], top) + mm(hit[...], rest)).reshape(SLAB, CY, CZ)
    outs[2].start()
    for out in outs:
        out.wait()


def on_device(*arrays):
    square, halo_w = stencil_constants()
    arrays = (
        *arrays[:7],
        arrays[7].reshape(1, 1),
        jnp.swapaxes(arrays[8], 1, 2),
        arrays[9],
        jnp.asarray(square),
        jnp.asarray(halo_w),
    )
    field = jax.ShapeDtypeStruct((1, CX, CY, CZ), jnp.float32)
    dma = pltpu.SemaphoreType.DMA
    bf, f32, i32 = jnp.bfloat16, jnp.float32, jnp.int32
    scratch = [
        pltpu.VMEM((2, CX, CY, CZ), f32),
        pltpu.VMEM((2, CX, CY, CZ), f32),
        pltpu.VMEM((2, ROWS, CZ), bf),
        pltpu.VMEM((2, ROWS, CZ), bf),
        pltpu.VMEM((2, 4, CY, CZ), f32),
        pltpu.VMEM((2, XH, CZ), bf),
        pltpu.VMEM((2, 4, CY, CZ), f32),
        pltpu.VMEM((SLAB, CY, CZ), bf),
        pltpu.VMEM((SLAB, CY, CZ), f32),
        pltpu.VMEM((1, CX), i32),
        pltpu.VMEM((2, NREC), i32),
        pltpu.VMEM((1, NREC), f32),
        pltpu.VMEM(square.shape, bf),
        pltpu.VMEM(halo_w.shape, bf),
        pltpu.VMEM((2, 2, YH, CZ), bf),
        pltpu.VMEM((2, HALO, CZ), bf),
        pltpu.VMEM((2, 1, 128), i32),
        pltpu.VMEM((NS, 1, 128), i32),
        pltpu.SMEM((NS, 1, 128), i32),
        pltpu.VMEM((NS, 2 * CY, CZ), bf),
        pltpu.VMEM((NS, 2 * CY, CZ), bf),
        pltpu.VMEM((2 * NS, CY, CZ), f32),
        pltpu.VMEM((NS, 1, CZ // 2), f32),
        pltpu.VMEM((NS, 2 * CY, CZ), jnp.int16),
        pltpu.VMEM((ROWS, ROWS), f32),
        pltpu.SMEM((2, 1, 128), i32),
        pltpu.SMEM((1, 2), i32),
        pltpu.SMEM((1, 1), f32),
        dma((10,)),
        dma,
        dma((2,)),
        dma,
        dma,
        dma,
        dma,
        dma((4,)),
        dma((4,)),
        dma,
        dma((4,)),
        dma((2,)),
        dma((2,)),
        pltpu.SemaphoreType.REGULAR((4,)),
        pltpu.SemaphoreType.REGULAR,
    ]
    anywhere = pl.BlockSpec(memory_space=pl.ANY)
    vmem = pl.BlockSpec(memory_space=pltpu.VMEM)
    values, peak_in, corr_in, hit = pl.pallas_call(
        kernel,
        out_shape=(
            jax.ShapeDtypeStruct((2, CX, CY, CZ), f32),
            jax.ShapeDtypeStruct((NS, 1, CZ // 2), f32),
            jax.ShapeDtypeStruct((NS, 2 * CY, CZ), jnp.int16),
            jax.ShapeDtypeStruct((ROWS, ROWS), bf),
        ),
        in_specs=[anywhere] * 12,
        out_specs=(vmem,) * 4,
        scratch_shapes=scratch,
        compiler_params=pltpu.CompilerParams(
            collective_id=0, has_side_effects=True, vmem_limit_bytes=LIMIT
        ),
    )(*[a if a.size == 1 else pltpu.with_memory_space_constraint(a, pltpu.HBM) for a in arrays])
    return pl.pallas_call(
        finish,
        out_shape=(field, field, field),
        in_specs=[vmem] * 4,
        out_specs=(anywhere,) * 3,
        scratch_shapes=[pltpu.VMEM((SLAB, CY, CZ), f32), dma((3,))],
        compiler_params=pltpu.CompilerParams(vmem_limit_bytes=LIMIT),
    )(values, peak_in, corr_in, hit)


def solution(mesh):
    in_specs = (
        P("shot", "tx", "ty", None),
        P("shot", "tx", "ty", None),
        P("shot", "tx", "ty", None),
        P("shot", "tx", "ty", None),
        P(("tx", "ty"), "shot", None, None),
        P("shot", ("tx", "ty"), None),
        P("shot", None),
        P("shot"),
        P("shot", None, None),
        P("shot", None),
    )
    out_specs = (
        P("shot", "tx", "ty", None),
        P("shot", "tx", "ty", None),
        P(("tx", "ty"), "shot", None, None),
    )
    return jax.shard_map(
        on_device, mesh=mesh, in_specs=in_specs, out_specs=out_specs, check_vma=False
    )
```

```python
import functools

import jax
import jax.numpy as jnp
import ml_dtypes
import numpy as np
from jax import lax
from jax.experimental import pallas as pl
from jax.experimental.pallas import tpu as pltpu
from jax.sharding import PartitionSpec as P

SURFACE_DEPTH = 8
STENCIL_WEIGHTS = (-205.0 / 72.0, 8.0 / 5.0, -1.0 / 5.0, 8.0 / 315.0, -1.0 / 560.0)
STEP_RATIO = 0.1
MESH = pl.DeviceIdType.MESH
NS, NTX, NTY = 16, 4, 8
CX, CY, CZ = 32, 8, 256
ROWS = CX * CY
SLAB = 32
NREC = 128
YH = CX * 4
XH = 4 * CY
HALO = 2 * YH + 2 * XH
STEPS = 32766.0
TINY = 1e-34
DIRECT = 1
LATE = 6
LIMIT = 40 * 1024 * 1024


def stencil_constants():
    w = np.array(STENCIL_WEIGHTS)
    band = np.zeros(600)
    band[1:5] = w[1:]
    row = np.arange(ROWS)
    x, y = row // CY, row % CY
    dx, dy = np.abs(x[:, None] - x[None, :]), np.abs(y[:, None] - y[None, :])
    inner = band[dx] * (dy == 0) + band[dy] * (dx == 0) + 3.0 * w[0] * ((dx == 0) & (dy == 0))
    z = np.arange(CZ)
    depth = band[np.abs(z[:, None] - z[None, :])]
    pick = np.zeros((ROWS, ROWS))
    halo = np.zeros((ROWS, 2 * YH))
    for cx in range(CX):
        for q in range(4):
            pick[cx * 4 + q, cx * CY + CY - 4 + q] = 1.0
            pick[YH + cx * 4 + q, cx * CY + q] = 1.0
            for cy in range(CY):
                halo[cx * CY + cy, cx * 4 + q] = band[cy + 4 - q]
                halo[cx * CY + cy, YH + cx * 4 + q] = band[CY + q - cy]

    def parts(matrix):
        high = matrix.astype(np.float32).astype(ml_dtypes.bfloat16)
        low = (matrix - high.astype(np.float64)).astype(np.float32).astype(ml_dtypes.bfloat16)
        return [high, low]

    square = np.concatenate(parts(inner) + parts(depth) + parts(pick)[:1], axis=0)
    return square, np.concatenate(parts(halo), axis=0)


def each_partner(body, near=0, row=None, up=0):
    me = lax.axis_index("shot")
    turn_x = (me < NS // 2).astype(jnp.int32)
    turn_y = (lax.rem(me, 4) < 2).astype(jnp.int32)
    turn_x = turn_x + near * (1 - 2 * turn_x)
    turn_y = turn_y + near * (1 - 2 * turn_y)
    turn_x, turn_y = turn_x * (1 - up), turn_y * (1 - up)
    corner, step_x, step_y = 12 * turn_x + 3 * turn_y, 4 - 8 * turn_x, 1 - 2 * turn_y

    @pl.loop(0, 4)
    def _(i):
        if row is not None:
            row(3 * turn_x + (1 - 2 * turn_x) * i)

        @pl.loop(0, 4)
        def _(j):
            other = corner + step_x * i + step_y * j

            @pl.when(other != me)
            def _():
                body(other)


def mm(a, b):
    return jnp.dot(a, b, preferred_element_type=jnp.float32)


def kernel(
    f_prev, f_now, a_prev, a_now, velocity, aperture, source_cell, strength, receivers, traces,
    square_hbm, halo_hbm,
    prev, peak_in, corr_in, hit_out, part,
    now, lap, high, low, edge_f, edge, far, slab_b, slab, ids, cell_v, trace_v, square, halo_w,
    pick_send, halo, tables, wanted, wanted_by, blocks, arrived, speed, peak_send, corr_send,
    hit,
    smem_tables, source_s, strength_s,
    load_sem, edge_sem, far_sem, table_sem, id_sem, id_send, id_recv, halo_send, halo_recv, v_send, v_recv,
    c_send, c_recv, ready, go,
):
    me = lax.axis_index("shot")
    tx = lax.axis_index("tx")
    ty = lax.axis_index("ty")

    loads = [
        pltpu.make_async_copy(aperture.at[0], ids, load_sem.at[0]),
        pltpu.make_async_copy(f_now.at[0], now.at[0], load_sem.at[1]),
        pltpu.make_async_copy(a_now.at[0], now.at[1], load_sem.at[1]),
        pltpu.make_async_copy(square_hbm, square, load_sem.at[3]),
        pltpu.make_async_copy(velocity.at[0], slab_b, load_sem.at[4]),
        pltpu.make_async_copy(halo_hbm, halo_w, load_sem.at[5]),
        pltpu.make_async_copy(f_prev.at[0], prev.at[0], load_sem.at[6]),
        pltpu.make_async_copy(a_prev.at[0], prev.at[1], load_sem.at[6]),
        pltpu.make_async_copy(receivers.at[0], cell_v, load_sem.at[8]),
        pltpu.make_async_copy(traces, trace_v, load_sem.at[9]),
        pltpu.make_async_copy(source_cell, source_s, load_sem.at[2]),
        pltpu.make_async_copy(strength, strength_s, load_sem.at[7]),
    ]
    edge_loads = [
        pltpu.make_async_copy(now_hbm.at[0, 0:4], edge_f.at[field], edge_sem)
        for field, now_hbm in enumerate((f_now, a_now))
    ]

    direct = ty < DIRECT

    @pl.when((tx == 2) & jnp.logical_not(direct))
    def _():
        edge_loads[0].start()
        edge_loads[1].start()

    for n in (0, 1, 2, 4):
        loads[n].start()

    relayed = tx == 2
    home = tx + relayed.astype(jnp.int32)
    odd = lax.rem(tx, 2) == 1
    sides = [
        (ty < NTY - 1, "ty", ty + 1),
        (ty > 0, "ty", ty - 1),
        (tx < NTX - 1, "tx", tx + 1),
        (tx > 0, "tx", tx - 1),
    ]
    first = [ty < NTY - 1, None, tx == 1, tx == 1]

    barrier = pltpu.get_barrier_semaphore()

    mutual = ty >= LATE
    for n, says in ((2, first[2]), (3, first[3] | (relayed & mutual))):

        @pl.when(says)
        def _():
            pl.semaphore_signal(
                barrier, inc=1, device_id={"tx": sides[n][2]}, device_id_type=MESH
            )

    def answer_first(n):
        axis, other = sides[n][1:]
        pl.semaphore_signal(
            ready.at[(1, 0, 3, 2)[n]], inc=1, device_id={axis: other}, device_id_type=MESH
        )

    def far_copy(field, x):
        return pltpu.make_async_remote_copy(
            src_ref=(f_now, a_now)[field].at[0, x],
            dst_ref=far.at[field, x],
            send_sem=far_sem.at[0],
            recv_sem=far_sem.at[1],
            device_id={"tx": tx - 1},
            device_id_type=MESH,
        )

    @pl.when(relayed & direct)
    def _():
        pl.semaphore_wait(barrier, 1)
        for x in range(4):
            far_copy(0, x).start()
            far_copy(1, x).start()
        answer_first(3)

    @pl.loop(1 - relayed.astype(jnp.int32), NS)
    def _(d):
        pl.semaphore_signal(
            barrier,
            inc=1,
            device_id={"shot": lax.rem(me + d, NS), "tx": home},
            device_id_type=MESH,
        )

    @pl.when(first[0])
    def _():
        pl.semaphore_signal(
            barrier, inc=1, device_id={"tx": home, "ty": ty + 1}, device_id_type=MESH
        )

    for n in (3, 5, 6, 7, 8, 9, 10, 11):
        loads[n].start()

    for present, start, size in (
        (ty > 0, 0, YH),
        (ty < NTY - 1, YH, YH),
        (tx > 0, 2 * YH, XH),
        (tx < NTX - 1, 2 * YH + XH, XH),
    ):

        @pl.when(jnp.logical_not(present))
        def _():
            halo[:, start : start + size, :] = jnp.zeros((2, size, CZ), jnp.bfloat16)

    def halo_copy(n, source=None):
        axis, other = sides[n][1], sides[n][2]
        start = (0, YH, 2 * YH, 2 * YH + XH)[n]
        size = YH if n < 2 else XH
        if source is None and n < 2:
            source = pick_send.at[n]
        elif source is None:
            source = high.at[:, pl.ds((CX - 4) * CY if n == 2 else 0, XH)]
        return pltpu.make_async_remote_copy(
            src_ref=source,
            dst_ref=halo.at[:, pl.ds(start, size)],
            send_sem=halo_send.at[n],
            recv_sem=halo_recv.at[n],
            device_id={axis: other},
            device_id_type=MESH,
        )

    def across():
        pl.semaphore_wait(barrier, 1)

        @pl.when(jnp.logical_not(mutual))
        def _():
            answer_first(3)

        halo_copy(3, edge).start()

    @pl.when(relayed & jnp.logical_not(direct))
    def _():
        pltpu.make_async_copy(edge_f, edge_f, edge_sem).wait()
        edge[...] = edge_f[...].reshape(2, XH, CZ).astype(jnp.bfloat16)

    @pl.when(relayed & (ty >= DIRECT) & jnp.logical_not(mutual))
    def _():
        across()

    pltpu.make_async_copy(now, now, load_sem.at[1]).wait()

    @pl.loop(0, 2)
    def _(field):
        u = now[field].reshape(ROWS, CZ)
        top = u.astype(jnp.bfloat16)
        high[field] = top
        low[field] = (u - top.astype(jnp.float32)).astype(jnp.bfloat16)

    loads[0].wait()
    row_l = lax.broadcasted_iota(jnp.int32, (CX, CX), 1)
    row_s = lax.broadcasted_iota(jnp.int32, (CX, CX), 0)
    ids_l = jnp.broadcast_to(ids[...], (CX, CX))
    ids_s = ids_l.T
    earlier = ((ids_s >> 5) == (ids_l >> 5)) & (row_s < row_l)
    rank = jnp.sum(earlier.astype(jnp.int32), axis=0, keepdims=True)
    slot = 2 * (ids[...] >> 5) + rank
    placed = jnp.broadcast_to(slot, (CX, CX)).T == row_l
    tables[0, :, 0:CX] = slot
    tables[1, :, 0:CX] = jnp.sum(jnp.where(placed, row_s, 0), axis=0, keepdims=True)
    wanted[me, :, 0:CX] = jnp.sum(jnp.where(placed, ids_s & (SLAB - 1), 0), axis=0, keepdims=True)
    table_copy = pltpu.make_async_copy(tables, smem_tables, table_sem)
    table_copy.start()

    loads[3].wait()

    @pl.loop(0, 2)
    def _(field):
        picked = mm(square[4 * ROWS : 5 * ROWS, :], high[field]).astype(jnp.bfloat16)
        pick_send[0, field] = picked[0:YH]
        pick_send[1, field] = picked[YH:]

    partners = NS - 1 + (ty > 0).astype(jnp.int32) + (tx == 0).astype(jnp.int32)
    partners = partners + ((tx == 1) & mutual).astype(jnp.int32)
    partners = partners + jnp.where(tx == 3, NS + (ty > 0).astype(jnp.int32), 0)

    @pl.when(jnp.logical_not(relayed))
    def _():
        pl.semaphore_wait(barrier, partners)

    @pl.when(tx == 3)
    def _():
        pl.semaphore_signal(go, inc=1, device_id={"tx": 2}, device_id_type=MESH)

    upper = me // 4 + lax.rem(me, 4) >= 2

    @pl.when(relayed & mutual & jnp.logical_not(upper))
    def _():
        across()

    @pl.when(relayed)
    def _():
        pl.semaphore_wait(go, 1)

    def id_copy(other):
        return pltpu.make_async_remote_copy(
            src_ref=wanted.at[me],
            dst_ref=wanted.at[me],
            send_sem=id_send,
            recv_sem=id_recv,
            device_id={"shot": other},
            device_id_type=MESH,
        )

    each_partner(lambda other: id_copy(other).start())

    @pl.when(relayed & mutual & upper)
    def _():
        across()

    @pl.when(ty > 0)
    def _():
        answer_first(1)

    @pl.when(tx == 0)
    def _():
        answer_first(2)

    @pl.when(jnp.logical_not(odd) | ((tx == 1) & mutual))
    def _():
        halo_copy(2).start()

    @pl.when(tx == 3)
    def _():
        halo_copy(3).start()

    @pl.when(ty > 0)
    def _():
        halo_copy(1).start()

    def answer(n):
        @pl.when(first[n])
        def _():
            pl.semaphore_wait(ready.at[n], 1)
            halo_copy(n).start()

    loads[4].wait()
    slab[...] = slab_b[...].astype(jnp.float32)

    def serve(shot):
        rows = [slab[wanted_by[shot, 0, 2 * me + k]] for k in range(2)]
        return jnp.concatenate(rows, axis=0).astype(jnp.bfloat16)

    def block_copy(owner, shot):
        return pltpu.make_async_remote_copy(
            src_ref=blocks.at[shot],
            dst_ref=arrived.at[owner],
            send_sem=v_send,
            recv_sem=v_recv.at[me // 4],
            device_id={"shot": shot},
            device_id_type=MESH,
        )

    @pl.loop(0, 2)
    def _(field):
        top, rest = high[field], low[field]
        lap[field] = (
            mm(square[0:ROWS, :], top)
            + mm(square[0:ROWS, :], rest)
            + mm(square[ROWS : 2 * ROWS, :], top)
            + mm(top, square[2 * ROWS : 3 * ROWS, :])
            + mm(rest, square[2 * ROWS : 3 * ROWS, :])
            + mm(top, square[3 * ROWS : 4 * ROWS, :])
        ).reshape(CX, CY, CZ)

    for load in loads[8:]:
        load.wait()
    row = lax.broadcasted_iota(jnp.int32, (ROWS, 1), 0)

    def local_row(along_x, along_y):
        inside = (along_x >= tx * CX) & (along_x < tx * CX + CX)
        inside = inside & (along_y >= ty * CY) & (along_y < ty * CY + CY)
        return jnp.where(inside, (along_x - tx * CX) * CY + along_y - ty * CY, -1)

    source_row = local_row(source_s[0, 0], source_s[0, 1])
    cell_row = local_row(cell_v[0:1, :], cell_v[1:2, :])
    injected = jnp.where(row == source_row, strength_s[0, 0], 0.0)
    recorded = jnp.sum(
        jnp.where(jnp.broadcast_to(row, (ROWS, NREC)) == cell_row, trace_v[...], 0.0),
        axis=1,
        keepdims=True,
    )
    surface = lax.broadcasted_iota(jnp.int32, (ROWS, CZ), 1) == SURFACE_DEPTH

    loads[5].wait()
    pltpu.make_async_copy(prev, prev, load_sem.at[6]).wait()
    answer(0)

    all_but_one = pl.ds(0, NS - 1)
    pltpu.make_async_copy(wanted.at[all_but_one], wanted.at[all_but_one], id_recv).wait()
    id_local = pltpu.make_async_copy(wanted, wanted_by, id_sem)
    id_local.start()
    id_local.wait()

    @each_partner
    def _(shot):
        blocks[shot] = serve(shot)
        block_copy(me, shot).start()

    arrived[me] = serve(me)
    @pl.when(ty >= 5)
    def _():
        answer(3)

        @pl.when(jnp.logical_not(mutual))
        def _():
            answer(2)

    depth_l = lax.broadcasted_iota(jnp.int32, (CY, ROWS), 1)
    same_y = (depth_l & (CY - 1)) == lax.broadcasted_iota(jnp.int32, (CY, ROWS), 0)
    block_l = jnp.where(same_y, depth_l >> 3, -1)


    @pl.loop(0, NS)
    def _(shot):
        hits = [block_l == wanted_by[shot, 0, 2 * me + k] for k in range(2)]
        rows = pl.ds(pl.multiple_of(shot * 16, 16), 16)
        hit[rows, :] = jnp.where(jnp.concatenate(hits, axis=0), 1.0, 0.0)

    hit_out[...] = hit[...].T.astype(jnp.bfloat16)

    def halo_wait(n):
        @pl.when(sides[(1, 0, 3, 2)[n]][0])
        def _():
            halo_copy(n).wait_recv()

    halo_wait(0)
    halo_wait(1)
    @pl.loop(0, 2)
    def _(field):
        extra = jnp.where(field == 0, injected, recorded)
        layers = halo[field, 0 : 2 * YH]
        beyond = mm(halo_w[0:ROWS, :], layers) + mm(halo_w[ROWS:, :], layers)
        beyond = beyond + jnp.where(surface, jnp.broadcast_to(extra, (ROWS, CZ)), 0.0)
        lap[field] = lap[field] + beyond.reshape(CX, CY, CZ)
        prev[field] = 2.0 * now[field] - prev[field]

    @pl.when(ty < 5)
    def _():
        answer(3)
        answer(2)

    halo_wait(2)

    @pl.when((tx == 1) & direct)
    def _():
        pltpu.make_async_copy(far, far, far_sem.at[1]).wait()

    @pl.when((tx < NTX - 1) & jnp.logical_not((tx == 1) & direct))
    def _():
        halo_copy(3).wait_recv()

    @pl.when(jnp.logical_not((tx == 1) & direct))
    def _():
        far[...] = halo[:, 2 * YH + XH :].astype(jnp.float32).reshape(2, 4, CY, CZ)

    @pl.loop(0, 2)
    def _(field):
        near = halo[field, 2 * YH : 2 * YH + XH].astype(jnp.float32).reshape(4, CY, CZ)
        for q in range(4):
            for x in range(4):
                if x <= q:
                    weight = STENCIL_WEIGHTS[x + 4 - q]
                    lap[field, x] = lap[field, x] + weight * near[q]
                if x >= q:
                    weight = STENCIL_WEIGHTS[4 + q - x]
                    lap[field, CX - 4 + x] = lap[field, CX - 4 + x] + weight * far[field, q]

    table_copy.wait()

    def corr_copies(owner):
        return [
            pltpu.make_async_remote_copy(
                src_ref=source.at[owner],
                dst_ref=target.at[me],
                send_sem=c_send.at[n],
                recv_sem=c_recv.at[2 * (me // 8) + n],
                device_id={"shot": owner},
                device_id_type=MESH,
            )
            for n, (source, target) in enumerate(((peak_send, peak_in), (corr_send, corr_in)))
        ]

    def contribute(owner):
        pair = arrived[owner].astype(jnp.float32)
        products = []
        for k in range(2):
            scaled = pair[k * CY : (k + 1) * CY] * STEP_RATIO
            courant = scaled * scaled
            speed[2 * owner + k] = courant
            r = smem_tables[1, 0, 2 * owner + k]
            products.append(
                (prev[0, r] + courant * lap[0, r]) * (prev[1, r] + courant * lap[1, r])
            )
        both = jnp.concatenate(products, axis=0)
        top = jnp.max(jnp.abs(both), axis=0, keepdims=True)
        top = jnp.maximum(jnp.maximum(top[:, : CZ // 2], top[:, CZ // 2 :]), TINY)
        scale = STEPS / top
        code = jnp.round(both * jnp.concatenate([scale, scale], axis=1))
        return top, code.astype(jnp.int32).astype(jnp.int16)

    peak_in[me], corr_in[me] = contribute(me)

    def one_owner(owner):
        peak_send[owner], corr_send[owner] = contribute(owner)
        for copy in corr_copies(owner):
            copy.start()

    def row_of_blocks(x):
        for mine, count in ((x == me // 4, 3), (x != me // 4, 4)):

            @pl.when(mine)
            def _():
                four = arrived.at[pl.ds(4 * x, count)]
                pltpu.make_async_copy(four, four, v_recv.at[x]).wait()

    near = ((tx == 0) | (tx == 3)).astype(jnp.int32)
    each_partner(one_owner, near, row_of_blocks, ((tx == 1) & direct).astype(jnp.int32))

    @pl.loop(0, CX)
    def _(r):
        courant = speed[smem_tables[0, 0, r]]
        for field in range(2):
            prev[field, r] = prev[field, r] + courant * lap[field, r]

    def all_sent(ref, sem):
        pltpu.make_async_copy(ref.at[all_but_one], ref.at[all_but_one], sem).wait()

    all_sent(wanted, id_send)
    all_sent(blocks, v_send)
    for n in range(3):

        @pl.when(sides[n][0])
        def _():
            halo_copy(n).wait_send()

    @pl.when((tx > 0) & jnp.logical_not(relayed & direct))
    def _():
        halo_copy(3).wait_send()

    @pl.when(relayed & direct)
    def _():
        pltpu.make_async_copy(far, far, far_sem.at[0]).wait()

    all_sent(peak_send, c_send.at[0])
    all_sent(corr_send, c_send.at[1])
    def arrive(half, count):
        for n, ref in enumerate((peak_in, corr_in)):
            some = ref.at[pl.ds(0, count)]
            pltpu.make_async_copy(some, some, c_recv.at[2 * half + n]).wait()

    arrive(me // 8, 7)
    part[...] = image_of(me // 8, peak_in, corr_in, hit_out)
    arrive(1 - me // 8, 8)


def image_of(half, peak_in, corr_in, hit):
    shots = pl.ds(8 * half, 8)
    peak = peak_in[shots]
    peak = jnp.broadcast_to(jnp.concatenate([peak, peak], axis=2), (8, 2 * CY, CZ))
    share = corr_in[shots].astype(jnp.int32).astype(jnp.float32) * (1.0 / STEPS)
    rows = (share * peak).reshape(ROWS // 2, CZ)
    top = rows.astype(jnp.bfloat16)
    rest = (rows - top.astype(jnp.float32)).astype(jnp.bfloat16)
    chosen = hit[:, pl.ds(pl.multiple_of(ROWS // 2 * half, ROWS // 2), ROWS // 2)]
    return mm(chosen, top) + mm(chosen, rest)


def finish(values, peak_in, corr_in, hit, part, f_out, a_out, image_out, image, out_sem):
    outs = [
        pltpu.make_async_copy(values.at[0], f_out.at[0], out_sem.at[0]),
        pltpu.make_async_copy(values.at[1], a_out.at[0], out_sem.at[1]),
        pltpu.make_async_copy(image, image_out.at[0], out_sem.at[2]),
    ]
    outs[0].start()
    outs[1].start()
    half = 1 - lax.axis_index("shot") // 8
    total = part[...] + image_of(half, peak_in, corr_in, hit)
    image[...] = total.reshape(SLAB, CY, CZ)
    outs[2].start()
    for out in outs:
        out.wait()


def on_device(*arrays):
    square, halo_w = stencil_constants()
    arrays = (
        *arrays[:7],
        arrays[7].reshape(1, 1),
        jnp.swapaxes(arrays[8], 1, 2),
        arrays[9],
        jnp.asarray(square),
        jnp.asarray(halo_w),
    )
    field = jax.ShapeDtypeStruct((1, CX, CY, CZ), jnp.float32)
    dma = pltpu.SemaphoreType.DMA
    bf, f32, i32 = jnp.bfloat16, jnp.float32, jnp.int32
    scratch = [
        pltpu.VMEM((2, CX, CY, CZ), f32),
        pltpu.VMEM((2, CX, CY, CZ), f32),
        pltpu.VMEM((2, ROWS, CZ), bf),
        pltpu.VMEM((2, ROWS, CZ), bf),
        pltpu.VMEM((2, 4, CY, CZ), f32),
        pltpu.VMEM((2, XH, CZ), bf),
        pltpu.VMEM((2, 4, CY, CZ), f32),
        pltpu.VMEM((SLAB, CY, CZ), bf),
        pltpu.VMEM((SLAB, CY, CZ), f32),
        pltpu.VMEM((1, CX), i32),
        pltpu.VMEM((2, NREC), i32),
        pltpu.VMEM((1, NREC), f32),
        pltpu.VMEM(square.shape, bf),
        pltpu.VMEM(halo_w.shape, bf),
        pltpu.VMEM((2, 2, YH, CZ), bf),
        pltpu.VMEM((2, HALO, CZ), bf),
        pltpu.VMEM((2, 1, 128), i32),
        pltpu.VMEM((NS, 1, 128), i32),
        pltpu.SMEM((NS, 1, 128), i32),
        pltpu.VMEM((NS, 2 * CY, CZ), bf),
        pltpu.VMEM((NS, 2 * CY, CZ), bf),
        pltpu.VMEM((2 * NS, CY, CZ), f32),
        pltpu.VMEM((NS, 1, CZ // 2), f32),
        pltpu.VMEM((NS, 2 * CY, CZ), jnp.int16),
        pltpu.VMEM((ROWS, ROWS), f32),
        pltpu.SMEM((2, 1, 128), i32),
        pltpu.SMEM((1, 2), i32),
        pltpu.SMEM((1, 1), f32),
        dma((10,)),
        dma,
        dma((2,)),
        dma,
        dma,
        dma,
        dma,
        dma((4,)),
        dma((4,)),
        dma,
        dma((4,)),
        dma((2,)),
        dma((4,)),
        pltpu.SemaphoreType.REGULAR((4,)),
        pltpu.SemaphoreType.REGULAR,
    ]
    anywhere = pl.BlockSpec(memory_space=pl.ANY)
    vmem = pl.BlockSpec(memory_space=pltpu.VMEM)
    results = pl.pallas_call(
        kernel,
        out_shape=(
            jax.ShapeDtypeStruct((2, CX, CY, CZ), f32),
            jax.ShapeDtypeStruct((NS, 1, CZ // 2), f32),
            jax.ShapeDtypeStruct((NS, 2 * CY, CZ), jnp.int16),
            jax.ShapeDtypeStruct((ROWS, ROWS), bf),
            jax.ShapeDtypeStruct((ROWS, CZ), f32),
        ),
        in_specs=[anywhere] * 12,
        out_specs=(vmem,) * 5,
        scratch_shapes=scratch,
        compiler_params=pltpu.CompilerParams(
            collective_id=0, has_side_effects=True, vmem_limit_bytes=LIMIT
        ),
    )(*[a if a.size == 1 else pltpu.with_memory_space_constraint(a, pltpu.HBM) for a in arrays])
    return pl.pallas_call(
        finish,
        out_shape=(field, field, field),
        in_specs=[vmem] * 5,
        out_specs=(anywhere,) * 3,
        scratch_shapes=[pltpu.VMEM((SLAB, CY, CZ), f32), dma((3,))],
        compiler_params=pltpu.CompilerParams(vmem_limit_bytes=LIMIT),
    )(*results)


def solution(mesh):
    in_specs = (
        P("shot", "tx", "ty", None),
        P("shot", "tx", "ty", None),
        P("shot", "tx", "ty", None),
        P("shot", "tx", "ty", None),
        P(("tx", "ty"), "shot", None, None),
        P("shot", ("tx", "ty"), None),
        P("shot", None),
        P("shot"),
        P("shot", None, None),
        P("shot", None),
    )
    out_specs = (
        P("shot", "tx", "ty", None),
        P("shot", "tx", "ty", None),
        P(("tx", "ty"), "shot", None, None),
    )
    return jax.shard_map(
        on_device, mesh=mesh, in_specs=in_specs, out_specs=out_specs, check_vma=False
    )
```

```python
import functools

import jax
import jax.numpy as jnp
import ml_dtypes
import numpy as np
from jax import lax
from jax.experimental import pallas as pl
from jax.experimental.pallas import tpu as pltpu
from jax.sharding import PartitionSpec as P

SURFACE_DEPTH = 8
STENCIL_WEIGHTS = (-205.0 / 72.0, 8.0 / 5.0, -1.0 / 5.0, 8.0 / 315.0, -1.0 / 560.0)
STEP_RATIO = 0.1
MESH = pl.DeviceIdType.MESH
NS, NTX, NTY = 16, 4, 8
CX, CY, CZ = 32, 8, 256
ROWS = CX * CY
SLAB = 32
NREC = 128
YH = CX * 4
XH = 4 * CY
HALO = 2 * YH + 2 * XH
STEPS = 32766.0
TINY = 1e-34
DIRECT = 1
LATE = 6
LIMIT = 40 * 1024 * 1024


def stencil_constants():
    w = np.array(STENCIL_WEIGHTS)
    band = np.zeros(600)
    band[1:5] = w[1:]
    row = np.arange(ROWS)
    x, y = row // CY, row % CY
    dx, dy = np.abs(x[:, None] - x[None, :]), np.abs(y[:, None] - y[None, :])
    inner = band[dx] * (dy == 0) + band[dy] * (dx == 0) + 3.0 * w[0] * ((dx == 0) & (dy == 0))
    z = np.arange(CZ)
    depth = band[np.abs(z[:, None] - z[None, :])]
    pick = np.zeros((ROWS, ROWS))
    halo = np.zeros((ROWS, 2 * YH))
    for cx in range(CX):
        for q in range(4):
            pick[cx * 4 + q, cx * CY + CY - 4 + q] = 1.0
            pick[YH + cx * 4 + q, cx * CY + q] = 1.0
            for cy in range(CY):
                halo[cx * CY + cy, cx * 4 + q] = band[cy + 4 - q]
                halo[cx * CY + cy, YH + cx * 4 + q] = band[CY + q - cy]

    def parts(matrix):
        high = matrix.astype(np.float32).astype(ml_dtypes.bfloat16)
        low = (matrix - high.astype(np.float64)).astype(np.float32).astype(ml_dtypes.bfloat16)
        return [high, low]

    square = np.concatenate(parts(inner) + parts(depth) + parts(pick)[:1], axis=0)
    return square, np.concatenate(parts(halo), axis=0)


def each_partner(body, near=0, row=None, up=0):
    me = lax.axis_index("shot")
    turn_x = (me < NS // 2).astype(jnp.int32)
    turn_y = (lax.rem(me, 4) < 2).astype(jnp.int32)
    turn_x = turn_x + near * (1 - 2 * turn_x)
    turn_y = turn_y + near * (1 - 2 * turn_y)
    turn_x, turn_y = turn_x * (1 - up), turn_y * (1 - up)
    corner, step_x, step_y = 12 * turn_x + 3 * turn_y, 4 - 8 * turn_x, 1 - 2 * turn_y

    @pl.loop(0, 4)
    def _(i):
        if row is not None:
            row(3 * turn_x + (1 - 2 * turn_x) * i)

        for j in range(4):
            other = corner + step_x * i + step_y * j

            @pl.when(other != me)
            def _():
                body(other)


def mm(a, b):
    return jnp.dot(a, b, preferred_element_type=jnp.float32)


def kernel(
    f_prev, f_now, a_prev, a_now, velocity, aperture, source_cell, strength, receivers, traces,
    square_hbm, halo_hbm,
    prev, peak_in, corr_in, hit_out, part,
    now, lap, high, low, edge_f, edge, far, slab_b, slab, ids, cell_v, trace_v, square, halo_w,
    pick_send, halo, tables, wanted, wanted_by, blocks, arrived, speed, peak_send, corr_send,
    hit,
    smem_tables, source_s, strength_s,
    load_sem, edge_sem, far_sem, table_sem, id_send, id_recv, halo_send, halo_recv, v_send, v_recv,
    c_send, c_recv, ready, go,
):
    me = lax.axis_index("shot")
    tx = lax.axis_index("tx")
    ty = lax.axis_index("ty")

    loads = [
        pltpu.make_async_copy(aperture.at[0], ids, load_sem.at[0]),
        pltpu.make_async_copy(f_now.at[0], now.at[0], load_sem.at[1]),
        pltpu.make_async_copy(a_now.at[0], now.at[1], load_sem.at[1]),
        pltpu.make_async_copy(square_hbm, square, load_sem.at[3]),
        pltpu.make_async_copy(velocity.at[0], slab_b, load_sem.at[4]),
        pltpu.make_async_copy(halo_hbm, halo_w, load_sem.at[5]),
        pltpu.make_async_copy(f_prev.at[0], prev.at[0], load_sem.at[6]),
        pltpu.make_async_copy(a_prev.at[0], prev.at[1], load_sem.at[6]),
        pltpu.make_async_copy(receivers.at[0], cell_v, load_sem.at[8]),
        pltpu.make_async_copy(traces, trace_v, load_sem.at[9]),
        pltpu.make_async_copy(source_cell, source_s, load_sem.at[2]),
        pltpu.make_async_copy(strength, strength_s, load_sem.at[7]),
    ]
    edge_loads = [
        pltpu.make_async_copy(now_hbm.at[0, 0:4], edge_f.at[field], edge_sem)
        for field, now_hbm in enumerate((f_now, a_now))
    ]

    direct = ty < DIRECT

    @pl.when((tx == 2) & jnp.logical_not(direct))
    def _():
        edge_loads[0].start()
        edge_loads[1].start()

    for n in (0, 1, 2, 4):
        loads[n].start()

    relayed = tx == 2
    home = tx + relayed.astype(jnp.int32)
    odd = lax.rem(tx, 2) == 1
    sides = [
        (ty < NTY - 1, "ty", ty + 1),
        (ty > 0, "ty", ty - 1),
        (tx < NTX - 1, "tx", tx + 1),
        (tx > 0, "tx", tx - 1),
    ]
    first = [ty < NTY - 1, None, tx == 1, tx == 1]

    barrier = pltpu.get_barrier_semaphore()

    mutual = ty >= LATE
    for n, says in ((2, first[2]), (3, first[3] | (relayed & mutual))):

        @pl.when(says)
        def _():
            pl.semaphore_signal(
                barrier, inc=1, device_id={"tx": sides[n][2]}, device_id_type=MESH
            )

    def answer_first(n):
        axis, other = sides[n][1:]
        pl.semaphore_signal(
            ready.at[(1, 0, 3, 2)[n]], inc=1, device_id={axis: other}, device_id_type=MESH
        )

    def far_copy(field, x):
        return pltpu.make_async_remote_copy(
            src_ref=(f_now, a_now)[field].at[0, x],
            dst_ref=far.at[field, x],
            send_sem=far_sem.at[0],
            recv_sem=far_sem.at[1],
            device_id={"tx": tx - 1},
            device_id_type=MESH,
        )

    @pl.when(relayed & direct)
    def _():
        pl.semaphore_wait(barrier, 1)
        for x in range(4):
            far_copy(0, x).start()
            far_copy(1, x).start()
        answer_first(3)

    @pl.loop(1 - relayed.astype(jnp.int32), NS)
    def _(d):
        pl.semaphore_signal(
            barrier,
            inc=1,
            device_id={"shot": lax.rem(me + d, NS), "tx": home},
            device_id_type=MESH,
        )

    @pl.when(first[0])
    def _():
        pl.semaphore_signal(
            barrier, inc=1, device_id={"tx": home, "ty": ty + 1}, device_id_type=MESH
        )

    for n in (3, 5, 6, 7, 8, 9, 10, 11):
        loads[n].start()

    for present, start, size in (
        (ty > 0, 0, YH),
        (ty < NTY - 1, YH, YH),
        (tx > 0, 2 * YH, XH),
        (tx < NTX - 1, 2 * YH + XH, XH),
    ):

        @pl.when(jnp.logical_not(present))
        def _():
            halo[:, start : start + size, :] = jnp.zeros((2, size, CZ), jnp.bfloat16)

    def halo_copy(n, source=None):
        axis, other = sides[n][1], sides[n][2]
        start = (0, YH, 2 * YH, 2 * YH + XH)[n]
        size = YH if n < 2 else XH
        if source is None and n < 2:
            source = pick_send.at[n]
        elif source is None:
            source = high.at[:, pl.ds((CX - 4) * CY if n == 2 else 0, XH)]
        return pltpu.make_async_remote_copy(
            src_ref=source,
            dst_ref=halo.at[:, pl.ds(start, size)],
            send_sem=halo_send.at[n],
            recv_sem=halo_recv.at[n],
            device_id={axis: other},
            device_id_type=MESH,
        )

    def across():
        pl.semaphore_wait(barrier, 1)

        @pl.when(jnp.logical_not(mutual))
        def _():
            answer_first(3)

        halo_copy(3, edge).start()

    @pl.when(relayed & jnp.logical_not(direct))
    def _():
        pltpu.make_async_copy(edge_f, edge_f, edge_sem).wait()
        edge[...] = edge_f[...].reshape(2, XH, CZ).astype(jnp.bfloat16)

    @pl.when(relayed & (ty >= DIRECT) & jnp.logical_not(mutual))
    def _():
        across()

    pltpu.make_async_copy(now, now, load_sem.at[1]).wait()

    @pl.loop(0, 2)
    def _(field):
        u = now[field].reshape(ROWS, CZ)
        top = u.astype(jnp.bfloat16)
        high[field] = top
        low[field] = (u - top.astype(jnp.float32)).astype(jnp.bfloat16)

    loads[0].wait()
    row_l = lax.broadcasted_iota(jnp.int32, (CX, CX), 1)
    row_s = lax.broadcasted_iota(jnp.int32, (CX, CX), 0)
    ids_l = jnp.broadcast_to(ids[...], (CX, CX))
    ids_s = ids_l.T
    earlier = ((ids_s >> 5) == (ids_l >> 5)) & (row_s < row_l)
    rank = jnp.sum(earlier.astype(jnp.int32), axis=0, keepdims=True)
    slot = 2 * (ids[...] >> 5) + rank
    placed = jnp.broadcast_to(slot, (CX, CX)).T == row_l
    tables[0, :, 0:CX] = slot
    tables[1, :, 0:CX] = jnp.sum(jnp.where(placed, row_s, 0), axis=0, keepdims=True)
    wanted[me, :, 0:CX] = jnp.sum(jnp.where(placed, ids_s & (SLAB - 1), 0), axis=0, keepdims=True)
    table_copy = pltpu.make_async_copy(tables, smem_tables, table_sem)
    table_copy.start()

    loads[3].wait()

    @pl.loop(0, 2)
    def _(field):
        picked = mm(square[4 * ROWS : 5 * ROWS, :], high[field]).astype(jnp.bfloat16)
        pick_send[0, field] = picked[0:YH]
        pick_send[1, field] = picked[YH:]

    partners = NS - 1 + (ty > 0).astype(jnp.int32) + (tx == 0).astype(jnp.int32)
    partners = partners + ((tx == 1) & mutual).astype(jnp.int32)
    partners = partners + jnp.where(tx == 3, NS + (ty > 0).astype(jnp.int32), 0)

    @pl.when(jnp.logical_not(relayed))
    def _():
        pl.semaphore_wait(barrier, partners)

    @pl.when(tx == 3)
    def _():
        pl.semaphore_signal(go, inc=1, device_id={"tx": 2}, device_id_type=MESH)

    upper = me // 4 + lax.rem(me, 4) >= 2

    @pl.when(relayed & mutual & jnp.logical_not(upper))
    def _():
        across()

    @pl.when(relayed)
    def _():
        pl.semaphore_wait(go, 1)

    def id_copy(other):
        return pltpu.make_async_remote_copy(
            src_ref=wanted.at[me],
            dst_ref=wanted.at[me],
            send_sem=id_send,
            recv_sem=id_recv,
            device_id={"shot": other},
            device_id_type=MESH,
        )

    each_partner(lambda other: id_copy(other).start())

    @pl.when(relayed & mutual & upper)
    def _():
        across()

    @pl.when(ty > 0)
    def _():
        answer_first(1)

    @pl.when(tx == 0)
    def _():
        answer_first(2)

    @pl.when(jnp.logical_not(odd) | ((tx == 1) & mutual))
    def _():
        halo_copy(2).start()

    @pl.when(tx == 3)
    def _():
        halo_copy(3).start()

    @pl.when(ty > 0)
    def _():
        halo_copy(1).start()

    def answer(n):
        @pl.when(first[n])
        def _():
            pl.semaphore_wait(ready.at[n], 1)
            halo_copy(n).start()

    loads[4].wait()
    slab[...] = slab_b[...].astype(jnp.float32)

    def serve(shot):
        rows = [slab[wanted_by[shot, 0, 2 * me + k]] for k in range(2)]
        return jnp.concatenate(rows, axis=0).astype(jnp.bfloat16)

    def block_copy(owner, shot):
        return pltpu.make_async_remote_copy(
            src_ref=blocks.at[shot],
            dst_ref=arrived.at[owner],
            send_sem=v_send,
            recv_sem=v_recv.at[me // 4],
            device_id={"shot": shot},
            device_id_type=MESH,
        )

    @pl.loop(0, 2)
    def _(field):
        top, rest = high[field], low[field]
        lap[field] = (
            mm(square[0:ROWS, :], top)
            + mm(square[0:ROWS, :], rest)
            + mm(square[ROWS : 2 * ROWS, :], top)
            + mm(top, square[2 * ROWS : 3 * ROWS, :])
            + mm(rest, square[2 * ROWS : 3 * ROWS, :])
            + mm(top, square[3 * ROWS : 4 * ROWS, :])
        ).reshape(CX, CY, CZ)

    for load in loads[8:]:
        load.wait()
    row = lax.broadcasted_iota(jnp.int32, (ROWS, 1), 0)

    def local_row(along_x, along_y):
        inside = (along_x >= tx * CX) & (along_x < tx * CX + CX)
        inside = inside & (along_y >= ty * CY) & (along_y < ty * CY + CY)
        return jnp.where(inside, (along_x - tx * CX) * CY + along_y - ty * CY, -1)

    source_row = local_row(source_s[0, 0], source_s[0, 1])
    cell_row = local_row(cell_v[0:1, :], cell_v[1:2, :])
    injected = jnp.where(row == source_row, strength_s[0, 0], 0.0)
    recorded = jnp.sum(
        jnp.where(jnp.broadcast_to(row, (ROWS, NREC)) == cell_row, trace_v[...], 0.0),
        axis=1,
        keepdims=True,
    )
    surface = lax.broadcasted_iota(jnp.int32, (ROWS, CZ), 1) == SURFACE_DEPTH

    loads[5].wait()
    pltpu.make_async_copy(prev, prev, load_sem.at[6]).wait()
    answer(0)

    all_but_one = pl.ds(0, NS - 1)
    pltpu.make_async_copy(wanted.at[all_but_one], wanted.at[all_but_one], id_recv).wait()
    table_copy.wait()
    id_local = pltpu.make_async_copy(wanted, wanted_by, table_sem)
    id_local.start()
    id_local.wait()

    @each_partner
    def _(shot):
        blocks[shot] = serve(shot)
        block_copy(me, shot).start()

    arrived[me] = serve(me)
    @pl.when(ty >= 5)
    def _():
        answer(3)

        @pl.when(jnp.logical_not(mutual))
        def _():
            answer(2)

    depth_l = lax.broadcasted_iota(jnp.int32, (CY, ROWS), 1)
    same_y = (depth_l & (CY - 1)) == lax.broadcasted_iota(jnp.int32, (CY, ROWS), 0)
    block_l = jnp.where(same_y, depth_l >> 3, -1)


    @pl.loop(0, NS)
    def _(shot):
        hits = [block_l == wanted_by[shot, 0, 2 * me + k] for k in range(2)]
        rows = pl.ds(pl.multiple_of(shot * 16, 16), 16)
        hit[rows, :] = jnp.where(jnp.concatenate(hits, axis=0), 1.0, 0.0)

    hit_out[...] = hit[...].T.astype(jnp.bfloat16)

    def halo_wait(n):
        @pl.when(sides[(1, 0, 3, 2)[n]][0])
        def _():
            halo_copy(n).wait_recv()

    halo_wait(0)
    halo_wait(1)
    @pl.loop(0, 2)
    def _(field):
        extra = jnp.where(field == 0, injected, recorded)
        layers = halo[field, 0 : 2 * YH]
        beyond = mm(halo_w[0:ROWS, :], layers) + mm(halo_w[ROWS:, :], layers)
        beyond = beyond + jnp.where(surface, jnp.broadcast_to(extra, (ROWS, CZ)), 0.0)
        lap[field] = lap[field] + beyond.reshape(CX, CY, CZ)
        prev[field] = 2.0 * now[field] - prev[field]

    @pl.when(ty < 5)
    def _():
        answer(3)
        answer(2)

    halo_wait(2)

    @pl.when((tx == 1) & direct)
    def _():
        pltpu.make_async_copy(far, far, far_sem.at[1]).wait()

    @pl.when((tx < NTX - 1) & jnp.logical_not((tx == 1) & direct))
    def _():
        halo_copy(3).wait_recv()

    @pl.when(jnp.logical_not((tx == 1) & direct))
    def _():
        far[...] = halo[:, 2 * YH + XH :].astype(jnp.float32).reshape(2, 4, CY, CZ)

    @pl.loop(0, 2)
    def _(field):
        near = halo[field, 2 * YH : 2 * YH + XH].astype(jnp.float32).reshape(4, CY, CZ)
        for q in range(4):
            for x in range(4):
                if x <= q:
                    weight = STENCIL_WEIGHTS[x + 4 - q]
                    lap[field, x] = lap[field, x] + weight * near[q]
                if x >= q:
                    weight = STENCIL_WEIGHTS[4 + q - x]
                    lap[field, CX - 4 + x] = lap[field, CX - 4 + x] + weight * far[field, q]


    def corr_copies(owner):
        return [
            pltpu.make_async_remote_copy(
                src_ref=source.at[owner],
                dst_ref=target.at[me],
                send_sem=c_send.at[n],
                recv_sem=c_recv.at[2 * (me // 8) + n],
                device_id={"shot": owner},
                device_id_type=MESH,
            )
            for n, (source, target) in enumerate(((peak_send, peak_in), (corr_send, corr_in)))
        ]

    def contribute(owner):
        pair = arrived[owner].astype(jnp.float32)
        products = []
        for k in range(2):
            scaled = pair[k * CY : (k + 1) * CY] * STEP_RATIO
            courant = scaled * scaled
            speed[2 * owner + k] = courant
            r = smem_tables[1, 0, 2 * owner + k]
            products.append(
                (prev[0, r] + courant * lap[0, r]) * (prev[1, r] + courant * lap[1, r])
            )
        both = jnp.concatenate(products, axis=0)
        top = jnp.max(jnp.abs(both), axis=0, keepdims=True)
        top = jnp.maximum(jnp.maximum(top[:, : CZ // 2], top[:, CZ // 2 :]), TINY)
        scale = STEPS / top
        code = jnp.round(both * jnp.concatenate([scale, scale], axis=1))
        return top, code.astype(jnp.int32).astype(jnp.int16)

    peak_in[me], corr_in[me] = contribute(me)

    def one_owner(owner):
        peak_send[owner], corr_send[owner] = contribute(owner)
        for copy in corr_copies(owner):
            copy.start()

    def row_of_blocks(x):
        for mine, count in ((x == me // 4, 3), (x != me // 4, 4)):

            @pl.when(mine)
            def _():
                four = arrived.at[pl.ds(4 * x, count)]
                pltpu.make_async_copy(four, four, v_recv.at[x]).wait()

    near = ((tx == 0) | (tx == 3)).astype(jnp.int32)
    each_partner(one_owner, near, row_of_blocks, ((tx == 1) & direct).astype(jnp.int32))

    @pl.loop(0, CX)
    def _(r):
        courant = speed[smem_tables[0, 0, r]]
        for field in range(2):
            prev[field, r] = prev[field, r] + courant * lap[field, r]

    def all_sent(ref, sem):
        pltpu.make_async_copy(ref.at[all_but_one], ref.at[all_but_one], sem).wait()

    all_sent(wanted, id_send)
    all_sent(blocks, v_send)
    for n in range(3):

        @pl.when(sides[n][0])
        def _():
            halo_copy(n).wait_send()

    @pl.when((tx > 0) & jnp.logical_not(relayed & direct))
    def _():
        halo_copy(3).wait_send()

    @pl.when(relayed & direct)
    def _():
        pltpu.make_async_copy(far, far, far_sem.at[0]).wait()

    all_sent(peak_send, c_send.at[0])
    all_sent(corr_send, c_send.at[1])
    def arrive(half, count):
        for n, ref in enumerate((peak_in, corr_in)):
            some = ref.at[pl.ds(0, count)]
            pltpu.make_async_copy(some, some, c_recv.at[2 * half + n]).wait()

    arrive(me // 8, 7)
    part[...] = image_of(me // 8, peak_in, corr_in, hit_out)
    arrive(1 - me // 8, 8)


def image_of(half, peak_in, corr_in, hit):
    shots = pl.ds(8 * half, 8)
    peak = peak_in[shots]
    peak = jnp.broadcast_to(jnp.concatenate([peak, peak], axis=2), (8, 2 * CY, CZ))
    share = corr_in[shots].astype(jnp.int32).astype(jnp.float32) * (1.0 / STEPS)
    rows = (share * peak).reshape(ROWS // 2, CZ)
    top = rows.astype(jnp.bfloat16)
    rest = (rows - top.astype(jnp.float32)).astype(jnp.bfloat16)
    chosen = hit[:, pl.ds(pl.multiple_of(ROWS // 2 * half, ROWS // 2), ROWS // 2)]
    return mm(chosen, top) + mm(chosen, rest)


def finish(values, peak_in, corr_in, hit, part, f_out, a_out, image_out, image, out_sem):
    outs = [
        pltpu.make_async_copy(values.at[0], f_out.at[0], out_sem.at[0]),
        pltpu.make_async_copy(values.at[1], a_out.at[0], out_sem.at[1]),
        pltpu.make_async_copy(image, image_out.at[0], out_sem.at[2]),
    ]
    outs[0].start()
    outs[1].start()
    half = 1 - lax.axis_index("shot") // 8
    total = part[...] + image_of(half, peak_in, corr_in, hit)
    image[...] = total.reshape(SLAB, CY, CZ)
    outs[2].start()
    for out in outs:
        out.wait()


def on_device(*arrays):
    square, halo_w = stencil_constants()
    arrays = (
        *arrays[:7],
        arrays[7].reshape(1, 1),
        jnp.swapaxes(arrays[8], 1, 2),
        arrays[9],
        jnp.asarray(square),
        jnp.asarray(halo_w),
    )
    field = jax.ShapeDtypeStruct((1, CX, CY, CZ), jnp.float32)
    dma = pltpu.SemaphoreType.DMA
    bf, f32, i32 = jnp.bfloat16, jnp.float32, jnp.int32
    scratch = [
        pltpu.VMEM((2, CX, CY, CZ), f32),
        pltpu.VMEM((2, CX, CY, CZ), f32),
        pltpu.VMEM((2, ROWS, CZ), bf),
        pltpu.VMEM((2, ROWS, CZ), bf),
        pltpu.VMEM((2, 4, CY, CZ), f32),
        pltpu.VMEM((2, XH, CZ), bf),
        pltpu.VMEM((2, 4, CY, CZ), f32),
        pltpu.VMEM((SLAB, CY, CZ), bf),
        pltpu.VMEM((SLAB, CY, CZ), f32),
        pltpu.VMEM((1, CX), i32),
        pltpu.VMEM((2, NREC), i32),
        pltpu.VMEM((1, NREC), f32),
        pltpu.VMEM(square.shape, bf),
        pltpu.VMEM(halo_w.shape, bf),
        pltpu.VMEM((2, 2, YH, CZ), bf),
        pltpu.VMEM((2, HALO, CZ), bf),
        pltpu.VMEM((2, 1, 128), i32),
        pltpu.VMEM((NS, 1, 128), i32),
        pltpu.SMEM((NS, 1, 128), i32),
        pltpu.VMEM((NS, 2 * CY, CZ), bf),
        pltpu.VMEM((NS, 2 * CY, CZ), bf),
        pltpu.VMEM((2 * NS, CY, CZ), f32),
        pltpu.VMEM((NS, 1, CZ // 2), f32),
        pltpu.VMEM((NS, 2 * CY, CZ), jnp.int16),
        pltpu.VMEM((ROWS, ROWS), f32),
        pltpu.SMEM((2, 1, 128), i32),
        pltpu.SMEM((1, 2), i32),
        pltpu.SMEM((1, 1), f32),
        dma((10,)),
        dma,
        dma((2,)),
        dma,
        dma,
        dma,
        dma((4,)),
        dma((4,)),
        dma,
        dma((4,)),
        dma((2,)),
        dma((4,)),
        pltpu.SemaphoreType.REGULAR((4,)),
        pltpu.SemaphoreType.REGULAR,
    ]
    anywhere = pl.BlockSpec(memory_space=pl.ANY)
    vmem = pl.BlockSpec(memory_space=pltpu.VMEM)
    results = pl.pallas_call(
        kernel,
        out_shape=(
            jax.ShapeDtypeStruct((2, CX, CY, CZ), f32),
            jax.ShapeDtypeStruct((NS, 1, CZ // 2), f32),
            jax.ShapeDtypeStruct((NS, 2 * CY, CZ), jnp.int16),
            jax.ShapeDtypeStruct((ROWS, ROWS), bf),
            jax.ShapeDtypeStruct((ROWS, CZ), f32),
        ),
        in_specs=[anywhere] * 12,
        out_specs=(vmem,) * 5,
        scratch_shapes=scratch,
        compiler_params=pltpu.CompilerParams(
            collective_id=0, has_side_effects=True, vmem_limit_bytes=LIMIT
        ),
    )(*[a if a.size == 1 else pltpu.with_memory_space_constraint(a, pltpu.HBM) for a in arrays])
    return pl.pallas_call(
        finish,
        out_shape=(field, field, field),
        in_specs=[vmem] * 5,
        out_specs=(anywhere,) * 3,
        scratch_shapes=[pltpu.VMEM((SLAB, CY, CZ), f32), dma((3,))],
        compiler_params=pltpu.CompilerParams(vmem_limit_bytes=LIMIT),
    )(*results)


def solution(mesh):
    in_specs = (
        P("shot", "tx", "ty", None),
        P("shot", "tx", "ty", None),
        P("shot", "tx", "ty", None),
        P("shot", "tx", "ty", None),
        P(("tx", "ty"), "shot", None, None),
        P("shot", ("tx", "ty"), None),
        P("shot", None),
        P("shot"),
        P("shot", None, None),
        P("shot", None),
    )
    out_specs = (
        P("shot", "tx", "ty", None),
        P("shot", "tx", "ty", None),
        P(("tx", "ty"), "shot", None, None),
    )
    return jax.shard_map(
        on_device, mesh=mesh, in_specs=in_specs, out_specs=out_specs, check_vma=False
    )
```

```python
import functools

import jax
import jax.numpy as jnp
import ml_dtypes
import numpy as np
from jax import lax
from jax.experimental import pallas as pl
from jax.experimental.pallas import tpu as pltpu
from jax.sharding import PartitionSpec as P

SURFACE_DEPTH = 8
STENCIL_WEIGHTS = (-205.0 / 72.0, 8.0 / 5.0, -1.0 / 5.0, 8.0 / 315.0, -1.0 / 560.0)
STEP_RATIO = 0.1
MESH = pl.DeviceIdType.MESH
NS, NTX, NTY = 16, 4, 8
CX, CY, CZ = 32, 8, 256
ROWS = CX * CY
SLAB = 32
NREC = 128
YH = CX * 4
XH = 4 * CY
HALO = 2 * YH + 2 * XH
STEPS = 32766.0
TINY = 1e-34
DIRECT = 1
LATE = 6
LIMIT = 40 * 1024 * 1024


def stencil_constants():
    w = np.array(STENCIL_WEIGHTS)
    band = np.zeros(600)
    band[1:5] = w[1:]
    row = np.arange(ROWS)
    x, y = row // CY, row % CY
    dx, dy = np.abs(x[:, None] - x[None, :]), np.abs(y[:, None] - y[None, :])
    inner = band[dx] * (dy == 0) + band[dy] * (dx == 0) + 3.0 * w[0] * ((dx == 0) & (dy == 0))
    z = np.arange(CZ)
    depth = band[np.abs(z[:, None] - z[None, :])]
    pick = np.zeros((ROWS, ROWS))
    halo = np.zeros((ROWS, 2 * YH))
    for cx in range(CX):
        for q in range(4):
            pick[cx * 4 + q, cx * CY + CY - 4 + q] = 1.0
            pick[YH + cx * 4 + q, cx * CY + q] = 1.0
            for cy in range(CY):
                halo[cx * CY + cy, cx * 4 + q] = band[cy + 4 - q]
                halo[cx * CY + cy, YH + cx * 4 + q] = band[CY + q - cy]

    def parts(matrix):
        high = matrix.astype(np.float32).astype(ml_dtypes.bfloat16)
        low = (matrix - high.astype(np.float64)).astype(np.float32).astype(ml_dtypes.bfloat16)
        return [high, low]

    square = np.concatenate(parts(inner) + parts(depth) + parts(pick)[:1], axis=0)
    return square, np.concatenate(parts(halo), axis=0)


def each_partner(body, near=0, row=None, up=0):
    me = lax.axis_index("shot")
    turn_x = (me < NS // 2).astype(jnp.int32)
    turn_y = (lax.rem(me, 4) < 2).astype(jnp.int32)
    turn_x = turn_x + near * (1 - 2 * turn_x)
    turn_y = turn_y + near * (1 - 2 * turn_y)
    turn_x, turn_y = turn_x * (1 - up), turn_y * (1 - up)
    corner, step_x, step_y = 12 * turn_x + 3 * turn_y, 4 - 8 * turn_x, 1 - 2 * turn_y

    @pl.loop(0, 4)
    def _(i):
        if row is not None:
            row(3 * turn_x + (1 - 2 * turn_x) * i)

        for j in range(4):
            other = corner + step_x * i + step_y * j

            @pl.when(other != me)
            def _():
                body(other)


def mm(a, b):
    return jnp.dot(a, b, preferred_element_type=jnp.float32)


def kernel(
    f_prev, f_now, a_prev, a_now, velocity, aperture, source_cell, strength, receivers, traces,
    square_hbm, halo_hbm,
    prev, peak_in, corr_in, hit_out, part,
    now, lap, high, low, edge_f, edge, far, slab_b, slab, ids, cell_v, trace_v, square, halo_w,
    pick_send, halo, tables, wanted, wanted_by, blocks, arrived, speed, peak_send, corr_send,
    hit,
    smem_tables, source_s, strength_s,
    load_sem, edge_sem, far_sem, table_sem, id_send, id_recv, halo_send, halo_recv, v_send, v_recv,
    c_send, c_recv, ready, go,
):
    me = lax.axis_index("shot")
    tx = lax.axis_index("tx")
    ty = lax.axis_index("ty")

    loads = [
        pltpu.make_async_copy(aperture.at[0], ids, load_sem.at[0]),
        pltpu.make_async_copy(f_now.at[0], now.at[0], load_sem.at[1]),
        pltpu.make_async_copy(a_now.at[0], now.at[1], load_sem.at[1]),
        pltpu.make_async_copy(square_hbm, square, load_sem.at[3]),
        pltpu.make_async_copy(velocity.at[0], slab_b, load_sem.at[4]),
        pltpu.make_async_copy(halo_hbm, halo_w, load_sem.at[5]),
        pltpu.make_async_copy(f_prev.at[0], prev.at[0], load_sem.at[6]),
        pltpu.make_async_copy(a_prev.at[0], prev.at[1], load_sem.at[6]),
        pltpu.make_async_copy(receivers.at[0], cell_v, load_sem.at[8]),
        pltpu.make_async_copy(traces, trace_v, load_sem.at[9]),
        pltpu.make_async_copy(source_cell, source_s, load_sem.at[2]),
        pltpu.make_async_copy(strength, strength_s, load_sem.at[7]),
    ]
    edge_loads = [
        pltpu.make_async_copy(now_hbm.at[0, 0:4], edge_f.at[field], edge_sem)
        for field, now_hbm in enumerate((f_now, a_now))
    ]

    direct = ty < DIRECT

    @pl.when((tx == 2) & jnp.logical_not(direct))
    def _():
        edge_loads[0].start()
        edge_loads[1].start()

    for n in (0, 1, 2, 4):
        loads[n].start()

    relayed = tx == 2
    home = tx + relayed.astype(jnp.int32)
    odd = lax.rem(tx, 2) == 1
    sides = [
        (ty < NTY - 1, "ty", ty + 1),
        (ty > 0, "ty", ty - 1),
        (tx < NTX - 1, "tx", tx + 1),
        (tx > 0, "tx", tx - 1),
    ]
    first = [ty < NTY - 1, None, tx == 1, tx == 1]

    barrier = pltpu.get_barrier_semaphore()

    mutual = ty >= LATE
    for n, says in ((2, first[2]), (3, first[3] | (relayed & mutual))):

        @pl.when(says)
        def _():
            pl.semaphore_signal(
                barrier, inc=1, device_id={"tx": sides[n][2]}, device_id_type=MESH
            )

    def answer_first(n):
        axis, other = sides[n][1:]
        pl.semaphore_signal(
            ready.at[(1, 0, 3, 2)[n]], inc=1, device_id={axis: other}, device_id_type=MESH
        )

    def far_copy(field, x):
        return pltpu.make_async_remote_copy(
            src_ref=(f_now, a_now)[field].at[0, x],
            dst_ref=far.at[field, x],
            send_sem=far_sem.at[0],
            recv_sem=far_sem.at[1],
            device_id={"tx": tx - 1},
            device_id_type=MESH,
        )

    @pl.when(relayed & direct)
    def _():
        pl.semaphore_wait(barrier, 1)
        for x in range(4):
            far_copy(0, x).start()
            far_copy(1, x).start()
        answer_first(3)

    @pl.loop(1 - relayed.astype(jnp.int32), NS)
    def _(d):
        pl.semaphore_signal(
            barrier,
            inc=1,
            device_id={"shot": lax.rem(me + d, NS), "tx": home},
            device_id_type=MESH,
        )

    @pl.when(first[0])
    def _():
        pl.semaphore_signal(
            barrier, inc=1, device_id={"tx": home, "ty": ty + 1}, device_id_type=MESH
        )

    for n in (3, 5, 6, 7, 8, 9, 10, 11):
        loads[n].start()

    for present, start, size in (
        (ty > 0, 0, YH),
        (ty < NTY - 1, YH, YH),
        (tx > 0, 2 * YH, XH),
        (tx < NTX - 1, 2 * YH + XH, XH),
    ):

        @pl.when(jnp.logical_not(present))
        def _():
            halo[:, start : start + size, :] = jnp.zeros((2, size, CZ), jnp.bfloat16)

    def halo_copy(n, source=None):
        axis, other = sides[n][1], sides[n][2]
        start = (0, YH, 2 * YH, 2 * YH + XH)[n]
        size = YH if n < 2 else XH
        if source is None and n < 2:
            source = pick_send.at[n]
        elif source is None:
            source = high.at[:, pl.ds((CX - 4) * CY if n == 2 else 0, XH)]
        return pltpu.make_async_remote_copy(
            src_ref=source,
            dst_ref=halo.at[:, pl.ds(start, size)],
            send_sem=halo_send.at[n],
            recv_sem=halo_recv.at[n],
            device_id={axis: other},
            device_id_type=MESH,
        )

    def across():
        pl.semaphore_wait(barrier, 1)

        @pl.when(jnp.logical_not(mutual))
        def _():
            answer_first(3)

        halo_copy(3, edge).start()

    @pl.when(relayed & jnp.logical_not(direct))
    def _():
        pltpu.make_async_copy(edge_f, edge_f, edge_sem).wait()
        edge[...] = edge_f[...].reshape(2, XH, CZ).astype(jnp.bfloat16)

    @pl.when(relayed & (ty >= DIRECT) & jnp.logical_not(mutual))
    def _():
        across()

    pltpu.make_async_copy(now, now, load_sem.at[1]).wait()

    @pl.loop(0, 2)
    def _(field):
        u = now[field].reshape(ROWS, CZ)
        top = u.astype(jnp.bfloat16)
        high[field] = top
        low[field] = (u - top.astype(jnp.float32)).astype(jnp.bfloat16)

    loads[0].wait()
    row_l = lax.broadcasted_iota(jnp.int32, (CX, CX), 1)
    row_s = lax.broadcasted_iota(jnp.int32, (CX, CX), 0)
    ids_l = jnp.broadcast_to(ids[...], (CX, CX))
    ids_s = ids_l.T
    earlier = ((ids_s >> 5) == (ids_l >> 5)) & (row_s < row_l)
    rank = jnp.sum(earlier.astype(jnp.int32), axis=0, keepdims=True)
    slot = 2 * (ids[...] >> 5) + rank
    placed = jnp.broadcast_to(slot, (CX, CX)).T == row_l
    tables[0, :, 0:CX] = slot
    tables[1, :, 0:CX] = jnp.sum(jnp.where(placed, row_s, 0), axis=0, keepdims=True)
    wanted[me, :, 0:CX] = jnp.sum(jnp.where(placed, ids_s & (SLAB - 1), 0), axis=0, keepdims=True)
    table_copy = pltpu.make_async_copy(tables, smem_tables, table_sem)
    table_copy.start()

    loads[3].wait()

    @pl.loop(0, 2)
    def _(field):
        picked = mm(square[4 * ROWS : 5 * ROWS, :], high[field]).astype(jnp.bfloat16)
        pick_send[0, field] = picked[0:YH]
        pick_send[1, field] = picked[YH:]

    partners = NS - 1 + (ty > 0).astype(jnp.int32) + (tx == 0).astype(jnp.int32)
    partners = partners + ((tx == 1) & mutual).astype(jnp.int32)
    partners = partners + jnp.where(tx == 3, NS + (ty > 0).astype(jnp.int32), 0)

    @pl.when(jnp.logical_not(relayed))
    def _():
        pl.semaphore_wait(barrier, partners)

    @pl.when(tx == 3)
    def _():
        pl.semaphore_signal(go, inc=1, device_id={"tx": 2}, device_id_type=MESH)

    upper = me // 4 + lax.rem(me, 4) >= 2

    @pl.when(relayed & mutual & jnp.logical_not(upper))
    def _():
        across()

    @pl.when(relayed)
    def _():
        pl.semaphore_wait(go, 1)

    def id_copy(other):
        return pltpu.make_async_remote_copy(
            src_ref=wanted.at[me],
            dst_ref=wanted.at[me],
            send_sem=id_send,
            recv_sem=id_recv,
            device_id={"shot": other},
            device_id_type=MESH,
        )

    each_partner(lambda other: id_copy(other).start())

    @pl.when(relayed & mutual & upper)
    def _():
        across()

    @pl.when(ty > 0)
    def _():
        answer_first(1)

    @pl.when(tx == 0)
    def _():
        answer_first(2)

    @pl.when(jnp.logical_not(odd) | ((tx == 1) & mutual))
    def _():
        halo_copy(2).start()

    @pl.when(tx == 3)
    def _():
        halo_copy(3).start()

    @pl.when(ty > 0)
    def _():
        halo_copy(1).start()

    def answer(n):
        @pl.when(first[n])
        def _():
            pl.semaphore_wait(ready.at[n], 1)
            halo_copy(n).start()

    loads[4].wait()
    slab[...] = slab_b[...].astype(jnp.float32)

    def serve(shot):
        rows = [slab[wanted_by[shot, 0, 2 * me + k]] for k in range(2)]
        return jnp.concatenate(rows, axis=0).astype(jnp.bfloat16)

    def block_copy(owner, shot):
        return pltpu.make_async_remote_copy(
            src_ref=blocks.at[shot],
            dst_ref=arrived.at[owner],
            send_sem=v_send,
            recv_sem=v_recv.at[me // 4],
            device_id={"shot": shot},
            device_id_type=MESH,
        )

    @pl.loop(0, 2)
    def _(field):
        top, rest = high[field], low[field]
        lap[field] = (
            mm(square[0:ROWS, :], top)
            + mm(square[0:ROWS, :], rest)
            + mm(square[ROWS : 2 * ROWS, :], top)
            + mm(top, square[2 * ROWS : 3 * ROWS, :])
            + mm(rest, square[2 * ROWS : 3 * ROWS, :])
            + mm(top, square[3 * ROWS : 4 * ROWS, :])
        ).reshape(CX, CY, CZ)

    for load in loads[8:]:
        load.wait()
    row = lax.broadcasted_iota(jnp.int32, (ROWS, 1), 0)

    def local_row(along_x, along_y):
        inside = (along_x >= tx * CX) & (along_x < tx * CX + CX)
        inside = inside & (along_y >= ty * CY) & (along_y < ty * CY + CY)
        return jnp.where(inside, (along_x - tx * CX) * CY + along_y - ty * CY, -1)

    source_row = local_row(source_s[0, 0], source_s[0, 1])
    cell_row = local_row(cell_v[0:1, :], cell_v[1:2, :])
    injected = jnp.where(row == source_row, strength_s[0, 0], 0.0)
    recorded = jnp.sum(
        jnp.where(jnp.broadcast_to(row, (ROWS, NREC)) == cell_row, trace_v[...], 0.0),
        axis=1,
        keepdims=True,
    )
    surface = lax.broadcasted_iota(jnp.int32, (ROWS, CZ), 1) == SURFACE_DEPTH

    loads[5].wait()
    pltpu.make_async_copy(prev, prev, load_sem.at[6]).wait()
    answer(0)

    all_but_one = pl.ds(0, NS - 1)
    pltpu.make_async_copy(wanted.at[all_but_one], wanted.at[all_but_one], id_recv).wait()
    table_copy.wait()
    id_local = pltpu.make_async_copy(wanted, wanted_by, table_sem)
    id_local.start()
    id_local.wait()

    @each_partner
    def _(shot):
        blocks[shot] = serve(shot)
        block_copy(me, shot).start()

    arrived[me] = serve(me)
    @pl.when(ty >= 5)
    def _():
        answer(3)

        @pl.when(jnp.logical_not(mutual))
        def _():
            answer(2)

    depth_l = lax.broadcasted_iota(jnp.int32, (CY, ROWS), 1)
    same_y = (depth_l & (CY - 1)) == lax.broadcasted_iota(jnp.int32, (CY, ROWS), 0)
    block_l = jnp.where(same_y, depth_l >> 3, -1)


    @pl.loop(0, NS)
    def _(shot):
        hits = [block_l == wanted_by[shot, 0, 2 * me + k] for k in range(2)]
        rows = pl.ds(pl.multiple_of(shot * 16, 16), 16)
        hit[rows, :] = jnp.where(jnp.concatenate(hits, axis=0), 1.0, 0.0)

    hit_out[...] = hit[...].T.astype(jnp.bfloat16)

    def halo_wait(n):
        @pl.when(sides[(1, 0, 3, 2)[n]][0])
        def _():
            halo_copy(n).wait_recv()

    halo_wait(0)
    halo_wait(1)
    @pl.loop(0, 2)
    def _(field):
        extra = jnp.where(field == 0, injected, recorded)
        layers = halo[field, 0 : 2 * YH]
        beyond = mm(halo_w[0:ROWS, :], layers) + mm(halo_w[ROWS:, :], layers)
        beyond = beyond + jnp.where(surface, jnp.broadcast_to(extra, (ROWS, CZ)), 0.0)
        lap[field] = lap[field] + beyond.reshape(CX, CY, CZ)
        prev[field] = 2.0 * now[field] - prev[field]

    @pl.when(ty < 5)
    def _():
        answer(3)
        answer(2)

    halo_wait(2)

    @pl.when((tx == 1) & direct)
    def _():
        pltpu.make_async_copy(far, far, far_sem.at[1]).wait()

    @pl.when((tx < NTX - 1) & jnp.logical_not((tx == 1) & direct))
    def _():
        halo_copy(3).wait_recv()

    @pl.when(jnp.logical_not((tx == 1) & direct))
    def _():
        far[...] = halo[:, 2 * YH + XH :].astype(jnp.float32).reshape(2, 4, CY, CZ)

    @pl.loop(0, 2)
    def _(field):
        near = halo[field, 2 * YH : 2 * YH + XH].astype(jnp.float32).reshape(4, CY, CZ)
        for q in range(4):
            for x in range(4):
                if x <= q:
                    weight = STENCIL_WEIGHTS[x + 4 - q]
                    lap[field, x] = lap[field, x] + weight * near[q]
                if x >= q:
                    weight = STENCIL_WEIGHTS[4 + q - x]
                    lap[field, CX - 4 + x] = lap[field, CX - 4 + x] + weight * far[field, q]


    def corr_copies(owner):
        return [
            pltpu.make_async_remote_copy(
                src_ref=source.at[owner],
                dst_ref=target.at[me],
                send_sem=c_send.at[n],
                recv_sem=c_recv.at[2 * (me // 8) + n],
                device_id={"shot": owner},
                device_id_type=MESH,
            )
            for n, (source, target) in enumerate(((peak_send, peak_in), (corr_send, corr_in)))
        ]

    def contribute(owner):
        pair = arrived[owner].astype(jnp.float32)
        products = []
        for k in range(2):
            scaled = pair[k * CY : (k + 1) * CY] * STEP_RATIO
            courant = scaled * scaled
            speed[2 * owner + k] = courant
            r = smem_tables[1, 0, 2 * owner + k]
            products.append(
                (prev[0, r] + courant * lap[0, r]) * (prev[1, r] + courant * lap[1, r])
            )
        both = jnp.concatenate(products, axis=0)
        top = jnp.max(jnp.abs(both), axis=0, keepdims=True)
        top = jnp.maximum(jnp.maximum(top[:, : CZ // 2], top[:, CZ // 2 :]), TINY)
        scale = STEPS / top
        code = jnp.round(both * jnp.concatenate([scale, scale], axis=1))
        return top, code.astype(jnp.int32).astype(jnp.int16)

    peak_in[me], corr_in[me] = contribute(me)

    def one_owner(owner):
        peak_send[owner], corr_send[owner] = contribute(owner)
        for copy in corr_copies(owner):
            copy.start()

    def row_of_blocks(x):
        for mine, count in ((x == me // 4, 3), (x != me // 4, 4)):

            @pl.when(mine)
            def _():
                four = arrived.at[pl.ds(4 * x, count)]
                pltpu.make_async_copy(four, four, v_recv.at[x]).wait()

    near = ((tx == 0) | (tx == 3)).astype(jnp.int32)
    each_partner(one_owner, near, row_of_blocks, ((tx == 1) & direct).astype(jnp.int32))

    @pl.loop(0, CX)
    def _(r):
        courant = speed[smem_tables[0, 0, r]]
        for field in range(2):
            prev[field, r] = prev[field, r] + courant * lap[field, r]

    def all_sent(ref, sem):
        pltpu.make_async_copy(ref.at[all_but_one], ref.at[all_but_one], sem).wait()

    all_sent(wanted, id_send)
    all_sent(blocks, v_send)
    for n in range(3):

        @pl.when(sides[n][0])
        def _():
            halo_copy(n).wait_send()

    @pl.when((tx > 0) & jnp.logical_not(relayed & direct))
    def _():
        halo_copy(3).wait_send()

    @pl.when(relayed & direct)
    def _():
        pltpu.make_async_copy(far, far, far_sem.at[0]).wait()

    all_sent(peak_send, c_send.at[0])
    all_sent(corr_send, c_send.at[1])
    def arrive(half, count):
        for n, ref in enumerate((peak_in, corr_in)):
            some = ref.at[pl.ds(0, count)]
            pltpu.make_async_copy(some, some, c_recv.at[2 * half + n]).wait()

    arrive(me // 8, 7)
    part[...] = image_of(me // 8, peak_in, corr_in, hit_out)
    arrive(1 - me // 8, 8)


def image_of(half, peak_in, corr_in, hit):
    shots = pl.ds(8 * half, 8)
    peak = peak_in[shots]
    peak = jnp.broadcast_to(jnp.concatenate([peak, peak], axis=2), (8, 2 * CY, CZ))
    share = corr_in[shots].astype(jnp.int32).astype(jnp.float32) * (1.0 / STEPS)
    rows = (share * peak).reshape(ROWS // 2, CZ)
    top = rows.astype(jnp.bfloat16)
    rest = (rows - top.astype(jnp.float32)).astype(jnp.bfloat16)
    chosen = hit[:, pl.ds(pl.multiple_of(ROWS // 2 * half, ROWS // 2), ROWS // 2)]
    return mm(chosen, top) + mm(chosen, rest)


def finish(values, peak_in, corr_in, hit, part, f_out, a_out, image_out, image, out_sem):
    def write(n, source, target):
        for part_of in range(4):
            rows = pl.ds(8 * part_of, 8)
            pltpu.make_async_copy(source.at[rows], target.at[0, rows], out_sem.at[n]).start()

    write(0, values.at[0], f_out)
    write(1, values.at[1], a_out)
    half = 1 - lax.axis_index("shot") // 8
    total = part[...] + image_of(half, peak_in, corr_in, hit)
    image[...] = total.reshape(SLAB, CY, CZ)
    write(2, image, image_out)
    for n, target in enumerate((f_out, a_out, image_out)):
        pltpu.make_async_copy(image, target.at[0], out_sem.at[n]).wait()


def on_device(*arrays):
    square, halo_w = stencil_constants()
    arrays = (
        *arrays[:7],
        arrays[7].reshape(1, 1),
        jnp.swapaxes(arrays[8], 1, 2),
        arrays[9],
        jnp.asarray(square),
        jnp.asarray(halo_w),
    )
    field = jax.ShapeDtypeStruct((1, CX, CY, CZ), jnp.float32)
    dma = pltpu.SemaphoreType.DMA
    bf, f32, i32 = jnp.bfloat16, jnp.float32, jnp.int32
    scratch = [
        pltpu.VMEM((2, CX, CY, CZ), f32),
        pltpu.VMEM((2, CX, CY, CZ), f32),
        pltpu.VMEM((2, ROWS, CZ), bf),
        pltpu.VMEM((2, ROWS, CZ), bf),
        pltpu.VMEM((2, 4, CY, CZ), f32),
        pltpu.VMEM((2, XH, CZ), bf),
        pltpu.VMEM((2, 4, CY, CZ), f32),
        pltpu.VMEM((SLAB, CY, CZ), bf),
        pltpu.VMEM((SLAB, CY, CZ), f32),
        pltpu.VMEM((1, CX), i32),
        pltpu.VMEM((2, NREC), i32),
        pltpu.VMEM((1, NREC), f32),
        pltpu.VMEM(square.shape, bf),
        pltpu.VMEM(halo_w.shape, bf),
        pltpu.VMEM((2, 2, YH, CZ), bf),
        pltpu.VMEM((2, HALO, CZ), bf),
        pltpu.VMEM((2, 1, 128), i32),
        pltpu.VMEM((NS, 1, 128), i32),
        pltpu.SMEM((NS, 1, 128), i32),
        pltpu.VMEM((NS, 2 * CY, CZ), bf),
        pltpu.VMEM((NS, 2 * CY, CZ), bf),
        pltpu.VMEM((2 * NS, CY, CZ), f32),
        pltpu.VMEM((NS, 1, CZ // 2), f32),
        pltpu.VMEM((NS, 2 * CY, CZ), jnp.int16),
        pltpu.VMEM((ROWS, ROWS), f32),
        pltpu.SMEM((2, 1, 128), i32),
        pltpu.SMEM((1, 2), i32),
        pltpu.SMEM((1, 1), f32),
        dma((10,)),
        dma,
        dma((2,)),
        dma,
        dma,
        dma,
        dma((4,)),
        dma((4,)),
        dma,
        dma((4,)),
        dma((2,)),
        dma((4,)),
        pltpu.SemaphoreType.REGULAR((4,)),
        pltpu.SemaphoreType.REGULAR,
    ]
    anywhere = pl.BlockSpec(memory_space=pl.ANY)
    vmem = pl.BlockSpec(memory_space=pltpu.VMEM)
    results = pl.pallas_call(
        kernel,
        out_shape=(
            jax.ShapeDtypeStruct((2, CX, CY, CZ), f32),
            jax.ShapeDtypeStruct((NS, 1, CZ // 2), f32),
            jax.ShapeDtypeStruct((NS, 2 * CY, CZ), jnp.int16),
            jax.ShapeDtypeStruct((ROWS, ROWS), bf),
            jax.ShapeDtypeStruct((ROWS, CZ), f32),
        ),
        in_specs=[anywhere] * 12,
        out_specs=(vmem,) * 5,
        scratch_shapes=scratch,
        compiler_params=pltpu.CompilerParams(
            collective_id=0, has_side_effects=True, vmem_limit_bytes=LIMIT
        ),
    )(*[a if a.size == 1 else pltpu.with_memory_space_constraint(a, pltpu.HBM) for a in arrays])
    return pl.pallas_call(
        finish,
        out_shape=(field, field, field),
        in_specs=[vmem] * 5,
        out_specs=(anywhere,) * 3,
        scratch_shapes=[pltpu.VMEM((SLAB, CY, CZ), f32), dma((3,))],
        compiler_params=pltpu.CompilerParams(vmem_limit_bytes=LIMIT),
    )(*results)


def solution(mesh):
    in_specs = (
        P("shot", "tx", "ty", None),
        P("shot", "tx", "ty", None),
        P("shot", "tx", "ty", None),
        P("shot", "tx", "ty", None),
        P(("tx", "ty"), "shot", None, None),
        P("shot", ("tx", "ty"), None),
        P("shot", None),
        P("shot"),
        P("shot", None, None),
        P("shot", None),
    )
    out_specs = (
        P("shot", "tx", "ty", None),
        P("shot", "tx", "ty", None),
        P(("tx", "ty"), "shot", None, None),
    )
    return jax.shard_map(
        on_device, mesh=mesh, in_specs=in_specs, out_specs=out_specs, check_vma=False
    )
```

```python
import functools

import jax
import jax.numpy as jnp
import ml_dtypes
import numpy as np
from jax import lax
from jax.experimental import pallas as pl
from jax.experimental.pallas import tpu as pltpu
from jax.sharding import PartitionSpec as P

SURFACE_DEPTH = 8
STENCIL_WEIGHTS = (-205.0 / 72.0, 8.0 / 5.0, -1.0 / 5.0, 8.0 / 315.0, -1.0 / 560.0)
STEP_RATIO = 0.1
MESH = pl.DeviceIdType.MESH
NS, NTX, NTY = 16, 4, 8
CX, CY, CZ = 32, 8, 256
ROWS = CX * CY
SLAB = 32
NREC = 128
YH = CX * 4
XH = 4 * CY
HALO = 2 * YH + 2 * XH
STEPS = 32766.0
TINY = 1e-34
DIRECT = 1
LATE = 6
LIMIT = 40 * 1024 * 1024


def stencil_constants():
    w = np.array(STENCIL_WEIGHTS)
    band = np.zeros(600)
    band[1:5] = w[1:]
    row = np.arange(ROWS)
    x, y = row // CY, row % CY
    dx, dy = np.abs(x[:, None] - x[None, :]), np.abs(y[:, None] - y[None, :])
    inner = band[dx] * (dy == 0) + band[dy] * (dx == 0) + 3.0 * w[0] * ((dx == 0) & (dy == 0))
    z = np.arange(CZ)
    depth = band[np.abs(z[:, None] - z[None, :])]
    pick = np.zeros((ROWS, ROWS))
    halo = np.zeros((ROWS, 2 * YH))
    for cx in range(CX):
        for q in range(4):
            pick[cx * 4 + q, cx * CY + CY - 4 + q] = 1.0
            pick[YH + cx * 4 + q, cx * CY + q] = 1.0
            for cy in range(CY):
                halo[cx * CY + cy, cx * 4 + q] = band[cy + 4 - q]
                halo[cx * CY + cy, YH + cx * 4 + q] = band[CY + q - cy]

    def parts(matrix):
        high = matrix.astype(np.float32).astype(ml_dtypes.bfloat16)
        low = (matrix - high.astype(np.float64)).astype(np.float32).astype(ml_dtypes.bfloat16)
        return [high, low]

    square = np.concatenate(parts(inner) + parts(depth) + parts(pick)[:1], axis=0)
    return square, np.concatenate(parts(halo), axis=0)


def each_partner(body, near=0, row=None, up=0):
    me = lax.axis_index("shot")
    turn_x = (me < NS // 2).astype(jnp.int32)
    turn_y = (lax.rem(me, 4) < 2).astype(jnp.int32)
    turn_x = turn_x + near * (1 - 2 * turn_x)
    turn_y = turn_y + near * (1 - 2 * turn_y)
    turn_x, turn_y = turn_x * (1 - up), turn_y * (1 - up)
    corner, step_x, step_y = 12 * turn_x + 3 * turn_y, 4 - 8 * turn_x, 1 - 2 * turn_y

    @pl.loop(0, 4)
    def _(i):
        if row is not None:
            row(3 * turn_x + (1 - 2 * turn_x) * i)

        for j in range(4):
            other = corner + step_x * i + step_y * j

            @pl.when(other != me)
            def _():
                body(other)


def mm(a, b):
    return jnp.dot(a, b, preferred_element_type=jnp.float32)


def kernel(
    f_prev, f_now, a_prev, a_now, velocity, aperture, source_cell, strength, receivers, traces,
    square_hbm, halo_hbm,
    prev, peak_in, corr_in, hit_out, part,
    now, lap, high, low, edge_f, edge, far, slab_b, slab, ids, cell_v, trace_v, square, halo_w,
    pick_send, halo, tables, wanted, wanted_by, blocks, arrived, speed, peak_send, corr_send,
    hit,
    smem_tables, source_s, strength_s,
    load_sem, edge_sem, far_sem, table_sem, id_send, id_recv, halo_send, halo_recv, v_send, v_recv,
    c_send, c_recv, ready, go,
):
    me = lax.axis_index("shot")
    tx = lax.axis_index("tx")
    ty = lax.axis_index("ty")

    loads = [
        pltpu.make_async_copy(aperture.at[0], ids, load_sem.at[0]),
        pltpu.make_async_copy(f_now.at[0], now.at[0], load_sem.at[1]),
        pltpu.make_async_copy(a_now.at[0], now.at[1], load_sem.at[1]),
        pltpu.make_async_copy(square_hbm, square, load_sem.at[3]),
        pltpu.make_async_copy(velocity.at[0], slab_b, load_sem.at[4]),
        pltpu.make_async_copy(halo_hbm, halo_w, load_sem.at[5]),
        pltpu.make_async_copy(f_prev.at[0], prev.at[0], load_sem.at[6]),
        pltpu.make_async_copy(a_prev.at[0], prev.at[1], load_sem.at[6]),
        pltpu.make_async_copy(receivers.at[0], cell_v, load_sem.at[8]),
        pltpu.make_async_copy(traces, trace_v, load_sem.at[9]),
        pltpu.make_async_copy(source_cell, source_s, load_sem.at[2]),
        pltpu.make_async_copy(strength, strength_s, load_sem.at[7]),
    ]
    edge_loads = [
        pltpu.make_async_copy(now_hbm.at[0, 0:4], edge_f.at[field], edge_sem)
        for field, now_hbm in enumerate((f_now, a_now))
    ]

    direct = ty < DIRECT

    @pl.when((tx == 2) & jnp.logical_not(direct))
    def _():
        edge_loads[0].start()
        edge_loads[1].start()

    for n in (0, 1, 2, 4):
        loads[n].start()

    relayed = tx == 2
    home = tx + relayed.astype(jnp.int32)
    odd = lax.rem(tx, 2) == 1
    sides = [
        (ty < NTY - 1, "ty", ty + 1),
        (ty > 0, "ty", ty - 1),
        (tx < NTX - 1, "tx", tx + 1),
        (tx > 0, "tx", tx - 1),
    ]
    first = [ty < NTY - 1, None, tx == 1, tx == 1]

    barrier = pltpu.get_barrier_semaphore()

    mutual = ty >= LATE
    for n, says in ((2, first[2]), (3, first[3] | (relayed & mutual))):

        @pl.when(says)
        def _():
            pl.semaphore_signal(
                barrier, inc=1, device_id={"tx": sides[n][2]}, device_id_type=MESH
            )

    def answer_first(n):
        axis, other = sides[n][1:]
        pl.semaphore_signal(
            ready.at[(1, 0, 3, 2)[n]], inc=1, device_id={axis: other}, device_id_type=MESH
        )

    def far_copy(field, x):
        return pltpu.make_async_remote_copy(
            src_ref=(f_now, a_now)[field].at[0, x],
            dst_ref=far.at[field, x],
            send_sem=far_sem.at[0],
            recv_sem=far_sem.at[1],
            device_id={"tx": tx - 1},
            device_id_type=MESH,
        )

    @pl.when(relayed & direct)
    def _():
        pl.semaphore_wait(barrier, 1)
        for x in range(4):
            far_copy(0, x).start()
            far_copy(1, x).start()
        answer_first(3)

    @pl.loop(1 - relayed.astype(jnp.int32), NS)
    def _(d):
        pl.semaphore_signal(
            barrier,
            inc=1,
            device_id={"shot": lax.rem(me + d, NS), "tx": home},
            device_id_type=MESH,
        )

    @pl.when(first[0])
    def _():
        pl.semaphore_signal(
            barrier, inc=1, device_id={"tx": home, "ty": ty + 1}, device_id_type=MESH
        )

    for n in (3, 5, 6, 7, 8, 9, 10, 11):
        loads[n].start()

    for present, start, size in (
        (ty > 0, 0, YH),
        (ty < NTY - 1, YH, YH),
        (tx > 0, 2 * YH, XH),
        (tx < NTX - 1, 2 * YH + XH, XH),
    ):

        @pl.when(jnp.logical_not(present))
        def _():
            halo[:, start : start + size, :] = jnp.zeros((2, size, CZ), jnp.bfloat16)

    def halo_copy(n, source=None):
        axis, other = sides[n][1], sides[n][2]
        start = (0, YH, 2 * YH, 2 * YH + XH)[n]
        size = YH if n < 2 else XH
        if source is None and n < 2:
            source = pick_send.at[n]
        elif source is None:
            source = high.at[:, pl.ds((CX - 4) * CY if n == 2 else 0, XH)]
        return pltpu.make_async_remote_copy(
            src_ref=source,
            dst_ref=halo.at[:, pl.ds(start, size)],
            send_sem=halo_send.at[n],
            recv_sem=halo_recv.at[n],
            device_id={axis: other},
            device_id_type=MESH,
        )

    def across():
        pl.semaphore_wait(barrier, 1)

        @pl.when(jnp.logical_not(mutual))
        def _():
            answer_first(3)

        halo_copy(3, edge).start()

    @pl.when(relayed & jnp.logical_not(direct))
    def _():
        pltpu.make_async_copy(edge_f, edge_f, edge_sem).wait()
        edge[...] = edge_f[...].reshape(2, XH, CZ).astype(jnp.bfloat16)

    pltpu.make_async_copy(now, now, load_sem.at[1]).wait()

    @pl.loop(0, 2)
    def _(field):
        u = now[field].reshape(ROWS, CZ)
        top = u.astype(jnp.bfloat16)
        high[field] = top
        low[field] = (u - top.astype(jnp.float32)).astype(jnp.bfloat16)

    loads[0].wait()
    row_l = lax.broadcasted_iota(jnp.int32, (CX, CX), 1)
    row_s = lax.broadcasted_iota(jnp.int32, (CX, CX), 0)
    ids_l = jnp.broadcast_to(ids[...], (CX, CX))
    ids_s = ids_l.T
    earlier = ((ids_s >> 5) == (ids_l >> 5)) & (row_s < row_l)
    rank = jnp.sum(earlier.astype(jnp.int32), axis=0, keepdims=True)
    slot = 2 * (ids[...] >> 5) + rank
    placed = jnp.broadcast_to(slot, (CX, CX)).T == row_l
    tables[0, :, 0:CX] = slot
    tables[1, :, 0:CX] = jnp.sum(jnp.where(placed, row_s, 0), axis=0, keepdims=True)
    wanted[me, :, 0:CX] = jnp.sum(jnp.where(placed, ids_s & (SLAB - 1), 0), axis=0, keepdims=True)
    table_copy = pltpu.make_async_copy(tables, smem_tables, table_sem)
    table_copy.start()

    loads[3].wait()

    @pl.loop(0, 2)
    def _(field):
        picked = mm(square[4 * ROWS : 5 * ROWS, :], high[field]).astype(jnp.bfloat16)
        pick_send[0, field] = picked[0:YH]
        pick_send[1, field] = picked[YH:]

    partners = NS - 1 + (ty > 0).astype(jnp.int32) + (tx == 0).astype(jnp.int32)
    partners = partners + ((tx == 1) & mutual).astype(jnp.int32)
    partners = partners + jnp.where(tx == 3, NS + (ty > 0).astype(jnp.int32), 0)

    @pl.when(jnp.logical_not(relayed))
    def _():
        pl.semaphore_wait(barrier, partners)

    @pl.when(tx == 3)
    def _():
        pl.semaphore_signal(go, inc=1, device_id={"tx": 2}, device_id_type=MESH)

    upper = me // 4 + lax.rem(me, 4) >= 2

    @pl.when(relayed & (ty >= DIRECT) & jnp.logical_not(mutual))
    def _():
        across()

    @pl.when(relayed & mutual & jnp.logical_not(upper))
    def _():
        across()

    @pl.when(relayed)
    def _():
        pl.semaphore_wait(go, 1)

    def id_copy(other):
        return pltpu.make_async_remote_copy(
            src_ref=wanted.at[me],
            dst_ref=wanted.at[me],
            send_sem=id_send,
            recv_sem=id_recv,
            device_id={"shot": other},
            device_id_type=MESH,
        )

    each_partner(lambda other: id_copy(other).start())

    @pl.when(relayed & mutual & upper)
    def _():
        across()

    @pl.when(ty > 0)
    def _():
        answer_first(1)

    @pl.when(tx == 0)
    def _():
        answer_first(2)

    @pl.when(jnp.logical_not(odd) | ((tx == 1) & mutual))
    def _():
        halo_copy(2).start()

    @pl.when(tx == 3)
    def _():
        halo_copy(3).start()

    @pl.when(ty > 0)
    def _():
        halo_copy(1).start()

    def answer(n):
        @pl.when(first[n])
        def _():
            pl.semaphore_wait(ready.at[n], 1)
            halo_copy(n).start()

    loads[4].wait()
    slab[...] = slab_b[...].astype(jnp.float32)

    def serve(shot):
        rows = [slab[wanted_by[shot, 0, 2 * me + k]] for k in range(2)]
        return jnp.concatenate(rows, axis=0).astype(jnp.bfloat16)

    def block_copy(owner, shot):
        return pltpu.make_async_remote_copy(
            src_ref=blocks.at[shot],
            dst_ref=arrived.at[owner],
            send_sem=v_send,
            recv_sem=v_recv.at[me // 4],
            device_id={"shot": shot},
            device_id_type=MESH,
        )

    @pl.loop(0, 2)
    def _(field):
        top, rest = high[field], low[field]
        lap[field] = (
            mm(square[0:ROWS, :], top)
            + mm(square[0:ROWS, :], rest)
            + mm(square[ROWS : 2 * ROWS, :], top)
            + mm(top, square[2 * ROWS : 3 * ROWS, :])
            + mm(rest, square[2 * ROWS : 3 * ROWS, :])
            + mm(top, square[3 * ROWS : 4 * ROWS, :])
        ).reshape(CX, CY, CZ)

    for load in loads[8:]:
        load.wait()
    row = lax.broadcasted_iota(jnp.int32, (ROWS, 1), 0)

    def local_row(along_x, along_y):
        inside = (along_x >= tx * CX) & (along_x < tx * CX + CX)
        inside = inside & (along_y >= ty * CY) & (along_y < ty * CY + CY)
        return jnp.where(inside, (along_x - tx * CX) * CY + along_y - ty * CY, -1)

    source_row = local_row(source_s[0, 0], source_s[0, 1])
    cell_row = local_row(cell_v[0:1, :], cell_v[1:2, :])
    injected = jnp.where(row == source_row, strength_s[0, 0], 0.0)
    recorded = jnp.sum(
        jnp.where(jnp.broadcast_to(row, (ROWS, NREC)) == cell_row, trace_v[...], 0.0),
        axis=1,
        keepdims=True,
    )
    surface = lax.broadcasted_iota(jnp.int32, (ROWS, CZ), 1) == SURFACE_DEPTH

    loads[5].wait()
    pltpu.make_async_copy(prev, prev, load_sem.at[6]).wait()
    answer(0)

    all_but_one = pl.ds(0, NS - 1)
    pltpu.make_async_copy(wanted.at[all_but_one], wanted.at[all_but_one], id_recv).wait()
    table_copy.wait()
    id_local = pltpu.make_async_copy(wanted, wanted_by, table_sem)
    id_local.start()
    id_local.wait()

    @each_partner
    def _(shot):
        blocks[shot] = serve(shot)
        block_copy(me, shot).start()

    arrived[me] = serve(me)
    @pl.when(ty >= 5)
    def _():
        answer(3)

        @pl.when(jnp.logical_not(mutual))
        def _():
            answer(2)

    depth_l = lax.broadcasted_iota(jnp.int32, (CY, ROWS), 1)
    same_y = (depth_l & (CY - 1)) == lax.broadcasted_iota(jnp.int32, (CY, ROWS), 0)
    block_l = jnp.where(same_y, depth_l >> 3, -1)


    @pl.loop(0, NS)
    def _(shot):
        hits = [block_l == wanted_by[shot, 0, 2 * me + k] for k in range(2)]
        rows = pl.ds(pl.multiple_of(shot * 16, 16), 16)
        hit[rows, :] = jnp.where(jnp.concatenate(hits, axis=0), 1.0, 0.0)

    hit_out[...] = hit[...].T.astype(jnp.bfloat16)

    def halo_wait(n):
        @pl.when(sides[(1, 0, 3, 2)[n]][0])
        def _():
            halo_copy(n).wait_recv()

    halo_wait(0)
    halo_wait(1)
    @pl.loop(0, 2)
    def _(field):
        extra = jnp.where(field == 0, injected, recorded)
        layers = halo[field, 0 : 2 * YH]
        beyond = mm(halo_w[0:ROWS, :], layers) + mm(halo_w[ROWS:, :], layers)
        beyond = beyond + jnp.where(surface, jnp.broadcast_to(extra, (ROWS, CZ)), 0.0)
        lap[field] = lap[field] + beyond.reshape(CX, CY, CZ)
        prev[field] = 2.0 * now[field] - prev[field]

    @pl.when(ty < 5)
    def _():
        answer(3)
        answer(2)

    halo_wait(2)

    @pl.when((tx == 1) & direct)
    def _():
        pltpu.make_async_copy(far, far, far_sem.at[1]).wait()

    @pl.when((tx < NTX - 1) & jnp.logical_not((tx == 1) & direct))
    def _():
        halo_copy(3).wait_recv()

    @pl.when(jnp.logical_not((tx == 1) & direct))
    def _():
        far[...] = halo[:, 2 * YH + XH :].astype(jnp.float32).reshape(2, 4, CY, CZ)

    @pl.loop(0, 2)
    def _(field):
        near = halo[field, 2 * YH : 2 * YH + XH].astype(jnp.float32).reshape(4, CY, CZ)
        for q in range(4):
            for x in range(4):
                if x <= q:
                    weight = STENCIL_WEIGHTS[x + 4 - q]
                    lap[field, x] = lap[field, x] + weight * near[q]
                if x >= q:
                    weight = STENCIL_WEIGHTS[4 + q - x]
                    lap[field, CX - 4 + x] = lap[field, CX - 4 + x] + weight * far[field, q]


    def corr_copies(owner):
        return [
            pltpu.make_async_remote_copy(
                src_ref=source.at[owner],
                dst_ref=target.at[me],
                send_sem=c_send.at[n],
                recv_sem=c_recv.at[2 * (me // 8) + n],
                device_id={"shot": owner},
                device_id_type=MESH,
            )
            for n, (source, target) in enumerate(((peak_send, peak_in), (corr_send, corr_in)))
        ]

    def contribute(owner):
        pair = arrived[owner].astype(jnp.float32)
        products = []
        for k in range(2):
            scaled = pair[k * CY : (k + 1) * CY] * STEP_RATIO
            courant = scaled * scaled
            speed[2 * owner + k] = courant
            r = smem_tables[1, 0, 2 * owner + k]
            products.append(
                (prev[0, r] + courant * lap[0, r]) * (prev[1, r] + courant * lap[1, r])
            )
        both = jnp.concatenate(products, axis=0)
        top = jnp.max(jnp.abs(both), axis=0, keepdims=True)
        top = jnp.maximum(jnp.maximum(top[:, : CZ // 2], top[:, CZ // 2 :]), TINY)
        scale = STEPS / top
        code = jnp.round(both * jnp.concatenate([scale, scale], axis=1))
        return top, code.astype(jnp.int32).astype(jnp.int16)

    peak_in[me], corr_in[me] = contribute(me)

    def one_owner(owner):
        peak_send[owner], corr_send[owner] = contribute(owner)
        for copy in corr_copies(owner):
            copy.start()

    def row_of_blocks(x):
        for mine, count in ((x == me // 4, 3), (x != me // 4, 4)):

            @pl.when(mine)
            def _():
                four = arrived.at[pl.ds(4 * x, count)]
                pltpu.make_async_copy(four, four, v_recv.at[x]).wait()

    near = ((tx == 0) | (tx == 3)).astype(jnp.int32)
    each_partner(one_owner, near, row_of_blocks, ((tx == 1) & direct).astype(jnp.int32))

    @pl.loop(0, CX)
    def _(r):
        courant = speed[smem_tables[0, 0, r]]
        for field in range(2):
            prev[field, r] = prev[field, r] + courant * lap[field, r]

    def all_sent(ref, sem):
        pltpu.make_async_copy(ref.at[all_but_one], ref.at[all_but_one], sem).wait()

    all_sent(wanted, id_send)
    all_sent(blocks, v_send)
    for n in range(3):

        @pl.when(sides[n][0])
        def _():
            halo_copy(n).wait_send()

    @pl.when((tx > 0) & jnp.logical_not(relayed & direct))
    def _():
        halo_copy(3).wait_send()

    @pl.when(relayed & direct)
    def _():
        pltpu.make_async_copy(far, far, far_sem.at[0]).wait()

    all_sent(peak_send, c_send.at[0])
    all_sent(corr_send, c_send.at[1])
    def arrive(half, count):
        for n, ref in enumerate((peak_in, corr_in)):
            some = ref.at[pl.ds(0, count)]
            pltpu.make_async_copy(some, some, c_recv.at[2 * half + n]).wait()

    arrive(me // 8, 7)
    part[...] = image_of(me // 8, peak_in, corr_in, hit_out)
    arrive(1 - me // 8, 8)


def image_of(half, peak_in, corr_in, hit):
    shots = pl.ds(8 * half, 8)
    peak = peak_in[shots]
    peak = jnp.broadcast_to(jnp.concatenate([peak, peak], axis=2), (8, 2 * CY, CZ))
    share = corr_in[shots].astype(jnp.int32).astype(jnp.float32) * (1.0 / STEPS)
    rows = (share * peak).reshape(ROWS // 2, CZ)
    top = rows.astype(jnp.bfloat16)
    rest = (rows - top.astype(jnp.float32)).astype(jnp.bfloat16)
    chosen = hit[:, pl.ds(pl.multiple_of(ROWS // 2 * half, ROWS // 2), ROWS // 2)]
    return mm(chosen, top) + mm(chosen, rest)


def finish(values, peak_in, corr_in, hit, part, f_out, a_out, image_out, image, out_sem):
    def write(n, source, target):
        for part_of in range(4):
            rows = pl.ds(8 * part_of, 8)
            pltpu.make_async_copy(source.at[rows], target.at[0, rows], out_sem.at[n]).start()

    write(0, values.at[0], f_out)
    write(1, values.at[1], a_out)
    half = 1 - lax.axis_index("shot") // 8
    total = part[...] + image_of(half, peak_in, corr_in, hit)
    image[...] = total.reshape(SLAB, CY, CZ)
    write(2, image, image_out)
    for n, target in enumerate((f_out, a_out, image_out)):
        pltpu.make_async_copy(image, target.at[0], out_sem.at[n]).wait()


def on_device(*arrays):
    square, halo_w = stencil_constants()
    arrays = (
        *arrays[:7],
        arrays[7].reshape(1, 1),
        jnp.swapaxes(arrays[8], 1, 2),
        arrays[9],
        jnp.asarray(square),
        jnp.asarray(halo_w),
    )
    field = jax.ShapeDtypeStruct((1, CX, CY, CZ), jnp.float32)
    dma = pltpu.SemaphoreType.DMA
    bf, f32, i32 = jnp.bfloat16, jnp.float32, jnp.int32
    scratch = [
        pltpu.VMEM((2, CX, CY, CZ), f32),
        pltpu.VMEM((2, CX, CY, CZ), f32),
        pltpu.VMEM((2, ROWS, CZ), bf),
        pltpu.VMEM((2, ROWS, CZ), bf),
        pltpu.VMEM((2, 4, CY, CZ), f32),
        pltpu.VMEM((2, XH, CZ), bf),
        pltpu.VMEM((2, 4, CY, CZ), f32),
        pltpu.VMEM((SLAB, CY, CZ), bf),
        pltpu.VMEM((SLAB, CY, CZ), f32),
        pltpu.VMEM((1, CX), i32),
        pltpu.VMEM((2, NREC), i32),
        pltpu.VMEM((1, NREC), f32),
        pltpu.VMEM(square.shape, bf),
        pltpu.VMEM(halo_w.shape, bf),
        pltpu.VMEM((2, 2, YH, CZ), bf),
        pltpu.VMEM((2, HALO, CZ), bf),
        pltpu.VMEM((2, 1, 128), i32),
        pltpu.VMEM((NS, 1, 128), i32),
        pltpu.SMEM((NS, 1, 128), i32),
        pltpu.VMEM((NS, 2 * CY, CZ), bf),
        pltpu.VMEM((NS, 2 * CY, CZ), bf),
        pltpu.VMEM((2 * NS, CY, CZ), f32),
        pltpu.VMEM((NS, 1, CZ // 2), f32),
        pltpu.VMEM((NS, 2 * CY, CZ), jnp.int16),
        pltpu.VMEM((ROWS, ROWS), f32),
        pltpu.SMEM((2, 1, 128), i32),
        pltpu.SMEM((1, 2), i32),
        pltpu.SMEM((1, 1), f32),
        dma((10,)),
        dma,
        dma((2,)),
        dma,
        dma,
        dma,
        dma((4,)),
        dma((4,)),
        dma,
        dma((4,)),
        dma((2,)),
        dma((4,)),
        pltpu.SemaphoreType.REGULAR((4,)),
        pltpu.SemaphoreType.REGULAR,
    ]
    anywhere = pl.BlockSpec(memory_space=pl.ANY)
    vmem = pl.BlockSpec(memory_space=pltpu.VMEM)
    results = pl.pallas_call(
        kernel,
        out_shape=(
            jax.ShapeDtypeStruct((2, CX, CY, CZ), f32),
            jax.ShapeDtypeStruct((NS, 1, CZ // 2), f32),
            jax.ShapeDtypeStruct((NS, 2 * CY, CZ), jnp.int16),
            jax.ShapeDtypeStruct((ROWS, ROWS), bf),
            jax.ShapeDtypeStruct((ROWS, CZ), f32),
        ),
        in_specs=[anywhere] * 12,
        out_specs=(vmem,) * 5,
        scratch_shapes=scratch,
        compiler_params=pltpu.CompilerParams(
            collective_id=0, has_side_effects=True, vmem_limit_bytes=LIMIT
        ),
    )(*[a if a.size == 1 else pltpu.with_memory_space_constraint(a, pltpu.HBM) for a in arrays])
    return pl.pallas_call(
        finish,
        out_shape=(field, field, field),
        in_specs=[vmem] * 5,
        out_specs=(anywhere,) * 3,
        scratch_shapes=[pltpu.VMEM((SLAB, CY, CZ), f32), dma((3,))],
        compiler_params=pltpu.CompilerParams(vmem_limit_bytes=LIMIT),
    )(*results)


def solution(mesh):
    in_specs = (
        P("shot", "tx", "ty", None),
        P("shot", "tx", "ty", None),
        P("shot", "tx", "ty", None),
        P("shot", "tx", "ty", None),
        P(("tx", "ty"), "shot", None, None),
        P("shot", ("tx", "ty"), None),
        P("shot", None),
        P("shot"),
        P("shot", None, None),
        P("shot", None),
    )
    out_specs = (
        P("shot", "tx", "ty", None),
        P("shot", "tx", "ty", None),
        P(("tx", "ty"), "shot", None, None),
    )
    return jax.shard_map(
        on_device, mesh=mesh, in_specs=in_specs, out_specs=out_specs, check_vma=False
    )
```
